32 devices in a mesh: groups: 2 (over x), ctx: 8 (over z, y), head: 2 (over core).
Axes of the slice: x: 2, y: 2, z: 4, core: 2. Of those that a mesh axis runs over, the one named last changes fastest.
Arguments:
- queries: bfloat16 [4096, 2048], P(('groups', 'ctx'), 'head'), parts along dimension 0, may hold values from -180 to 180
- keys: bfloat16 [4096, 2048], P(('groups', 'ctx'), 'head'), parts along dimension 0, may hold values from -6 to 6
- values: bfloat16 [4096, 2048], P(('groups', 'ctx'), 'head'), parts along dimension 0, may hold values from -6 to 6
- out_weight: bfloat16 [2048, 2048], P(None, 'head'), may hold values from -0.125 to 0.125
- random_blocks: int32 [32, 3], P('groups'), parts along dimension 0, may hold values from 0 to 15, as said below
- window_blocks: int32 [32], P(('groups', 'ctx')), parts along dimension 0, may hold values from 0 to 1
- global_blocks: int32 [4], P('groups'), parts along dimension 0, may hold values from 0 to 15, as said below
Outputs:
- layer_out: bfloat16 [4096, 2048], P(('groups', 'ctx'), 'head'), parts along dimension 0
The draws below stay inside these ranges and needn't reach their ends.
There are 2 independent parts, one for each index of `groups`. The reference program is written for one: setup_inputs(seed, part) draws one part's arguments, and reference() takes and returns one part's arrays. A program takes and returns all parts, laid end to end along the dimension named above; an argument that names none is the same for every part. Nothing has to cross between parts.
Inputs may be any that keep to these rules, and one draw needn't show every extreme that they name: `random_blocks`: the random blocks named in the rows of one index j of ctx (rows j * 2 to j * 2 + 1) lie outside blocks j * 2 to j * 2 + 1; counted with repeats, at most 1 of them lie in the blocks k * 2 to k * 2 + 1 of any one other index k, and exactly 1 for some k. `global_blocks`: 2 different block numbers.
All inputs are finite; a program needn't handle non-finite values.
Results may differ from the reference program's by a relative error of at most 0.0055.
Values may be sent and summed in bfloat16 or wider, within the bound.
A program may use at most 128 MiB of HBM per device.

```python
import math
import jax
import jax.numpy as jnp
from jax import lax

HEADS = 16
HEAD = 128
D_OUT = 2048
BLOCK = 128
WMAX = 1
GLOB = 2
RAND = 3
BLK_DEV = 2
BLOCKS = 16
TOKENS = 2048


def draw_pair(key):
    width_all = HEADS * HEAD
    key_draw = jnp.clip(jax.random.normal(jax.random.fold_in(key, 11), (TOKENS, width_all), jnp.float32), -6.0, 6.0)
    query_draw = jnp.clip(jax.random.normal(jax.random.fold_in(key, 12), (TOKENS, width_all), jnp.float32), -6.0, 6.0)
    return (query_draw, key_draw)


def draw_queries(key, part):
    return draw_pair(key)[0].astype(jnp.bfloat16)


def draw_keys(key, part):
    return draw_pair(key)[1].astype(jnp.bfloat16)


def draw_random_blocks(key, part):
    dev_count = BLOCKS // BLK_DEV
    request_count = BLK_DEV * RAND
    dev_keys = jax.random.split(jax.random.fold_in(key, 7), dev_count)
    orders = jax.vmap(lambda subkey: jax.random.permutation(subkey, dev_count - 1))(dev_keys)
    cycle_pos = jnp.arange(request_count) % (dev_count - 1)
    owner_step = orders[:, cycle_pos] + 1
    shuffle_keys = jax.random.split(jax.random.fold_in(key, 8), dev_count)
    shuffles = jax.vmap(lambda subkey: jax.random.permutation(subkey, request_count))(shuffle_keys)
    owner_step = jnp.take_along_axis(owner_step, shuffles, axis=1)
    dev_index = jnp.arange(dev_count)[:, None]
    owners = (dev_index + owner_step) % dev_count
    within = jax.random.randint(jax.random.fold_in(key, 9), (dev_count, request_count), 0, BLK_DEV)
    return (owners * BLK_DEV + within).reshape(BLOCKS, RAND).astype(jnp.int32)


def draw_global_blocks(key, part):
    return jax.random.permutation(jax.random.fold_in(key, 5), BLOCKS)[:GLOB].astype(jnp.int32)


def touch_ends(array, stream_key, smallest, top_value):
    longest = array.shape.index(max(array.shape))
    spots = []
    for shift in (0, 1):
        where = [jax.random.randint(jax.random.fold_in(stream_key, axis), (), 0, length) for axis, length in enumerate(array.shape)]
        where[longest] = (where[longest] + shift) % array.shape[longest]
        spots.append(tuple(where))
    return array.at[spots[0]].set(smallest).at[spots[1]].set(top_value)


def levels(rng, dims, pieces, low, largest):
    factor_of, own = 1.0, jax.random.fold_in(rng, 6)
    for dim, shards_of in pieces:
        steps = jnp.exp(jax.random.uniform(jax.random.fold_in(own, dim), (shards_of,), jnp.float32, low / len(pieces), largest / len(pieces)))
        factor_of = factor_of * jnp.repeat(steps, dims[dim] // shards_of).reshape([-1 if axis == dim else 1 for axis in range(len(dims))])
    return factor_of


def centred(own_key, shape, deviation, most, cuts=(), held_as=jnp.bfloat16):
    entries = deviation * jax.random.normal(own_key, shape, jnp.float32)
    if cuts:
        entries = entries * levels(own_key, shape, cuts, -0.22, 0.18)
    return jnp.clip(entries, -most, most).astype(held_as)


def setup_inputs(seed: int = 0, part: int = 0) -> dict:
    arg_keys = jax.random.split(jax.random.key(seed), 8)
    part_splits = jax.random.split(jax.random.fold_in(arg_keys[7], part), 8)
    queries = draw_queries(jax.random.fold_in(jax.random.fold_in(arg_keys[7], part), 71), part)
    keys = draw_keys(jax.random.fold_in(jax.random.fold_in(arg_keys[7], part), 71), part)
    values = centred(part_splits[2], (TOKENS, HEADS * HEAD), 1.0, 6.0, ((0, 8), (1, 2)))
    out_weight = centred(arg_keys[3], (HEADS * HEAD, D_OUT), (HEADS * HEAD) ** -0.5, 0.125, ((1, 2),))
    random_blocks = draw_random_blocks(jax.random.fold_in(jax.random.fold_in(arg_keys[7], part), 71), part)
    window_blocks = touch_ends(jax.random.randint(part_splits[5], (BLOCKS,), 0, WMAX + 1), jax.random.fold_in(part_splits[5], 1), 0, WMAX).astype(jnp.int32)
    global_blocks = draw_global_blocks(jax.random.fold_in(jax.random.fold_in(arg_keys[7], part), 71), part)
    return dict(queries=queries, keys=keys, values=values, out_weight=out_weight, random_blocks=random_blocks, window_blocks=window_blocks, global_blocks=global_blocks)


LARGE_NEG = -1e+30

def split_heads(tensor):
    return tensor.reshape(tensor.shape[:-1] + (tensor.shape[-1] // HEAD, HEAD))

def block_partial(query_rows, key_rows, value_rows):
    query_heads = split_heads(query_rows).astype(jnp.float32)
    key_heads = split_heads(key_rows).astype(jnp.float32)
    value_heads = split_heads(value_rows).astype(jnp.float32)
    scores = jnp.einsum('gqhd,gckhd->gchqk', query_heads, key_heads) * (1.0 / math.sqrt(HEAD))
    row_peak = lax.optimization_barrier(jnp.max(scores, axis=-1))
    weights = jnp.exp(scores - row_peak[..., None])
    row_total = lax.optimization_barrier(jnp.sum(weights, axis=-1))
    rounded = lax.optimization_barrier(weights.astype(jnp.bfloat16)).astype(jnp.float32)
    partial_out = jnp.einsum('gchqk,gckhd->gcqhd', rounded, value_heads)
    partial_out = partial_out.reshape(partial_out.shape[:-2] + (-1,))
    return (partial_out, jnp.swapaxes(row_peak, -1, -2), jnp.swapaxes(row_total, -1, -2))

def combine(partial_out, row_peak, row_total, used_flags):
    used_mask = used_flags[:, :, None, None]
    best_peak = lax.optimization_barrier(jnp.max(jnp.where(used_mask, row_peak, LARGE_NEG), axis=1, keepdims=True))
    factor = jnp.where(used_mask, jnp.exp(row_peak - best_peak), 0.0)
    weighted = lax.optimization_barrier(jnp.sum(split_heads(partial_out) * factor[..., None], axis=1))
    normalizer = lax.optimization_barrier(jnp.sum(row_total * factor, axis=1))
    result = weighted / normalizer[..., None]
    return result.reshape(result.shape[:-2] + (-1,))

def candidates(first_block, block_count, widths, global_ids, random_rows, total_blocks):
    query_ids = first_block + jnp.arange(block_count, dtype=jnp.int32)
    offsets = jnp.arange(-WMAX, WMAX + 1, dtype=jnp.int32)
    window_ids = query_ids[:, None] + offsets[None, :]
    window_valid = (jnp.abs(offsets)[None, :] <= widths[:, None]) & (window_ids >= 0) & (window_ids < total_blocks)
    global_rows = jnp.broadcast_to(global_ids[None, :], (block_count, GLOB)).astype(jnp.int32)
    block_ids = jnp.concatenate([window_ids, global_rows, random_rows.astype(jnp.int32)], axis=1)
    valid = jnp.concatenate([window_valid, jnp.ones((block_count, GLOB + RAND), dtype=bool)], axis=1)
    width_all = block_ids.shape[1]
    same_block = block_ids[:, :, None] == block_ids[:, None, :]
    earlier = jnp.arange(width_all)[None, :] < jnp.arange(width_all)[:, None]
    shadowed = jnp.any(same_block & valid[:, None, :] & earlier[None, :, :], axis=2)
    return (block_ids, valid & jnp.logical_not(shadowed))

def reference(queries, keys, values, out_weight, random_blocks, window_blocks, global_blocks):
    tok_total, row_width = queries.shape
    total_blocks = tok_total // BLOCK
    query_blocks = queries.reshape(total_blocks, BLOCK, row_width)
    key_blocks = keys.reshape(total_blocks, BLOCK, row_width)
    value_blocks = values.reshape(total_blocks, BLOCK, row_width)
    block_ids, used_flags = candidates(0, total_blocks, window_blocks, global_blocks, random_blocks, total_blocks)
    clipped_ids = jnp.clip(block_ids, 0, total_blocks - 1).astype(jnp.int32)

    def attend(inputs):
        query_one, chosen_ids, used_row = inputs
        parts = block_partial(query_one[None], key_blocks[chosen_ids][None], value_blocks[chosen_ids][None])
        return combine(parts[0], parts[1], parts[2], used_row[None])[0].astype(jnp.bfloat16)
    attended = lax.map(attend, (query_blocks, clipped_ids, used_flags)).reshape(tok_total, row_width)
    return jnp.dot(attended, out_weight, preferred_element_type=jnp.float32).astype(jnp.bfloat16)
```

```python
import functools
import math

import jax
import jax.numpy as jnp
from jax import lax
from jax.experimental import pallas as pl
from jax.experimental.pallas import tpu as pltpu
from jax.sharding import PartitionSpec as P

HEAD = 128
BLOCK = 128
WMAX = 1
GLOB = 2
RAND = 3

LARGE_NEG = -1e30
MESH = pl.DeviceIdType.MESH

K_FWD, V_FWD, K_BWD, V_BWD = range(4)


GRID_DEPTH = 4
GRID_WIDTH = 2
OWN, NEAR, CROSS, FAR = range(4)
PARTNER, BELOW, BELOW_PARTNER = 1, 2, 3
SCALE = math.log2(math.e) / math.sqrt(HEAD)


def grid_kernel(
    random_ref,
    window_ref,
    global_ref,
    q_hbm,
    k_hbm,
    v_hbm,
    w_hbm,
    out_any,
    q_all,
    k_all,
    v_all,
    w_ref,
    win_all,
    bias_ref,
    peak_ref,
    total_ref,
    acc_ref,
    up_part,
    up_stat,
    up_part_in,
    up_stat_in,
    side_part,
    side_stat,
    side_part_in,
    side_stat_in,
    own_ref,
    other_ref,
    sum_ref,
    out_ref,
    load_sem,
    kv_send,
    kv_recv,
    q_send,
    q_recv,
    win_send,
    win_recv,
    up_send,
    up_recv,
    side_send,
    side_recv,
    pair_send,
    pair_recv,
):
    rows, width = q_hbm.shape
    heads = width // HEAD
    half = heads // 2
    dev_blocks = rows // BLOCK
    position = lax.axis_index("ctx")
    side = lax.axis_index("head")
    depth, column = position // GRID_WIDTH, position % GRID_WIDTH
    inner = (depth > 0) & (depth < GRID_DEPTH - 1)

    def mate(level):
        return level + 1 - 2 * (level % 2)

    cross_depth = GRID_DEPTH - 1 - depth
    partner = depth * GRID_WIDTH + 1 - column
    near = mate(depth) * GRID_WIDTH + column
    near_partner = mate(depth) * GRID_WIDTH + 1 - column
    cross = cross_depth * GRID_WIDTH + column
    far = mate(cross_depth) * GRID_WIDTH + column

    def at(h):
        if isinstance(h, int):
            return pl.ds(h * HEAD, HEAD)
        return pl.ds(pl.multiple_of(h * HEAD, HEAD), HEAD)

    def send(src, dst, send_sem, recv_sem, target):
        return pltpu.make_async_remote_copy(
            src_ref=src,
            dst_ref=dst,
            send_sem=send_sem,
            recv_sem=recv_sem,
            device_id=target,
            device_id_type=MESH,
        )

    def key_value(kind, slot, h):
        source = {
            NEAR: (k_hbm, v_hbm)[kind],
            CROSS: (k_hbm, v_hbm)[kind],
            FAR: (k_all, v_all)[kind].at[NEAR],
        }[slot]
        return send(
            source.at[:, at(h)],
            (k_all, v_all)[kind].at[slot, :, at(h)],
            kv_send.at[slot, kind, h],
            kv_recv.at[slot, kind, h],
            {"ctx": near if slot == NEAR else cross},
        )

    def query(slot):
        source = q_all.at[BELOW] if slot == BELOW_PARTNER else q_hbm
        return send(
            source,
            q_all.at[slot],
            q_send.at[slot],
            q_recv.at[slot],
            {"ctx": near if slot == BELOW else partner},
        )

    def reach(slot):
        return send(
            win_all.at[BELOW if slot == BELOW_PARTNER else OWN],
            win_all.at[slot],
            win_send.at[slot],
            win_recv.at[slot],
            {"ctx": near if slot == BELOW else partner},
        )

    def upward(which, h):
        return (
            send(up_part.at[which, h], up_part_in.at[which, h], up_send.at[0, which, h], up_recv.at[0, which, h], {"ctx": near}),
            send(up_stat.at[which, h], up_stat_in.at[which, h], up_send.at[1, which, h], up_recv.at[1, which, h], {"ctx": near}),
        )

    def sideways(h):
        return (
            send(side_part.at[h], side_part_in.at[h], side_send.at[0, h], side_recv.at[0, h], {"ctx": partner}),
            send(side_stat.at[h], side_stat_in.at[h], side_send.at[1, h], side_recv.at[1, h], {"ctx": partner}),
        )

    load_q = pltpu.make_async_copy(q_hbm, q_all.at[OWN], load_sem.at[0])
    load_k = pltpu.make_async_copy(k_hbm, k_all.at[OWN], load_sem.at[1])
    load_v = pltpu.make_async_copy(v_hbm, v_all.at[OWN], load_sem.at[2])
    load_w = pltpu.make_async_copy(w_hbm, w_ref, load_sem.at[3])
    load_q.start()
    load_k.start()
    load_v.start()

    barrier = pltpu.get_barrier_semaphore()
    pl.semaphore_signal(barrier, inc=1, device_id={"ctx": near}, device_id_type=MESH)
    pl.semaphore_signal(barrier, inc=1, device_id={"ctx": partner}, device_id_type=MESH)
    pl.semaphore_signal(barrier, inc=1, device_id={"head": 1 - side}, device_id_type=MESH)

    @pl.when(inner)
    def _():
        pl.semaphore_signal(barrier, inc=1, device_id={"ctx": cross}, device_id_type=MESH)

    for a in range(dev_blocks):
        win_all[OWN, a] = jnp.full((8, HEAD), window_ref[a], jnp.int32)
    sum_ref[...] = jnp.zeros_like(sum_ref)

    def use_bias(q, query_chip, pairs):
        for k, key_chip in pairs:
            for a in range(dev_blocks):
                query_block = query_chip * dev_blocks + a
                for b in range(dev_blocks):
                    key_block = key_chip * dev_blocks + b
                    offset = jnp.abs(key_block - query_block)
                    needed = jnp.where(offset <= WMAX, offset, 1 << 30)
                    used = global_ref[0] == key_block
                    for g in range(1, GLOB):
                        used = used | (global_ref[g] == key_block)
                    for r in range(RAND):
                        used = used | (random_ref[r, query_block] == key_block)
                    bias = jnp.where(used, 0.0, LARGE_NEG)
                    bias = jnp.where(win_all[q, a] >= needed, 0.0, bias)
                    bias_ref[q, k, a, :, b * BLOCK : (b + 1) * BLOCK] = bias

    def step(q, k, h, first=False):
        cols = at(h)
        for a in range(dev_blocks):
            span = slice(a * BLOCK, (a + 1) * BLOCK)
            scores = lax.dot_general(
                q_all[q, span, cols],
                k_all[k, :, cols],
                (((1,), (1,)), ((), ())),
                preferred_element_type=jnp.float32,
            )
            scores = scores * SCALE + bias_ref[q, k, a, 0:1, :]
            best = jnp.max(scores, axis=1, keepdims=True)
            if first:
                best = jnp.broadcast_to(best, (BLOCK, HEAD))
            else:
                old = peak_ref[q, h, span]
                best = jnp.maximum(old, best)
            weights = [
                jnp.exp2(scores[:, b * BLOCK : (b + 1) * BLOCK] - best) for b in range(dev_blocks)
            ]
            total = functools.reduce(jnp.add, weights)
            acc = jnp.dot(
                jnp.concatenate([w.astype(jnp.bfloat16) for w in weights], axis=1),
                v_all[k, :, cols],
                preferred_element_type=jnp.float32,
            )
            if not first:
                fade = jnp.exp2(old - best)
                total = total + total_ref[q, h, span] * fade
                acc = acc + acc_ref[q, h, span] * fade
            peak_ref[q, h, span] = best
            total_ref[q, h, span] = total
            acc_ref[q, h, span] = acc

    def pack(q, h, part, stat):
        total = jnp.sum(total_ref[q, h], axis=1, keepdims=True)
        part[...] = (acc_ref[q, h] / total).astype(jnp.bfloat16)
        level = peak_ref[q, h] + jnp.log2(total)
        stat[...] = level.T[:8]

    def merge(q, h, part, stat):
        level = jnp.broadcast_to(stat[0:1, :], (HEAD, rows)).T
        old = peak_ref[q, h]
        best = jnp.maximum(old, level)
        fade = jnp.exp2(old - best)
        gain = jnp.exp2(level - best)
        total = total_ref[q, h] * fade + gain * (1.0 / HEAD)
        acc = acc_ref[q, h] * fade + part[...].astype(jnp.float32) * gain
        return best, total, acc

    group = 2 * HEAD
    groups = width // group

    def group_cols(g):
        if isinstance(g, int):
            return pl.ds(g * group, group)
        return pl.ds(pl.multiple_of(g * group, group), group)

    def exchange(g):
        return send(
            own_ref.at[:, group_cols(g)],
            other_ref.at[:, group_cols(g)],
            pair_send.at[g],
            pair_recv.at[g],
            {"head": 1 - side},
        )

    def project(source, which, g):
        w_rows = pl.ds(pl.multiple_of(which * width + g * group, group), group)
        return jnp.dot(source[:, group_cols(g)], w_ref[w_rows, :], preferred_element_type=jnp.float32)

    def finish(h):
        for copy in sideways(h):
            copy.wait_recv()
        _, total, acc = merge(OWN, h, side_part_in.at[h], side_stat_in.at[h])
        total = jnp.sum(total, axis=1, keepdims=True)
        own_ref[:, at(h)] = (acc / total).astype(jnp.bfloat16)

        @pl.when(h % 2 == 1)
        def _():
            g = h // 2
            exchange(g).start()

            @pl.when(g == 0)
            def _():
                sum_ref[...] = project(own_ref, side, g)

            @pl.when(g > 0)
            def _():
                exchange(g - 1).wait_recv()
                sum_ref[...] += project(own_ref, side, g) + project(other_ref, 1 - side, g - 1)

    def loop(lower, upper, body):
        def run(h, carry):
            body(h)
            return carry

        lax.fori_loop(lower, upper, run, 0)

    def wait_key_value(slot, h):
        key_value(0, slot, h).wait_recv()
        key_value(1, slot, h).wait_recv()

    @pl.when(inner)
    def _():
        pl.semaphore_wait(barrier, 4)
        query(PARTNER).start()
        reach(PARTNER).start()

        def start_own(h):
            for kind in (0, 1):
                key_value(kind, CROSS, h).start()
            for kind in (0, 1):
                key_value(kind, NEAR, h).start()

        loop(0, heads, start_own)
        load_w.start()
        pairs = ((OWN, position), (NEAR, near), (CROSS, cross), (FAR, far))
        use_bias(OWN, position, pairs)
        load_q.wait()
        load_k.wait()
        load_v.wait()
        loop(0, heads, lambda h: step(OWN, OWN, h, first=True))

        query(BELOW).wait_recv()
        reach(BELOW).wait_recv()
        query(BELOW_PARTNER).start()
        reach(BELOW_PARTNER).start()
        query(PARTNER).wait_recv()
        reach(PARTNER).wait_recv()
        use_bias(PARTNER, partner, pairs)
        use_bias(BELOW, near, pairs[2:])
        loop(0, heads, lambda h: step(PARTNER, OWN, h, first=True))

        def pass_on(h):
            wait_key_value(NEAR, h)
            for kind in (0, 1):
                key_value(kind, FAR, h).start()

        def early(h):
            @pl.when(h >= half)
            def _():
                pass_on(h - half)

            wait_key_value(CROSS, h)
            step(OWN, CROSS, h)
            step(PARTNER, CROSS, h)
            step(BELOW, CROSS, h, first=True)

        loop(0, heads, early)
        query(BELOW_PARTNER).wait_recv()
        reach(BELOW_PARTNER).wait_recv()
        use_bias(BELOW_PARTNER, near_partner, pairs[2:])

        def late(h):
            @pl.when(h < half)
            def _():
                pass_on(h + half)

            step(BELOW_PARTNER, CROSS, h, first=True)
            step(PARTNER, NEAR, h)
            step(OWN, NEAR, h)
            wait_key_value(FAR, h)
            for which, q in ((1, BELOW_PARTNER), (0, BELOW)):
                step(q, FAR, h)
                pack(q, h, up_part.at[which, h], up_stat.at[which, h])
                for copy in upward(which, h):
                    copy.start()
            step(PARTNER, FAR, h)
            pack(PARTNER, h, side_part.at[h], side_stat.at[h])
            for copy in sideways(h):
                copy.start()
            step(OWN, FAR, h)

            @pl.when(h > 0)
            def _():
                finish(h - 1)

            @pl.when(h == 0)
            def _():
                load_w.wait()

        loop(0, heads, late)

    @pl.when(jnp.logical_not(inner))
    def _():
        pl.semaphore_wait(barrier, 3)
        query(BELOW).start()
        reach(BELOW).start()
        query(PARTNER).start()
        reach(PARTNER).start()

        def start_own(h):
            for kind in (0, 1):
                key_value(kind, NEAR, h).start()

        loop(0, heads, start_own)
        load_w.start()
        pairs = ((OWN, position), (NEAR, near))
        use_bias(OWN, position, pairs)
        load_q.wait()
        load_k.wait()
        load_v.wait()
        loop(0, heads, lambda h: step(OWN, OWN, h, first=True))
        query(PARTNER).wait_recv()
        reach(PARTNER).wait_recv()
        use_bias(PARTNER, partner, pairs)
        loop(0, heads, lambda h: step(PARTNER, OWN, h, first=True))

        def early(h):
            wait_key_value(NEAR, h)
            step(OWN, NEAR, h)
            step(PARTNER, NEAR, h)

        loop(0, heads, early)
        load_w.wait()

        def late(h):
            for which, q in ((1, PARTNER), (0, OWN)):
                for copy in upward(which, h):
                    copy.wait_recv()
                best, total, acc = merge(q, h, up_part_in.at[which, h], up_stat_in.at[which, h])
                peak_ref[q, h], total_ref[q, h], acc_ref[q, h] = best, total, acc
                if which == 1:
                    pack(q, h, side_part.at[h], side_stat.at[h])
                    for copy in sideways(h):
                        copy.start()

            @pl.when(h > 0)
            def _():
                finish(h - 1)

        loop(0, heads, late)

    finish(heads - 1)
    exchange(groups - 1).wait_recv()
    out_ref[...] = (sum_ref[...] + project(other_ref, 1 - side, groups - 1)).astype(out_ref.dtype)
    store = pltpu.make_async_copy(out_ref, out_any, load_sem.at[4])
    store.start()

    def drain(h):
        for kind in (0, 1):
            key_value(kind, NEAR, h).wait_send()
        for copy in sideways(h):
            copy.wait_send()

    loop(0, heads, drain)
    loop(0, groups, lambda g: exchange(g).wait_send())
    query(PARTNER).wait_send()
    reach(PARTNER).wait_send()

    @pl.when(inner)
    def _():
        def drain_inner(h):
            for slot in (CROSS, FAR):
                for kind in (0, 1):
                    key_value(kind, slot, h).wait_send()
            for which in (0, 1):
                for copy in upward(which, h):
                    copy.wait_send()

        loop(0, heads, drain_inner)
        query(BELOW_PARTNER).wait_send()
        reach(BELOW_PARTNER).wait_send()

    @pl.when(jnp.logical_not(inner))
    def _():
        query(BELOW).wait_send()
        reach(BELOW).wait_send()

    store.wait()


def grid_call(queries, keys, values, out_weight, random_blocks, window_blocks, global_blocks):
    rows, width = queries.shape
    heads = width // HEAD
    dev_blocks = rows // BLOCK
    out_width = out_weight.shape[1]
    smem = pl.BlockSpec(memory_space=pltpu.SMEM)
    hbm = pl.BlockSpec(memory_space=pltpu.HBM)
    state = pltpu.VMEM((4, heads, rows, HEAD), jnp.float32)
    dma = pltpu.SemaphoreType.DMA
    return pl.pallas_call(
        grid_kernel,
        out_shape=jax.ShapeDtypeStruct((rows, out_width), jnp.bfloat16),
        in_specs=[smem] * 3 + [hbm] * 4,
        out_specs=pl.BlockSpec(memory_space=pl.ANY),
        scratch_shapes=[
            pltpu.VMEM((4, rows, width), jnp.bfloat16),
            pltpu.VMEM((4, rows, width), jnp.bfloat16),
            pltpu.VMEM((4, rows, width), jnp.bfloat16),
            pltpu.VMEM(out_weight.shape, jnp.bfloat16),
            pltpu.VMEM((4, dev_blocks, 8, HEAD), jnp.int32),
            pltpu.VMEM((4, 4, dev_blocks, 8, rows), jnp.float32),
            state,
            state,
            state,
            pltpu.VMEM((2, heads, rows, HEAD), jnp.bfloat16),
            pltpu.VMEM((2, heads, 8, rows), jnp.float32),
            pltpu.VMEM((2, heads, rows, HEAD), jnp.bfloat16),
            pltpu.VMEM((2, heads, 8, rows), jnp.float32),
            pltpu.VMEM((heads, rows, HEAD), jnp.bfloat16),
            pltpu.VMEM((heads, 8, rows), jnp.float32),
            pltpu.VMEM((heads, rows, HEAD), jnp.bfloat16),
            pltpu.VMEM((heads, 8, rows), jnp.float32),
            pltpu.VMEM((rows, width), jnp.bfloat16),
            pltpu.VMEM((rows, width), jnp.bfloat16),
            pltpu.VMEM((rows, out_width), jnp.float32),
            pltpu.VMEM((rows, out_width), jnp.bfloat16),
            dma((5,)),
            dma((4, 2, heads)),
            dma((4, 2, heads)),
            dma((4,)),
            dma((4,)),
            dma((4,)),
            dma((4,)),
            dma((2, 2, heads)),
            dma((2, 2, heads)),
            dma((2, heads)),
            dma((2, heads)),
            dma((heads // 2,)),
            dma((heads // 2,)),
        ],
        compiler_params=pltpu.CompilerParams(
            collective_id=0, has_side_effects=True, vmem_limit_bytes=60 << 20
        ),
    )(random_blocks.T, window_blocks, global_blocks, queries, keys, values, out_weight)


def per_device(*arguments):
    if lax.axis_size("ctx") == GRID_DEPTH * GRID_WIDTH:
        return grid_call(*arguments)
    return ring_call(*arguments)


def ring_place(index, count):
    odd = index % 2
    return (1 - odd) * (index // 2) + odd * (count - 1 - index // 2)


def ring_index(place, count):
    late = place // (count // 2)
    return (1 - late) * (2 * place) + late * (2 * (count - 1 - place) + 1)


def ring_kernel(
    count,
    random_ref,
    window_ref,
    global_ref,
    q_hbm,
    k_hbm,
    v_hbm,
    w_hbm,
    out_any,
    q_ref,
    w_ref,
    k_all,
    v_all,
    peak_ref,
    total_ref,
    acc_ref,
    own_ref,
    other_ref,
    sum_ref,
    out_ref,
    load_sem,
    send_sem,
    recv_sem,
    last_send,
    last_recv,
    pair_send,
    pair_recv,
):
    rows, width = q_ref.shape
    heads = width // HEAD
    dev_blocks = rows // BLOCK
    half = count // 2
    position = lax.axis_index("ctx")
    side = lax.axis_index("head")
    place = ring_place(position, count)
    right = ring_index((place + 1) % count, count)
    left = ring_index((place + count - 1) % count, count)

    load_k = pltpu.make_async_copy(k_hbm, k_all.at[0], load_sem.at[0])
    load_v = pltpu.make_async_copy(v_hbm, v_all.at[0], load_sem.at[1])
    load_q = pltpu.make_async_copy(q_hbm, q_ref, load_sem.at[2])
    load_w = pltpu.make_async_copy(w_hbm, w_ref, load_sem.at[3])
    load_k.start()
    load_v.start()
    load_q.start()

    barrier = pltpu.get_barrier_semaphore()
    pl.semaphore_signal(barrier, inc=1, device_id={"ctx": left}, device_id_type=MESH)
    pl.semaphore_signal(barrier, inc=1, device_id={"ctx": right}, device_id_type=MESH)
    pl.semaphore_signal(barrier, inc=1, device_id={"head": 1 - side}, device_id_type=MESH)
    pl.semaphore_wait(barrier, 3)

    def hop(stream, slot):
        buffer = k_all if stream in (K_FWD, K_BWD) else v_all
        forward = stream in (K_FWD, V_FWD)
        source = slot - 1 if forward else (slot + 1) % count
        return pltpu.make_async_remote_copy(
            src_ref=buffer.at[source],
            dst_ref=buffer.at[slot],
            send_sem=send_sem.at[stream, slot],
            recv_sem=recv_sem.at[stream, slot],
            device_id={"ctx": right if forward else left},
            device_id_type=MESH,
        )

    load_k.wait()
    hop(K_FWD, 1).start()
    hop(K_BWD, count - 1).start()
    load_v.wait()
    hop(V_FWD, 1).start()
    hop(V_BWD, count - 1).start()
    load_q.wait()
    load_w.start()

    peak_ref[...] = jnp.full_like(peak_ref, LARGE_NEG)
    total_ref[...] = jnp.zeros_like(total_ref)
    acc_ref[...] = jnp.zeros_like(acc_ref)
    scale = math.log2(math.e) / math.sqrt(HEAD)

    def use_bias(slot):
        owner = ring_index((place + count - slot) % count, count)
        row_block = lax.broadcasted_iota(jnp.int32, (rows, HEAD), 0) // BLOCK
        biases = []
        for b in range(dev_blocks):
            key_block = owner * dev_blocks + b
            bias = jnp.full((rows, HEAD), LARGE_NEG, jnp.float32)
            for a in range(dev_blocks):
                query_block = position * dev_blocks + a
                offset = jnp.abs(key_block - query_block)
                used = (offset <= window_ref[a]) & (offset <= WMAX)
                for g in range(GLOB):
                    used = used | (global_ref[g] == key_block)
                for r in range(RAND):
                    used = used | (random_ref[r, query_block] == key_block)
                bias = jnp.where(row_block == a, jnp.where(used, 0.0, LARGE_NEG), bias)
            biases.append(bias)
        return biases

    def attend_head(slot, h, biases):
        cols = pl.ds(h * HEAD, HEAD)
        if not isinstance(h, int):
            cols = pl.ds(pl.multiple_of(h * HEAD, HEAD), HEAD)
        scores = lax.dot_general(
            q_ref[:, cols],
            k_all[slot, :, cols],
            (((1,), (1,)), ((), ())),
            preferred_element_type=jnp.float32,
        )
        scores = scores * scale
        old_peak = peak_ref[h]
        best_peak = old_peak
        parts = []
        for b, bias in enumerate(biases):
            block = scores[:, b * BLOCK : (b + 1) * BLOCK]
            row_peak = jnp.max(block, axis=1, keepdims=True)
            weights = jnp.exp2(block - row_peak)
            part = jnp.dot(
                weights.astype(jnp.bfloat16),
                v_all[slot, b * BLOCK : (b + 1) * BLOCK, cols],
                preferred_element_type=jnp.float32,
            )
            used_peak = row_peak + bias
            best_peak = jnp.maximum(best_peak, used_peak)
            parts.append((used_peak, weights, part))
        fade = jnp.exp2(old_peak - best_peak)
        total = total_ref[h] * fade
        acc = acc_ref[h] * fade
        for used_peak, weights, part in parts:
            factor = jnp.exp2(used_peak - best_peak)
            total = total + weights * factor
            acc = acc + part * factor
        return best_peak, total, acc

    def attend(slot):
        biases = use_bias(slot)

        def one_head(h, carry):
            peak_ref[h], total_ref[h], acc_ref[h] = attend_head(slot, h, biases)
            return carry

        lax.fori_loop(0, heads, one_head, 0, unroll=2)

    def last_hop(stream, h):
        buffer = k_all if stream == K_FWD else v_all
        forward = h % 2 == 0
        cols = pl.ds(h * HEAD, HEAD)
        return pltpu.make_async_remote_copy(
            src_ref=buffer.at[half - 1 if forward else half + 1, :, cols],
            dst_ref=buffer.at[half, :, cols],
            send_sem=last_send.at[stream, h],
            recv_sem=last_recv.at[stream, h],
            device_id={"ctx": right if forward else left},
            device_id_type=MESH,
        )

    attend(0)

    def middle(step, carry):
        back = count - step
        hop(K_FWD, step).wait_recv()
        hop(K_FWD, step + 1).start()
        hop(K_BWD, back).wait_recv()
        hop(K_BWD, back - 1).start()
        hop(V_FWD, step).wait_recv()
        hop(V_FWD, step + 1).start()
        hop(V_BWD, back).wait_recv()
        hop(V_BWD, back - 1).start()
        attend(step)
        attend(back)
        return carry

    lax.fori_loop(1, half - 1, middle, 0)

    for side_of, key_stream in ((0, K_FWD), (1, K_BWD)):
        hop(key_stream, half + 1 if side_of else half - 1).wait_recv()
        for pair in range(min(2, heads // 2)):
            last_hop(K_FWD, 2 * pair + side_of).start()
    for side_of, value_stream in ((0, V_FWD), (1, V_BWD)):
        hop(value_stream, half + 1 if side_of else half - 1).wait_recv()
        for pair in range(heads // 2):
            last_hop(V_FWD, 2 * pair + side_of).start()
            if pair + 2 < heads // 2:
                last_hop(K_FWD, 2 * (pair + 2) + side_of).start()
    attend(half - 1)
    attend(half + 1)
    load_w.wait()
    biases = use_bias(half)
    group = 2 * HEAD

    def exchange(g):
        cols = pl.ds(g * group, group)
        return pltpu.make_async_remote_copy(
            src_ref=own_ref.at[:, cols],
            dst_ref=other_ref.at[:, cols],
            send_sem=pair_send.at[g],
            recv_sem=pair_recv.at[g],
            device_id={"head": 1 - side},
            device_id_type=MESH,
        )

    def project(source, which, g):
        w_rows = pl.ds(pl.multiple_of(which * width + g * group, group), group)
        return jnp.dot(
            source[:, g * group : (g + 1) * group],
            w_ref[w_rows, :],
            preferred_element_type=jnp.float32,
        )

    groups = width // group
    for g in range(groups):
        for h in (2 * g, 2 * g + 1):
            last_hop(K_FWD, h).wait_recv()
            last_hop(V_FWD, h).wait_recv()
            _, total, acc = attend_head(half, h, biases)
            total = jnp.sum(total, axis=1, keepdims=True)
            own_ref[:, h * HEAD : (h + 1) * HEAD] = (acc / total).astype(jnp.bfloat16)
        exchange(g).start()
        if g == 0:
            sum_ref[...] = project(own_ref, side, g)
        else:
            exchange(g - 1).wait_recv()
            sum_ref[...] += project(other_ref, 1 - side, g - 1) + project(own_ref, side, g)
    exchange(groups - 1).wait_recv()
    out_ref[...] = (sum_ref[...] + project(other_ref, 1 - side, groups - 1)).astype(out_ref.dtype)

    store = pltpu.make_async_copy(out_ref, out_any, load_sem.at[4])
    store.start()
    for g in range(groups):
        exchange(g).wait_send()
    for h in range(heads):
        last_hop(K_FWD, h).wait_send()
        last_hop(V_FWD, h).wait_send()

    def drain(step, carry):
        hop(K_FWD, step).wait_send()
        hop(V_FWD, step).wait_send()
        hop(K_BWD, count - step).wait_send()
        hop(V_BWD, count - step).wait_send()
        return carry

    lax.fori_loop(1, half, drain, 0)
    store.wait()


def ring_call(queries, keys, values, out_weight, random_blocks, window_blocks, global_blocks):
    count = lax.axis_size("ctx")
    rows, width = queries.shape
    heads = width // HEAD
    out_width = out_weight.shape[1]
    smem = pl.BlockSpec(memory_space=pltpu.SMEM)
    hbm = pl.BlockSpec(memory_space=pltpu.HBM)
    return pl.pallas_call(
        functools.partial(ring_kernel, count),
        out_shape=jax.ShapeDtypeStruct((rows, out_width), jnp.bfloat16),
        in_specs=[smem] * 3 + [hbm] * 4,
        out_specs=pl.BlockSpec(memory_space=pl.ANY),
        scratch_shapes=[
            pltpu.VMEM((rows, width), jnp.bfloat16),
            pltpu.VMEM(out_weight.shape, jnp.bfloat16),
            pltpu.VMEM((count, rows, width), jnp.bfloat16),
            pltpu.VMEM((count, rows, width), jnp.bfloat16),
            pltpu.VMEM((heads, rows, HEAD), jnp.float32),
            pltpu.VMEM((heads, rows, HEAD), jnp.float32),
            pltpu.VMEM((heads, rows, HEAD), jnp.float32),
            pltpu.VMEM((rows, width), jnp.bfloat16),
            pltpu.VMEM((rows, width), jnp.bfloat16),
            pltpu.VMEM((rows, out_width), jnp.float32),
            pltpu.VMEM((rows, out_width), jnp.bfloat16),
            pltpu.SemaphoreType.DMA((5,)),
            pltpu.SemaphoreType.DMA((4, count)),
            pltpu.SemaphoreType.DMA((4, count)),
            pltpu.SemaphoreType.DMA((2, heads)),
            pltpu.SemaphoreType.DMA((2, heads)),
            pltpu.SemaphoreType.DMA((heads // 2,)),
            pltpu.SemaphoreType.DMA((heads // 2,)),
        ],
        compiler_params=pltpu.CompilerParams(
            collective_id=1, has_side_effects=True, vmem_limit_bytes=60 << 20
        ),
    )(random_blocks.T, window_blocks, global_blocks, queries, keys, values, out_weight)


def solution(mesh):
    placed = (
        P(("groups", "ctx"), "head"),
        P(("groups", "ctx"), "head"),
        P(("groups", "ctx"), "head"),
        P(None, "head"),
        P("groups", None),
        P(("groups", "ctx")),
        P("groups"),
    )
    return jax.shard_map(
        per_device,
        mesh=mesh,
        in_specs=placed,
        out_specs=P(("groups", "ctx"), "head"),
        check_vma=False,
    )
```

```python
import functools
import math

import jax
import jax.numpy as jnp
from jax import lax
from jax.experimental import pallas as pl
from jax.experimental.pallas import tpu as pltpu
from jax.sharding import PartitionSpec as P

HEAD = 128
BLOCK = 128
WMAX = 1
GLOB = 2
RAND = 3

LARGE_NEG = -1e30
MESH = pl.DeviceIdType.MESH

K_FWD, V_FWD, K_BWD, V_BWD = range(4)


GRID_DEPTH = 4
GRID_WIDTH = 2
OWN, NEAR, CROSS, FAR = range(4)
PARTNER, BELOW, BELOW_PARTNER = 1, 2, 3
SCALE = math.log2(math.e) / math.sqrt(HEAD)


def grid_kernel(
    random_ref,
    window_ref,
    global_ref,
    q_hbm,
    k_hbm,
    v_hbm,
    w_hbm,
    out_any,
    q_all,
    k_all,
    v_all,
    w_ref,
    win_all,
    bias_ref,
    peak_ref,
    total_ref,
    acc_ref,
    up_part,
    up_stat,
    up_part_in,
    up_stat_in,
    side_part,
    side_stat,
    side_part_in,
    side_stat_in,
    own_ref,
    other_ref,
    sum_ref,
    out_ref,
    load_sem,
    kv_send,
    kv_recv,
    q_send,
    q_recv,
    win_send,
    win_recv,
    up_send,
    up_recv,
    side_send,
    side_recv,
    pair_send,
    pair_recv,
):
    rows, width = q_hbm.shape
    heads = width // HEAD
    half = heads // 2
    dev_blocks = rows // BLOCK
    position = lax.axis_index("ctx")
    side = lax.axis_index("head")
    depth, column = position // GRID_WIDTH, position % GRID_WIDTH
    inner = (depth > 0) & (depth < GRID_DEPTH - 1)

    def mate(level):
        return level + 1 - 2 * (level % 2)

    cross_depth = GRID_DEPTH - 1 - depth
    partner = depth * GRID_WIDTH + 1 - column
    near = mate(depth) * GRID_WIDTH + column
    near_partner = mate(depth) * GRID_WIDTH + 1 - column
    cross = cross_depth * GRID_WIDTH + column
    far = mate(cross_depth) * GRID_WIDTH + column

    def at(h):
        if isinstance(h, int):
            return pl.ds(h * HEAD, HEAD)
        return pl.ds(pl.multiple_of(h * HEAD, HEAD), HEAD)

    def send(src, dst, send_sem, recv_sem, target):
        return pltpu.make_async_remote_copy(
            src_ref=src,
            dst_ref=dst,
            send_sem=send_sem,
            recv_sem=recv_sem,
            device_id=target,
            device_id_type=MESH,
        )

    def key_value(kind, slot, h):
        source = {
            NEAR: (k_hbm, v_hbm)[kind],
            CROSS: (k_hbm, v_hbm)[kind],
            FAR: (k_all, v_all)[kind].at[NEAR],
        }[slot]
        return send(
            source.at[:, at(h)],
            (k_all, v_all)[kind].at[slot, :, at(h)],
            kv_send.at[slot, kind, h],
            kv_recv.at[slot, kind, h],
            {"ctx": near if slot == NEAR else cross},
        )

    def query(slot):
        source = q_all.at[BELOW] if slot == BELOW_PARTNER else q_hbm
        return send(
            source,
            q_all.at[slot],
            q_send.at[slot],
            q_recv.at[slot],
            {"ctx": near if slot == BELOW else partner},
        )

    def reach(slot):
        return send(
            win_all.at[BELOW if slot == BELOW_PARTNER else OWN],
            win_all.at[slot],
            win_send.at[slot],
            win_recv.at[slot],
            {"ctx": near if slot == BELOW else partner},
        )

    def upward(which, h):
        target = {"ctx": near_partner if which else near}
        return (
            send(up_stat.at[which, h, 0:1], up_stat_in.at[which, h, 0:1], up_send.at[1, which, h], up_recv.at[1, which, h], target),
            send(up_part.at[which, h], up_part_in.at[which, h], up_send.at[0, which, h], up_recv.at[0, which, h], target),
        )

    def sideways(h):
        target = {"ctx": partner}
        return (
            send(side_stat.at[h, 0:1], side_stat_in.at[h, 0:1], side_send.at[1, h], side_recv.at[1, h], target),
            send(side_part.at[h], side_part_in.at[h], side_send.at[0, h], side_recv.at[0, h], target),
        )

    load_q = pltpu.make_async_copy(q_hbm, q_all.at[OWN], load_sem.at[0])
    load_k = pltpu.make_async_copy(k_hbm, k_all.at[OWN], load_sem.at[1])
    load_v = pltpu.make_async_copy(v_hbm, v_all.at[OWN], load_sem.at[2])
    load_w = pltpu.make_async_copy(w_hbm, w_ref, load_sem.at[3])
    load_q.start()
    load_k.start()
    load_v.start()

    barrier = pltpu.get_barrier_semaphore()
    pl.semaphore_signal(barrier, inc=1, device_id={"ctx": near}, device_id_type=MESH)
    pl.semaphore_signal(barrier, inc=1, device_id={"ctx": partner}, device_id_type=MESH)
    pl.semaphore_signal(barrier, inc=1, device_id={"ctx": near_partner}, device_id_type=MESH)
    pl.semaphore_signal(barrier, inc=1, device_id={"head": 1 - side}, device_id_type=MESH)

    @pl.when(inner)
    def _():
        pl.semaphore_signal(barrier, inc=1, device_id={"ctx": cross}, device_id_type=MESH)

    for a in range(dev_blocks):
        win_all[OWN, a] = jnp.full((8, HEAD), window_ref[a], jnp.int32)
    sum_ref[...] = jnp.zeros_like(sum_ref)

    def use_bias(q, query_chip, pairs):
        for k, key_chip in pairs:
            for a in range(dev_blocks):
                query_block = query_chip * dev_blocks + a
                for b in range(dev_blocks):
                    key_block = key_chip * dev_blocks + b
                    offset = jnp.abs(key_block - query_block)
                    needed = jnp.where(offset <= WMAX, offset, 1 << 30)
                    used = global_ref[0] == key_block
                    for g in range(1, GLOB):
                        used = used | (global_ref[g] == key_block)
                    for r in range(RAND):
                        used = used | (random_ref[r, query_block] == key_block)
                    bias = jnp.where(used, 0.0, LARGE_NEG)
                    bias = jnp.where(win_all[q, a] >= needed, 0.0, bias)
                    bias_ref[q, k, a, :, b * BLOCK : (b + 1) * BLOCK] = bias

    def step(q, k, h, first=False):
        cols = at(h)
        for a in range(dev_blocks):
            span = slice(a * BLOCK, (a + 1) * BLOCK)
            scores = lax.dot_general(
                q_all[q, span, cols],
                k_all[k, :, cols],
                (((1,), (1,)), ((), ())),
                preferred_element_type=jnp.float32,
            )
            scores = scores * SCALE + bias_ref[q, k, a, 0:1, :]
            best = jnp.max(scores, axis=1, keepdims=True)
            if first:
                best = jnp.broadcast_to(best, (BLOCK, HEAD))
            else:
                old = peak_ref[q, h, span]
                best = jnp.maximum(old, best)
            weights = [
                jnp.exp2(scores[:, b * BLOCK : (b + 1) * BLOCK] - best) for b in range(dev_blocks)
            ]
            total = functools.reduce(jnp.add, weights)
            acc = jnp.dot(
                jnp.concatenate([w.astype(jnp.bfloat16) for w in weights], axis=1),
                v_all[k, :, cols],
                preferred_element_type=jnp.float32,
            )
            if not first:
                fade = jnp.exp2(old - best)
                total = total + total_ref[q, h, span] * fade
                acc = acc + acc_ref[q, h, span] * fade
            peak_ref[q, h, span] = best
            total_ref[q, h, span] = total
            acc_ref[q, h, span] = acc

    def pack(q, h, part, stat):
        total = jnp.sum(total_ref[q, h], axis=1, keepdims=True)
        part[...] = (acc_ref[q, h] / total).astype(jnp.bfloat16)
        level = peak_ref[q, h] + jnp.log2(total)
        stat[...] = level.T[:8]

    def merge(q, h, incoming):
        old = peak_ref[q, h]
        levels = [jnp.broadcast_to(stat[0:1, :], (HEAD, rows)).T for _, stat in incoming]
        best = functools.reduce(jnp.maximum, levels, old)
        fade = jnp.exp2(old - best)
        total = total_ref[q, h] * fade
        acc = acc_ref[q, h] * fade
        for level, (part, _) in zip(levels, incoming):
            gain = jnp.exp2(level - best)
            total = total + gain * (1.0 / HEAD)
            acc = acc + part[...].astype(jnp.float32) * gain
        return best, total, acc

    group = 2 * HEAD
    groups = width // group

    def group_cols(g):
        if isinstance(g, int):
            return pl.ds(g * group, group)
        return pl.ds(pl.multiple_of(g * group, group), group)

    def exchange(g):
        return send(
            own_ref.at[:, group_cols(g)],
            other_ref.at[:, group_cols(g)],
            pair_send.at[g],
            pair_recv.at[g],
            {"head": 1 - side},
        )

    def project(source, which, g):
        w_rows = pl.ds(pl.multiple_of(which * width + g * group, group), group)
        return jnp.dot(source[:, group_cols(g)], w_ref[w_rows, :], preferred_element_type=jnp.float32)

    def finish(h, *incoming):
        _, total, acc = merge(OWN, h, incoming)
        total = jnp.sum(total, axis=1, keepdims=True)
        own_ref[:, at(h)] = (acc / total).astype(jnp.bfloat16)

        @pl.when(h % 2 == 1)
        def _():
            g = h // 2
            exchange(g).start()

            @pl.when(g == 0)
            def _():
                sum_ref[...] = project(own_ref, side, g)

            @pl.when(g > 0)
            def _():
                exchange(g - 1).wait_recv()
                sum_ref[...] += project(own_ref, side, g) + project(other_ref, 1 - side, g - 1)

    def loop(lower, upper, body):
        def run(h, carry):
            body(h)
            return carry

        lax.fori_loop(lower, upper, run, 0)

    def wait_key_value(slot, h):
        key_value(0, slot, h).wait_recv()
        key_value(1, slot, h).wait_recv()

    @pl.when(inner)
    def _():
        pl.semaphore_wait(barrier, 5)
        query(PARTNER).start()
        reach(PARTNER).start()

        def start_own(h):
            for kind in (0, 1):
                key_value(kind, CROSS, h).start()
            for kind in (0, 1):
                key_value(kind, NEAR, h).start()

        loop(0, heads, start_own)
        load_w.start()
        pairs = ((OWN, position), (NEAR, near), (CROSS, cross), (FAR, far))
        use_bias(OWN, position, pairs)
        load_q.wait()
        load_k.wait()
        load_v.wait()
        loop(0, heads, lambda h: step(OWN, OWN, h, first=True))

        query(BELOW).wait_recv()
        reach(BELOW).wait_recv()
        query(BELOW_PARTNER).start()
        reach(BELOW_PARTNER).start()
        query(PARTNER).wait_recv()
        reach(PARTNER).wait_recv()
        use_bias(PARTNER, partner, pairs)
        use_bias(BELOW, near, pairs[2:])
        loop(0, heads, lambda h: step(PARTNER, OWN, h, first=True))

        def pass_on(h):
            wait_key_value(NEAR, h)
            for kind in (0, 1):
                key_value(kind, FAR, h).start()

        def early(h):
            @pl.when(h >= half)
            def _():
                pass_on(h - half)
                step(PARTNER, NEAR, h - half)
                step(OWN, NEAR, h - half)

            wait_key_value(CROSS, h)
            step(OWN, CROSS, h)
            step(PARTNER, CROSS, h)
            step(BELOW, CROSS, h, first=True)

        loop(0, heads, early)
        query(BELOW_PARTNER).wait_recv()
        reach(BELOW_PARTNER).wait_recv()
        use_bias(BELOW_PARTNER, near_partner, pairs[2:])

        def late(h):
            @pl.when(h < half)
            def _():
                pass_on(h + half)

                step(PARTNER, NEAR, h + half)
                step(OWN, NEAR, h + half)

            step(BELOW_PARTNER, CROSS, h, first=True)
            wait_key_value(FAR, h)
            for which, q in ((1, BELOW_PARTNER), (0, BELOW)):
                step(q, FAR, h)
                pack(q, h, up_part.at[which, h], up_stat.at[which, h])
                for copy in upward(which, h):
                    copy.start()
            step(PARTNER, FAR, h)
            pack(PARTNER, h, side_part.at[h], side_stat.at[h])
            for copy in sideways(h):
                copy.start()
            step(OWN, FAR, h)

            @pl.when(h > 0)
            def _():
                close(h - 1)

            @pl.when(h == 0)
            def _():
                load_w.wait()

        def close(h):
            for copy in sideways(h):
                copy.wait_recv()
            finish(h, (side_part_in.at[h], side_stat_in.at[h]))

        loop(0, heads, late)
        close(heads - 1)

    @pl.when(jnp.logical_not(inner))
    def _():
        pl.semaphore_wait(barrier, 4)
        query(BELOW).start()
        reach(BELOW).start()
        query(PARTNER).start()
        reach(PARTNER).start()

        def start_own(h):
            for kind in (0, 1):
                key_value(kind, NEAR, h).start()

        loop(0, heads, start_own)
        load_w.start()
        pairs = ((OWN, position), (NEAR, near))
        use_bias(OWN, position, pairs)
        load_q.wait()
        load_k.wait()
        load_v.wait()
        loop(0, heads, lambda h: step(OWN, OWN, h, first=True))
        query(PARTNER).wait_recv()
        reach(PARTNER).wait_recv()
        use_bias(PARTNER, partner, pairs)
        loop(0, heads, lambda h: step(PARTNER, OWN, h, first=True))

        def early(h):
            wait_key_value(NEAR, h)
            step(PARTNER, NEAR, h)
            pack(PARTNER, h, side_part.at[h], side_stat.at[h])
            for copy in sideways(h):
                copy.start()
            step(OWN, NEAR, h)

        loop(0, heads, early)
        load_w.wait()

        def side_merge(h):
            for copy in sideways(h):
                copy.wait_recv()
            best, total, acc = merge(OWN, h, [(side_part_in.at[h], side_stat_in.at[h])])
            peak_ref[OWN, h], total_ref[OWN, h], acc_ref[OWN, h] = best, total, acc

        loop(0, heads, side_merge)

        def late(h):
            for which in (1, 0):
                for copy in upward(which, h):
                    copy.wait_recv()
            finish(h, *[(up_part_in.at[which, h], up_stat_in.at[which, h]) for which in (0, 1)])

        loop(0, heads, late)

    exchange(groups - 1).wait_recv()
    out_ref[...] = (sum_ref[...] + project(other_ref, 1 - side, groups - 1)).astype(out_ref.dtype)
    store = pltpu.make_async_copy(out_ref, out_any, load_sem.at[4])
    store.start()

    def drain(h):
        for kind in (0, 1):
            key_value(kind, NEAR, h).wait_send()
        for copy in sideways(h):
            copy.wait_send()

    loop(0, heads, drain)
    loop(0, groups, lambda g: exchange(g).wait_send())
    query(PARTNER).wait_send()
    reach(PARTNER).wait_send()

    @pl.when(inner)
    def _():
        def drain_inner(h):
            for slot in (CROSS, FAR):
                for kind in (0, 1):
                    key_value(kind, slot, h).wait_send()
            for which in (0, 1):
                for copy in upward(which, h):
                    copy.wait_send()

        loop(0, heads, drain_inner)
        query(BELOW_PARTNER).wait_send()
        reach(BELOW_PARTNER).wait_send()

    @pl.when(jnp.logical_not(inner))
    def _():
        query(BELOW).wait_send()
        reach(BELOW).wait_send()

    store.wait()


def grid_call(queries, keys, values, out_weight, random_blocks, window_blocks, global_blocks):
    rows, width = queries.shape
    heads = width // HEAD
    dev_blocks = rows // BLOCK
    out_width = out_weight.shape[1]
    smem = pl.BlockSpec(memory_space=pltpu.SMEM)
    hbm = pl.BlockSpec(memory_space=pltpu.HBM)
    state = pltpu.VMEM((4, heads, rows, HEAD), jnp.float32)
    dma = pltpu.SemaphoreType.DMA
    return pl.pallas_call(
        grid_kernel,
        out_shape=jax.ShapeDtypeStruct((rows, out_width), jnp.bfloat16),
        in_specs=[smem] * 3 + [hbm] * 4,
        out_specs=pl.BlockSpec(memory_space=pl.ANY),
        scratch_shapes=[
            pltpu.VMEM((4, rows, width), jnp.bfloat16),
            pltpu.VMEM((4, rows, width), jnp.bfloat16),
            pltpu.VMEM((4, rows, width), jnp.bfloat16),
            pltpu.VMEM(out_weight.shape, jnp.bfloat16),
            pltpu.VMEM((4, dev_blocks, 8, HEAD), jnp.int32),
            pltpu.VMEM((4, 4, dev_blocks, 8, rows), jnp.float32),
            state,
            state,
            state,
            pltpu.VMEM((2, heads, rows, HEAD), jnp.bfloat16),
            pltpu.VMEM((2, heads, 8, rows), jnp.float32),
            pltpu.VMEM((2, heads, rows, HEAD), jnp.bfloat16),
            pltpu.VMEM((2, heads, 8, rows), jnp.float32),
            pltpu.VMEM((heads, rows, HEAD), jnp.bfloat16),
            pltpu.VMEM((heads, 8, rows), jnp.float32),
            pltpu.VMEM((heads, rows, HEAD), jnp.bfloat16),
            pltpu.VMEM((heads, 8, rows), jnp.float32),
            pltpu.VMEM((rows, width), jnp.bfloat16),
            pltpu.VMEM((rows, width), jnp.bfloat16),
            pltpu.VMEM((rows, out_width), jnp.float32),
            pltpu.VMEM((rows, out_width), jnp.bfloat16),
            dma((5,)),
            dma((4, 2, heads)),
            dma((4, 2, heads)),
            dma((4,)),
            dma((4,)),
            dma((4,)),
            dma((4,)),
            dma((2, 2, heads)),
            dma((2, 2, heads)),
            dma((2, heads)),
            dma((2, heads)),
            dma((heads // 2,)),
            dma((heads // 2,)),
        ],
        compiler_params=pltpu.CompilerParams(
            collective_id=0, has_side_effects=True, vmem_limit_bytes=60 << 20
        ),
    )(random_blocks.T, window_blocks, global_blocks, queries, keys, values, out_weight)


def per_device(*arguments):
    if lax.axis_size("ctx") == GRID_DEPTH * GRID_WIDTH:
        return grid_call(*arguments)
    return ring_call(*arguments)


def ring_place(index, count):
    odd = index % 2
    return (1 - odd) * (index // 2) + odd * (count - 1 - index // 2)


def ring_index(place, count):
    late = place // (count // 2)
    return (1 - late) * (2 * place) + late * (2 * (count - 1 - place) + 1)


def ring_kernel(
    count,
    random_ref,
    window_ref,
    global_ref,
    q_hbm,
    k_hbm,
    v_hbm,
    w_hbm,
    out_any,
    q_ref,
    w_ref,
    k_all,
    v_all,
    peak_ref,
    total_ref,
    acc_ref,
    own_ref,
    other_ref,
    sum_ref,
    out_ref,
    load_sem,
    send_sem,
    recv_sem,
    last_send,
    last_recv,
    pair_send,
    pair_recv,
):
    rows, width = q_ref.shape
    heads = width // HEAD
    dev_blocks = rows // BLOCK
    half = count // 2
    position = lax.axis_index("ctx")
    side = lax.axis_index("head")
    place = ring_place(position, count)
    right = ring_index((place + 1) % count, count)
    left = ring_index((place + count - 1) % count, count)

    load_k = pltpu.make_async_copy(k_hbm, k_all.at[0], load_sem.at[0])
    load_v = pltpu.make_async_copy(v_hbm, v_all.at[0], load_sem.at[1])
    load_q = pltpu.make_async_copy(q_hbm, q_ref, load_sem.at[2])
    load_w = pltpu.make_async_copy(w_hbm, w_ref, load_sem.at[3])
    load_k.start()
    load_v.start()
    load_q.start()

    barrier = pltpu.get_barrier_semaphore()
    pl.semaphore_signal(barrier, inc=1, device_id={"ctx": left}, device_id_type=MESH)
    pl.semaphore_signal(barrier, inc=1, device_id={"ctx": right}, device_id_type=MESH)
    pl.semaphore_signal(barrier, inc=1, device_id={"head": 1 - side}, device_id_type=MESH)
    pl.semaphore_wait(barrier, 3)

    def hop(stream, slot):
        buffer = k_all if stream in (K_FWD, K_BWD) else v_all
        forward = stream in (K_FWD, V_FWD)
        source = slot - 1 if forward else (slot + 1) % count
        return pltpu.make_async_remote_copy(
            src_ref=buffer.at[source],
            dst_ref=buffer.at[slot],
            send_sem=send_sem.at[stream, slot],
            recv_sem=recv_sem.at[stream, slot],
            device_id={"ctx": right if forward else left},
            device_id_type=MESH,
        )

    load_k.wait()
    hop(K_FWD, 1).start()
    hop(K_BWD, count - 1).start()
    load_v.wait()
    hop(V_FWD, 1).start()
    hop(V_BWD, count - 1).start()
    load_q.wait()
    load_w.start()

    peak_ref[...] = jnp.full_like(peak_ref, LARGE_NEG)
    total_ref[...] = jnp.zeros_like(total_ref)
    acc_ref[...] = jnp.zeros_like(acc_ref)
    scale = math.log2(math.e) / math.sqrt(HEAD)

    def use_bias(slot):
        owner = ring_index((place + count - slot) % count, count)
        row_block = lax.broadcasted_iota(jnp.int32, (rows, HEAD), 0) // BLOCK
        biases = []
        for b in range(dev_blocks):
            key_block = owner * dev_blocks + b
            bias = jnp.full((rows, HEAD), LARGE_NEG, jnp.float32)
            for a in range(dev_blocks):
                query_block = position * dev_blocks + a
                offset = jnp.abs(key_block - query_block)
                used = (offset <= window_ref[a]) & (offset <= WMAX)
                for g in range(GLOB):
                    used = used | (global_ref[g] == key_block)
                for r in range(RAND):
                    used = used | (random_ref[r, query_block] == key_block)
                bias = jnp.where(row_block == a, jnp.where(used, 0.0, LARGE_NEG), bias)
            biases.append(bias)
        return biases

    def attend_head(slot, h, biases):
        cols = pl.ds(h * HEAD, HEAD)
        if not isinstance(h, int):
            cols = pl.ds(pl.multiple_of(h * HEAD, HEAD), HEAD)
        scores = lax.dot_general(
            q_ref[:, cols],
            k_all[slot, :, cols],
            (((1,), (1,)), ((), ())),
            preferred_element_type=jnp.float32,
        )
        scores = scores * scale
        old_peak = peak_ref[h]
        best_peak = old_peak
        parts = []
        for b, bias in enumerate(biases):
            block = scores[:, b * BLOCK : (b + 1) * BLOCK]
            row_peak = jnp.max(block, axis=1, keepdims=True)
            weights = jnp.exp2(block - row_peak)
            part = jnp.dot(
                weights.astype(jnp.bfloat16),
                v_all[slot, b * BLOCK : (b + 1) * BLOCK, cols],
                preferred_element_type=jnp.float32,
            )
            used_peak = row_peak + bias
            best_peak = jnp.maximum(best_peak, used_peak)
            parts.append((used_peak, weights, part))
        fade = jnp.exp2(old_peak - best_peak)
        total = total_ref[h] * fade
        acc = acc_ref[h] * fade
        for used_peak, weights, part in parts:
            factor = jnp.exp2(used_peak - best_peak)
            total = total + weights * factor
            acc = acc + part * factor
        return best_peak, total, acc

    def attend(slot):
        biases = use_bias(slot)

        def one_head(h, carry):
            peak_ref[h], total_ref[h], acc_ref[h] = attend_head(slot, h, biases)
            return carry

        lax.fori_loop(0, heads, one_head, 0, unroll=2)

    def last_hop(stream, h):
        buffer = k_all if stream == K_FWD else v_all
        forward = h % 2 == 0
        cols = pl.ds(h * HEAD, HEAD)
        return pltpu.make_async_remote_copy(
            src_ref=buffer.at[half - 1 if forward else half + 1, :, cols],
            dst_ref=buffer.at[half, :, cols],
            send_sem=last_send.at[stream, h],
            recv_sem=last_recv.at[stream, h],
            device_id={"ctx": right if forward else left},
            device_id_type=MESH,
        )

    attend(0)

    def middle(step, carry):
        back = count - step
        hop(K_FWD, step).wait_recv()
        hop(K_FWD, step + 1).start()
        hop(K_BWD, back).wait_recv()
        hop(K_BWD, back - 1).start()
        hop(V_FWD, step).wait_recv()
        hop(V_FWD, step + 1).start()
        hop(V_BWD, back).wait_recv()
        hop(V_BWD, back - 1).start()
        attend(step)
        attend(back)
        return carry

    lax.fori_loop(1, half - 1, middle, 0)

    for side_of, key_stream in ((0, K_FWD), (1, K_BWD)):
        hop(key_stream, half + 1 if side_of else half - 1).wait_recv()
        for pair in range(min(2, heads // 2)):
            last_hop(K_FWD, 2 * pair + side_of).start()
    for side_of, value_stream in ((0, V_FWD), (1, V_BWD)):
        hop(value_stream, half + 1 if side_of else half - 1).wait_recv()
        for pair in range(heads // 2):
            last_hop(V_FWD, 2 * pair + side_of).start()
            if pair + 2 < heads // 2:
                last_hop(K_FWD, 2 * (pair + 2) + side_of).start()
    attend(half - 1)
    attend(half + 1)
    load_w.wait()
    biases = use_bias(half)
    group = 2 * HEAD

    def exchange(g):
        cols = pl.ds(g * group, group)
        return pltpu.make_async_remote_copy(
            src_ref=own_ref.at[:, cols],
            dst_ref=other_ref.at[:, cols],
            send_sem=pair_send.at[g],
            recv_sem=pair_recv.at[g],
            device_id={"head": 1 - side},
            device_id_type=MESH,
        )

    def project(source, which, g):
        w_rows = pl.ds(pl.multiple_of(which * width + g * group, group), group)
        return jnp.dot(
            source[:, g * group : (g + 1) * group],
            w_ref[w_rows, :],
            preferred_element_type=jnp.float32,
        )

    groups = width // group
    for g in range(groups):
        for h in (2 * g, 2 * g + 1):
            last_hop(K_FWD, h).wait_recv()
            last_hop(V_FWD, h).wait_recv()
            _, total, acc = attend_head(half, h, biases)
            total = jnp.sum(total, axis=1, keepdims=True)
            own_ref[:, h * HEAD : (h + 1) * HEAD] = (acc / total).astype(jnp.bfloat16)
        exchange(g).start()
        if g == 0:
            sum_ref[...] = project(own_ref, side, g)
        else:
            exchange(g - 1).wait_recv()
            sum_ref[...] += project(other_ref, 1 - side, g - 1) + project(own_ref, side, g)
    exchange(groups - 1).wait_recv()
    out_ref[...] = (sum_ref[...] + project(other_ref, 1 - side, groups - 1)).astype(out_ref.dtype)

    store = pltpu.make_async_copy(out_ref, out_any, load_sem.at[4])
    store.start()
    for g in range(groups):
        exchange(g).wait_send()
    for h in range(heads):
        last_hop(K_FWD, h).wait_send()
        last_hop(V_FWD, h).wait_send()

    def drain(step, carry):
        hop(K_FWD, step).wait_send()
        hop(V_FWD, step).wait_send()
        hop(K_BWD, count - step).wait_send()
        hop(V_BWD, count - step).wait_send()
        return carry

    lax.fori_loop(1, half, drain, 0)
    store.wait()


def ring_call(queries, keys, values, out_weight, random_blocks, window_blocks, global_blocks):
    count = lax.axis_size("ctx")
    rows, width = queries.shape
    heads = width // HEAD
    out_width = out_weight.shape[1]
    smem = pl.BlockSpec(memory_space=pltpu.SMEM)
    hbm = pl.BlockSpec(memory_space=pltpu.HBM)
    return pl.pallas_call(
        functools.partial(ring_kernel, count),
        out_shape=jax.ShapeDtypeStruct((rows, out_width), jnp.bfloat16),
        in_specs=[smem] * 3 + [hbm] * 4,
        out_specs=pl.BlockSpec(memory_space=pl.ANY),
        scratch_shapes=[
            pltpu.VMEM((rows, width), jnp.bfloat16),
            pltpu.VMEM(out_weight.shape, jnp.bfloat16),
            pltpu.VMEM((count, rows, width), jnp.bfloat16),
            pltpu.VMEM((count, rows, width), jnp.bfloat16),
            pltpu.VMEM((heads, rows, HEAD), jnp.float32),
            pltpu.VMEM((heads, rows, HEAD), jnp.float32),
            pltpu.VMEM((heads, rows, HEAD), jnp.float32),
            pltpu.VMEM((rows, width), jnp.bfloat16),
            pltpu.VMEM((rows, width), jnp.bfloat16),
            pltpu.VMEM((rows, out_width), jnp.float32),
            pltpu.VMEM((rows, out_width), jnp.bfloat16),
            pltpu.SemaphoreType.DMA((5,)),
            pltpu.SemaphoreType.DMA((4, count)),
            pltpu.SemaphoreType.DMA((4, count)),
            pltpu.SemaphoreType.DMA((2, heads)),
            pltpu.SemaphoreType.DMA((2, heads)),
            pltpu.SemaphoreType.DMA((heads // 2,)),
            pltpu.SemaphoreType.DMA((heads // 2,)),
        ],
        compiler_params=pltpu.CompilerParams(
            collective_id=1, has_side_effects=True, vmem_limit_bytes=60 << 20
        ),
    )(random_blocks.T, window_blocks, global_blocks, queries, keys, values, out_weight)


def solution(mesh):
    placed = (
        P(("groups", "ctx"), "head"),
        P(("groups", "ctx"), "head"),
        P(("groups", "ctx"), "head"),
        P(None, "head"),
        P("groups", None),
        P(("groups", "ctx")),
        P("groups"),
    )
    return jax.shard_map(
        per_device,
        mesh=mesh,
        in_specs=placed,
        out_specs=P(("groups", "ctx"), "head"),
        check_vma=False,
    )
```

```python
import functools
import math

import jax
import jax.numpy as jnp
from jax import lax
from jax.experimental import pallas as pl
from jax.experimental.pallas import tpu as pltpu
from jax.sharding import PartitionSpec as P

HEAD = 128
BLOCK = 128
WMAX = 1
GLOB = 2
RAND = 3

LARGE_NEG = -1e30
MESH = pl.DeviceIdType.MESH

K_FWD, V_FWD, K_BWD, V_BWD = range(4)


GRID_DEPTH = 4
GRID_WIDTH = 2
OWN, NEAR, CROSS, FAR = range(4)
PARTNER, BELOW, BELOW_PARTNER = 1, 2, 3
SCALE = math.log2(math.e) / math.sqrt(HEAD)


def grid_kernel(
    random_ref,
    window_ref,
    global_ref,
    q_hbm,
    k_hbm,
    v_hbm,
    w_hbm,
    out_any,
    q_all,
    k_all,
    v_all,
    w_ref,
    win_all,
    bias_ref,
    peak_ref,
    total_ref,
    acc_ref,
    up_part,
    up_stat,
    up_part_in,
    up_stat_in,
    side_part,
    side_stat,
    side_part_in,
    side_stat_in,
    own_ref,
    other_ref,
    sum_ref,
    out_ref,
    load_sem,
    store_sem,
    kv_send,
    kv_recv,
    q_send,
    q_recv,
    win_send,
    win_recv,
    up_send,
    up_recv,
    side_send,
    side_recv,
    pair_send,
    pair_recv,
    ready,
):
    rows, width = q_hbm.shape
    heads = width // HEAD
    half = heads // 2
    dev_blocks = rows // BLOCK
    position = lax.axis_index("ctx")
    side = lax.axis_index("head")
    depth, column = position // GRID_WIDTH, position % GRID_WIDTH
    inner = (depth > 0) & (depth < GRID_DEPTH - 1)

    def mate(level):
        return level + 1 - 2 * (level % 2)

    cross_depth = GRID_DEPTH - 1 - depth
    partner = depth * GRID_WIDTH + 1 - column
    near = mate(depth) * GRID_WIDTH + column
    near_partner = mate(depth) * GRID_WIDTH + 1 - column
    cross = cross_depth * GRID_WIDTH + column
    far = mate(cross_depth) * GRID_WIDTH + column

    def at(h):
        if isinstance(h, int):
            return pl.ds(h * HEAD, HEAD)
        return pl.ds(pl.multiple_of(h * HEAD, HEAD), HEAD)

    def send(src, dst, send_sem, recv_sem, target):
        return pltpu.make_async_remote_copy(
            src_ref=src,
            dst_ref=dst,
            send_sem=send_sem,
            recv_sem=recv_sem,
            device_id=target,
            device_id_type=MESH,
        )

    def key_value(kind, slot, h):
        source = {
            NEAR: (k_hbm, v_hbm)[kind],
            CROSS: (k_hbm, v_hbm)[kind],
            FAR: (k_all, v_all)[kind].at[NEAR],
        }[slot]
        return send(
            source.at[:, at(h)],
            (k_all, v_all)[kind].at[slot, :, at(h)],
            kv_send.at[slot, kind, h],
            kv_recv.at[slot, kind, h],
            {"ctx": near if slot == NEAR else cross},
        )

    def query(slot):
        source = q_all.at[BELOW] if slot == BELOW_PARTNER else q_hbm
        return send(
            source,
            q_all.at[slot],
            q_send.at[slot],
            q_recv.at[slot],
            {"ctx": near if slot == BELOW else partner},
        )

    def reach(slot):
        return send(
            win_all.at[BELOW if slot == BELOW_PARTNER else OWN],
            win_all.at[slot],
            win_send.at[slot],
            win_recv.at[slot],
            {"ctx": near if slot == BELOW else partner},
        )

    def upward(which, h, joined=False):
        target = {"ctx": (partner if joined else near_partner) if which else near}
        return (
            send(up_stat.at[which, h, 0:1], up_stat_in.at[which, h, 0:1], up_send.at[1, which, h], up_recv.at[1, which, h], target),
            send(up_part.at[which, h], up_part_in.at[which, h], up_send.at[0, which, h], up_recv.at[0, which, h], target),
        )

    def sideways(h):
        target = {"ctx": partner}
        return (
            send(side_stat.at[h, 0:1], side_stat_in.at[h, 0:1], side_send.at[1, h], side_recv.at[1, h], target),
            send(side_part.at[h], side_part_in.at[h], side_send.at[0, h], side_recv.at[0, h], target),
        )

    load_q = pltpu.make_async_copy(q_hbm, q_all.at[OWN], load_sem.at[0])
    load_k = pltpu.make_async_copy(k_hbm, k_all.at[OWN], load_sem.at[1])
    load_v = pltpu.make_async_copy(v_hbm, v_all.at[OWN], load_sem.at[2])
    load_w = pltpu.make_async_copy(w_hbm, w_ref, load_sem.at[3])
    barrier = pltpu.get_barrier_semaphore()

    def greet(semaphore, target):
        pl.semaphore_signal(semaphore, inc=1, device_id=target, device_id_type=MESH)

    @pl.when(inner)
    def _():
        greet(barrier, {"ctx": cross})
        greet(barrier, {"ctx": near})
        greet(barrier, {"ctx": near_partner})

    greet(barrier, {"ctx": partner})
    greet(barrier, {"head": 1 - side})
    load_q.start()
    load_k.start()
    load_v.start()
    for a in range(dev_blocks):
        win_all[OWN, a] = jnp.full((8, HEAD), window_ref[a], jnp.int32)

    def use_bias(q, query_chip, pairs):
        for k, key_chip in pairs:
            for a in range(dev_blocks):
                query_block = query_chip * dev_blocks + a
                for b in range(dev_blocks):
                    key_block = key_chip * dev_blocks + b
                    offset = jnp.abs(key_block - query_block)
                    needed = jnp.where(offset <= WMAX, offset, 1 << 30)
                    used = global_ref[0] == key_block
                    for g in range(1, GLOB):
                        used = used | (global_ref[g] == key_block)
                    for r in range(RAND):
                        used = used | (random_ref[r, query_block] == key_block)
                    bias = jnp.where(used, 0.0, LARGE_NEG)
                    bias = jnp.where(win_all[q, a] >= needed, 0.0, bias)
                    bias_ref[q, k, a, :, b * BLOCK : (b + 1) * BLOCK] = bias

    def steps(pairs, h, first=False):
        cols = at(h)
        every = [
            lax.dot_general(
                q_all[q, :, cols],
                k_all[k, :, cols],
                (((1,), (1,)), ((), ())),
                preferred_element_type=jnp.float32,
            )
            for q, k in pairs
        ]
        held = []
        for (q, k), scores in zip(pairs, every):
            for a in range(dev_blocks):
                span = slice(a * BLOCK, (a + 1) * BLOCK)
                block = scores[span] * SCALE + bias_ref[q, k, a, 0:1, :]
                best = jnp.max(block, axis=1, keepdims=True)
                old = None
                if first:
                    best = jnp.broadcast_to(best, (BLOCK, HEAD))
                else:
                    old = peak_ref[q, h, span]
                    best = jnp.maximum(old, best)
                weights = [
                    jnp.exp2(block[:, b * BLOCK : (b + 1) * BLOCK] - best) for b in range(dev_blocks)
                ]
                total = functools.reduce(jnp.add, weights)
                rounded = jnp.concatenate([w.astype(jnp.bfloat16) for w in weights], axis=1)
                held.append((old, best, total, rounded))
        for i, (q, k) in enumerate(pairs):
            mine = held[i * dev_blocks : (i + 1) * dev_blocks]
            part = jnp.dot(
                jnp.concatenate([m[3] for m in mine], axis=0),
                v_all[k, :, cols],
                preferred_element_type=jnp.float32,
            )
            for a, (old, best, total, _) in enumerate(mine):
                span = slice(a * BLOCK, (a + 1) * BLOCK)
                acc = part[span]
                if not first:
                    fade = jnp.exp2(old - best)
                    total = total + total_ref[q, h, span] * fade
                    acc = acc + acc_ref[q, h, span] * fade
                peak_ref[q, h, span] = best
                total_ref[q, h, span] = total
                acc_ref[q, h, span] = acc

    def step(q, k, h, first=False):
        steps([(q, k)], h, first)

    def pack(q, h, part, stat):
        total = jnp.sum(total_ref[q, h], axis=1, keepdims=True)
        part[...] = (acc_ref[q, h] / total).astype(jnp.bfloat16)
        level = peak_ref[q, h] + jnp.log2(total)
        stat[...] = level.T[:8]

    def merge(q, h, incoming):
        old = peak_ref[q, h]
        levels = [jnp.broadcast_to(stat[0:1, :], (HEAD, rows)).T for _, stat in incoming]
        best = functools.reduce(jnp.maximum, levels, old)
        fade = jnp.exp2(old - best)
        total = total_ref[q, h] * fade
        acc = acc_ref[q, h] * fade
        for level, (part, _) in zip(levels, incoming):
            gain = jnp.exp2(level - best)
            total = total + gain * (1.0 / HEAD)
            acc = acc + part[...].astype(jnp.float32) * gain
        return best, total, acc

    def keep(q, h, state):
        peak_ref[q, h], total_ref[q, h], acc_ref[q, h] = state

    group = 2 * HEAD
    groups = width // group
    tiles = 2
    tile = out_ref.shape[1] // tiles

    def group_cols(g):
        if isinstance(g, int):
            return pl.ds(g * group, group)
        return pl.ds(pl.multiple_of(g * group, group), group)

    def exchange(g):
        return send(
            own_ref.at[:, group_cols(g)],
            other_ref.at[:, group_cols(g)],
            pair_send.at[g],
            pair_recv.at[g],
            {"head": 1 - side},
        )

    def project(source, which, g):
        w_rows = pl.ds(pl.multiple_of(which * width + g * group, group), group)
        return jnp.dot(source[:, group_cols(g)], w_ref[w_rows, :], preferred_element_type=jnp.float32)

    def finish(h, *incoming):
        _, total, acc = merge(OWN, h, incoming)
        total = jnp.sum(total, axis=1, keepdims=True)
        own_ref[:, at(h)] = (acc / total).astype(jnp.bfloat16)

        @pl.when(h % 2 == 1)
        def _():
            g = h // 2
            exchange(g).start()

            @pl.when(g == 0)
            def _():
                sum_ref[...] = project(own_ref, side, g)

            @pl.when(g > 0)
            def _():
                exchange(g - 1).wait_recv()
                sum_ref[...] += project(own_ref, side, g) + project(other_ref, 1 - side, g - 1)

    def loop(lower, upper, body):
        def run(h, carry):
            body(h)
            return carry

        lax.fori_loop(lower, upper, run, 0)

    def wait_key_value(slot, h):
        key_value(0, slot, h).wait_recv()
        key_value(1, slot, h).wait_recv()

    @pl.when(inner)
    def _():
        pl.semaphore_wait(barrier, 3)

        def start_own(slot, h):
            for kind in (0, 1):
                key_value(kind, slot, h).start()

        start_own(CROSS, 0)
        query(PARTNER).start()
        reach(PARTNER).start()
        loop(1, heads, lambda h: start_own(CROSS, h))
        pl.semaphore_wait(ready, 2)
        loop(0, heads, lambda h: start_own(NEAR, h))
        load_w.start()
        pairs = ((OWN, position), (NEAR, near), (CROSS, cross), (FAR, far))
        use_bias(OWN, position, pairs)
        load_q.wait()
        load_k.wait()
        load_v.wait()
        loop(0, heads, lambda h: step(OWN, OWN, h, first=True))

        query(BELOW).wait_recv()
        reach(BELOW).wait_recv()
        query(BELOW_PARTNER).start()
        reach(BELOW_PARTNER).start()
        query(PARTNER).wait_recv()
        reach(PARTNER).wait_recv()
        use_bias(PARTNER, partner, pairs)
        use_bias(BELOW, near, pairs[2:])
        loop(0, heads, lambda h: step(PARTNER, OWN, h, first=True))

        def pass_on(h):
            wait_key_value(NEAR, h)
            for kind in (0, 1):
                key_value(kind, FAR, h).start()

        def early(h):
            @pl.when(h >= half)
            def _():
                pass_on(h - half)
                steps([(PARTNER, NEAR), (OWN, NEAR)], h - half)

            wait_key_value(CROSS, h)
            steps([(OWN, CROSS), (PARTNER, CROSS)], h)
            step(BELOW, CROSS, h, first=True)

        loop(0, heads, early)
        query(BELOW_PARTNER).wait_recv()
        reach(BELOW_PARTNER).wait_recv()
        use_bias(BELOW_PARTNER, near_partner, pairs[2:])

        def ship(which, q, h, joined=False):
            pack(q, h, up_part.at[which, h], up_stat.at[which, h])
            for copy in upward(which, h, joined):
                copy.start()

        def close(h):
            for copy in sideways(h):
                copy.wait_recv()
            finish(h, (side_part_in.at[h], side_stat_in.at[h]))

        def ship_side(h):
            pack(PARTNER, h, side_part.at[h], side_stat.at[h])
            for copy in sideways(h):
                copy.start()

        def late(h, joined=False):
            @pl.when(h < half)
            def _():
                pass_on(h + half)
                steps([(PARTNER, NEAR), (OWN, NEAR)], h + half)

            step(BELOW_PARTNER, CROSS, h, first=True)
            wait_key_value(FAR, h)
            step(BELOW_PARTNER, FAR, h)
            ship(1, BELOW_PARTNER, h, joined)
            steps([(PARTNER, FAR), (BELOW, FAR)], h)
            ship_side(h)
            if not joined:
                ship(0, BELOW, h)
            step(OWN, FAR, h)

        def relay(h):
            for copy in upward(1, h, True):
                copy.wait_recv()
            keep(BELOW, h, merge(BELOW, h, [(up_part_in.at[1, h], up_stat_in.at[1, h])]))
            ship(0, BELOW, h)

        def late_pair(p):
            late(2 * p, True)

            @pl.when(p > 0)
            def _():
                close(2 * p - 1)

            @pl.when(p == 0)
            def _():
                load_w.wait()

            late(2 * p + 1)
            relay(2 * p)
            close(2 * p)

        loop(0, heads // 2 - 1, late_pair)
        late(heads - 2)
        close(heads - 3)
        late(heads - 1)
        close(heads - 2)

        def drain(h):
            for slot in (NEAR, CROSS, FAR):
                for kind in (0, 1):
                    key_value(kind, slot, h).wait_send()

        loop(0, heads, drain)
        for slot in (PARTNER, BELOW_PARTNER):
            query(slot).wait_send()
            reach(slot).wait_send()
        close(heads - 1)

    @pl.when(jnp.logical_not(inner))
    def _():
        pl.semaphore_wait(barrier, 4)
        greet(ready, {"ctx": near})
        greet(ready, {"ctx": near_partner})
        query(BELOW).start()
        reach(BELOW).start()
        query(PARTNER).start()
        reach(PARTNER).start()

        def start_own(h):
            for kind in (0, 1):
                key_value(kind, NEAR, h).start()

        loop(0, heads, start_own)
        load_w.start()
        pairs = ((OWN, position), (NEAR, near))
        use_bias(OWN, position, pairs)
        load_q.wait()
        load_k.wait()
        load_v.wait()
        loop(0, heads, lambda h: step(OWN, OWN, h, first=True))
        query(PARTNER).wait_recv()
        reach(PARTNER).wait_recv()
        use_bias(PARTNER, partner, pairs)
        loop(0, heads, lambda h: step(PARTNER, OWN, h, first=True))

        def early(h):
            wait_key_value(NEAR, h)
            step(PARTNER, NEAR, h)
            pack(PARTNER, h, side_part.at[h], side_stat.at[h])
            for copy in sideways(h):
                copy.start()
            step(OWN, NEAR, h)

        loop(0, heads, early)
        load_w.wait()

        def side_merge(h):
            for copy in sideways(h):
                copy.wait_recv()
            keep(OWN, h, merge(OWN, h, [(side_part_in.at[h], side_stat_in.at[h])]))

        loop(0, heads, side_merge)

        def drain(h):
            for kind in (0, 1):
                key_value(kind, NEAR, h).wait_send()

        loop(0, heads, drain)
        for slot in (PARTNER, BELOW):
            query(slot).wait_send()
            reach(slot).wait_send()

        def late(h, joined):
            parts = (0,) if joined else (1, 0)
            for which in parts:
                for copy in upward(which, h):
                    copy.wait_recv()
            finish(h, *[(up_part_in.at[which, h], up_stat_in.at[which, h]) for which in parts])

        def late_pair(p):
            late(2 * p, True)
            late(2 * p + 1, False)

        loop(0, heads // 2 - 1, late_pair)
        late(heads - 2, False)
        late(heads - 1, False)

    exchange(groups - 1).wait_recv()
    last_rows = pl.ds(pl.multiple_of((1 - side) * width + (groups - 1) * group, group), group)
    stores = []
    for t in range(tiles):
        cols = slice(t * tile, (t + 1) * tile)
        last = jnp.dot(other_ref[:, (groups - 1) * group :], w_ref[last_rows, cols], preferred_element_type=jnp.float32)
        out_ref[:, cols] = (sum_ref[:, cols] + last).astype(out_ref.dtype)
        stores.append(pltpu.make_async_copy(out_ref.at[:, cols], out_any.at[:, cols], store_sem.at[t]))
        stores[t].start()

    def drain_side(h):
        for copy in sideways(h):
            copy.wait_send()

    loop(0, heads, drain_side)
    loop(0, groups, lambda g: exchange(g).wait_send())

    @pl.when(inner)
    def _():
        def drain_up(h):
            for which in (0, 1):
                for copy in upward(which, h):
                    copy.wait_send()

        loop(0, heads, drain_up)

    for store in stores:
        store.wait()


def grid_call(queries, keys, values, out_weight, random_blocks, window_blocks, global_blocks):
    rows, width = queries.shape
    heads = width // HEAD
    dev_blocks = rows // BLOCK
    out_width = out_weight.shape[1]
    smem = pl.BlockSpec(memory_space=pltpu.SMEM)
    hbm = pl.BlockSpec(memory_space=pltpu.HBM)
    state = pltpu.VMEM((4, heads, rows, HEAD), jnp.float32)
    dma = pltpu.SemaphoreType.DMA
    return pl.pallas_call(
        grid_kernel,
        out_shape=jax.ShapeDtypeStruct((rows, out_width), jnp.bfloat16),
        in_specs=[smem] * 3 + [hbm] * 4,
        out_specs=pl.BlockSpec(memory_space=pl.ANY),
        scratch_shapes=[
            pltpu.VMEM((4, rows, width), jnp.bfloat16),
            pltpu.VMEM((4, rows, width), jnp.bfloat16),
            pltpu.VMEM((4, rows, width), jnp.bfloat16),
            pltpu.VMEM(out_weight.shape, jnp.bfloat16),
            pltpu.VMEM((4, dev_blocks, 8, HEAD), jnp.int32),
            pltpu.VMEM((4, 4, dev_blocks, 8, rows), jnp.float32),
            state,
            state,
            state,
            pltpu.VMEM((2, heads, rows, HEAD), jnp.bfloat16),
            pltpu.VMEM((2, heads, 8, rows), jnp.float32),
            pltpu.VMEM((2, heads, rows, HEAD), jnp.bfloat16),
            pltpu.VMEM((2, heads, 8, rows), jnp.float32),
            pltpu.VMEM((heads, rows, HEAD), jnp.bfloat16),
            pltpu.VMEM((heads, 8, rows), jnp.float32),
            pltpu.VMEM((heads, rows, HEAD), jnp.bfloat16),
            pltpu.VMEM((heads, 8, rows), jnp.float32),
            pltpu.VMEM((rows, width), jnp.bfloat16),
            pltpu.VMEM((rows, width), jnp.bfloat16),
            pltpu.VMEM((rows, out_width), jnp.float32),
            pltpu.VMEM((rows, out_width), jnp.bfloat16),
            dma((4,)),
            dma((2,)),
            dma((4, 2, heads)),
            dma((4, 2, heads)),
            dma((4,)),
            dma((4,)),
            dma((4,)),
            dma((4,)),
            dma((2, 2, heads)),
            dma((2, 2, heads)),
            dma((2, heads)),
            dma((2, heads)),
            dma((heads // 2,)),
            dma((heads // 2,)),
            pltpu.SemaphoreType.REGULAR,
        ],
        compiler_params=pltpu.CompilerParams(
            collective_id=0, has_side_effects=True, vmem_limit_bytes=60 << 20
        ),
    )(random_blocks.T, window_blocks, global_blocks, queries, keys, values, out_weight)


def per_device(*arguments):
    if lax.axis_size("ctx") == GRID_DEPTH * GRID_WIDTH:
        return grid_call(*arguments)
    return ring_call(*arguments)


def ring_place(index, count):
    odd = index % 2
    return (1 - odd) * (index // 2) + odd * (count - 1 - index // 2)


def ring_index(place, count):
    late = place // (count // 2)
    return (1 - late) * (2 * place) + late * (2 * (count - 1 - place) + 1)


def ring_kernel(
    count,
    random_ref,
    window_ref,
    global_ref,
    q_hbm,
    k_hbm,
    v_hbm,
    w_hbm,
    out_any,
    q_ref,
    w_ref,
    k_all,
    v_all,
    peak_ref,
    total_ref,
    acc_ref,
    own_ref,
    other_ref,
    sum_ref,
    out_ref,
    load_sem,
    send_sem,
    recv_sem,
    last_send,
    last_recv,
    pair_send,
    pair_recv,
):
    rows, width = q_ref.shape
    heads = width // HEAD
    dev_blocks = rows // BLOCK
    half = count // 2
    position = lax.axis_index("ctx")
    side = lax.axis_index("head")
    place = ring_place(position, count)
    right = ring_index((place + 1) % count, count)
    left = ring_index((place + count - 1) % count, count)

    load_k = pltpu.make_async_copy(k_hbm, k_all.at[0], load_sem.at[0])
    load_v = pltpu.make_async_copy(v_hbm, v_all.at[0], load_sem.at[1])
    load_q = pltpu.make_async_copy(q_hbm, q_ref, load_sem.at[2])
    load_w = pltpu.make_async_copy(w_hbm, w_ref, load_sem.at[3])
    load_k.start()
    load_v.start()
    load_q.start()

    barrier = pltpu.get_barrier_semaphore()
    pl.semaphore_signal(barrier, inc=1, device_id={"ctx": left}, device_id_type=MESH)
    pl.semaphore_signal(barrier, inc=1, device_id={"ctx": right}, device_id_type=MESH)
    pl.semaphore_signal(barrier, inc=1, device_id={"head": 1 - side}, device_id_type=MESH)
    pl.semaphore_wait(barrier, 3)

    def hop(stream, slot):
        buffer = k_all if stream in (K_FWD, K_BWD) else v_all
        forward = stream in (K_FWD, V_FWD)
        source = slot - 1 if forward else (slot + 1) % count
        return pltpu.make_async_remote_copy(
            src_ref=buffer.at[source],
            dst_ref=buffer.at[slot],
            send_sem=send_sem.at[stream, slot],
            recv_sem=recv_sem.at[stream, slot],
            device_id={"ctx": right if forward else left},
            device_id_type=MESH,
        )

    load_k.wait()
    hop(K_FWD, 1).start()
    hop(K_BWD, count - 1).start()
    load_v.wait()
    hop(V_FWD, 1).start()
    hop(V_BWD, count - 1).start()
    load_q.wait()
    load_w.start()

    peak_ref[...] = jnp.full_like(peak_ref, LARGE_NEG)
    total_ref[...] = jnp.zeros_like(total_ref)
    acc_ref[...] = jnp.zeros_like(acc_ref)
    scale = math.log2(math.e) / math.sqrt(HEAD)

    def use_bias(slot):
        owner = ring_index((place + count - slot) % count, count)
        row_block = lax.broadcasted_iota(jnp.int32, (rows, HEAD), 0) // BLOCK
        biases = []
        for b in range(dev_blocks):
            key_block = owner * dev_blocks + b
            bias = jnp.full((rows, HEAD), LARGE_NEG, jnp.float32)
            for a in range(dev_blocks):
                query_block = position * dev_blocks + a
                offset = jnp.abs(key_block - query_block)
                used = (offset <= window_ref[a]) & (offset <= WMAX)
                for g in range(GLOB):
                    used = used | (global_ref[g] == key_block)
                for r in range(RAND):
                    used = used | (random_ref[r, query_block] == key_block)
                bias = jnp.where(row_block == a, jnp.where(used, 0.0, LARGE_NEG), bias)
            biases.append(bias)
        return biases

    def attend_head(slot, h, biases):
        cols = pl.ds(h * HEAD, HEAD)
        if not isinstance(h, int):
            cols = pl.ds(pl.multiple_of(h * HEAD, HEAD), HEAD)
        scores = lax.dot_general(
            q_ref[:, cols],
            k_all[slot, :, cols],
            (((1,), (1,)), ((), ())),
            preferred_element_type=jnp.float32,
        )
        scores = scores * scale
        old_peak = peak_ref[h]
        best_peak = old_peak
        parts = []
        for b, bias in enumerate(biases):
            block = scores[:, b * BLOCK : (b + 1) * BLOCK]
            row_peak = jnp.max(block, axis=1, keepdims=True)
            weights = jnp.exp2(block - row_peak)
            part = jnp.dot(
                weights.astype(jnp.bfloat16),
                v_all[slot, b * BLOCK : (b + 1) * BLOCK, cols],
                preferred_element_type=jnp.float32,
            )
            used_peak = row_peak + bias
            best_peak = jnp.maximum(best_peak, used_peak)
            parts.append((used_peak, weights, part))
        fade = jnp.exp2(old_peak - best_peak)
        total = total_ref[h] * fade
        acc = acc_ref[h] * fade
        for used_peak, weights, part in parts:
            factor = jnp.exp2(used_peak - best_peak)
            total = total + weights * factor
            acc = acc + part * factor
        return best_peak, total, acc

    def attend(slot):
        biases = use_bias(slot)

        def one_head(h, carry):
            peak_ref[h], total_ref[h], acc_ref[h] = attend_head(slot, h, biases)
            return carry

        lax.fori_loop(0, heads, one_head, 0, unroll=2)

    def last_hop(stream, h):
        buffer = k_all if stream == K_FWD else v_all
        forward = h % 2 == 0
        cols = pl.ds(h * HEAD, HEAD)
        return pltpu.make_async_remote_copy(
            src_ref=buffer.at[half - 1 if forward else half + 1, :, cols],
            dst_ref=buffer.at[half, :, cols],
            send_sem=last_send.at[stream, h],
            recv_sem=last_recv.at[stream, h],
            device_id={"ctx": right if forward else left},
            device_id_type=MESH,
        )

    attend(0)

    def middle(step, carry):
        back = count - step
        hop(K_FWD, step).wait_recv()
        hop(K_FWD, step + 1).start()
        hop(K_BWD, back).wait_recv()
        hop(K_BWD, back - 1).start()
        hop(V_FWD, step).wait_recv()
        hop(V_FWD, step + 1).start()
        hop(V_BWD, back).wait_recv()
        hop(V_BWD, back - 1).start()
        attend(step)
        attend(back)
        return carry

    lax.fori_loop(1, half - 1, middle, 0)

    for side_of, key_stream in ((0, K_FWD), (1, K_BWD)):
        hop(key_stream, half + 1 if side_of else half - 1).wait_recv()
        for pair in range(min(2, heads // 2)):
            last_hop(K_FWD, 2 * pair + side_of).start()
    for side_of, value_stream in ((0, V_FWD), (1, V_BWD)):
        hop(value_stream, half + 1 if side_of else half - 1).wait_recv()
        for pair in range(heads // 2):
            last_hop(V_FWD, 2 * pair + side_of).start()
            if pair + 2 < heads // 2:
                last_hop(K_FWD, 2 * (pair + 2) + side_of).start()
    attend(half - 1)
    attend(half + 1)
    load_w.wait()
    biases = use_bias(half)
    group = 2 * HEAD

    def exchange(g):
        cols = pl.ds(g * group, group)
        return pltpu.make_async_remote_copy(
            src_ref=own_ref.at[:, cols],
            dst_ref=other_ref.at[:, cols],
            send_sem=pair_send.at[g],
            recv_sem=pair_recv.at[g],
            device_id={"head": 1 - side},
            device_id_type=MESH,
        )

    def project(source, which, g):
        w_rows = pl.ds(pl.multiple_of(which * width + g * group, group), group)
        return jnp.dot(
            source[:, g * group : (g + 1) * group],
            w_ref[w_rows, :],
            preferred_element_type=jnp.float32,
        )

    groups = width // group
    for g in range(groups):
        for h in (2 * g, 2 * g + 1):
            last_hop(K_FWD, h).wait_recv()
            last_hop(V_FWD, h).wait_recv()
            _, total, acc = attend_head(half, h, biases)
            total = jnp.sum(total, axis=1, keepdims=True)
            own_ref[:, h * HEAD : (h + 1) * HEAD] = (acc / total).astype(jnp.bfloat16)
        exchange(g).start()
        if g == 0:
            sum_ref[...] = project(own_ref, side, g)
        else:
            exchange(g - 1).wait_recv()
            sum_ref[...] += project(other_ref, 1 - side, g - 1) + project(own_ref, side, g)
    exchange(groups - 1).wait_recv()
    out_ref[...] = (sum_ref[...] + project(other_ref, 1 - side, groups - 1)).astype(out_ref.dtype)

    store = pltpu.make_async_copy(out_ref, out_any, load_sem.at[4])
    store.start()
    for g in range(groups):
        exchange(g).wait_send()
    for h in range(heads):
        last_hop(K_FWD, h).wait_send()
        last_hop(V_FWD, h).wait_send()

    def drain(step, carry):
        hop(K_FWD, step).wait_send()
        hop(V_FWD, step).wait_send()
        hop(K_BWD, count - step).wait_send()
        hop(V_BWD, count - step).wait_send()
        return carry

    lax.fori_loop(1, half, drain, 0)
    store.wait()


def ring_call(queries, keys, values, out_weight, random_blocks, window_blocks, global_blocks):
    count = lax.axis_size("ctx")
    rows, width = queries.shape
    heads = width // HEAD
    out_width = out_weight.shape[1]
    smem = pl.BlockSpec(memory_space=pltpu.SMEM)
    hbm = pl.BlockSpec(memory_space=pltpu.HBM)
    return pl.pallas_call(
        functools.partial(ring_kernel, count),
        out_shape=jax.ShapeDtypeStruct((rows, out_width), jnp.bfloat16),
        in_specs=[smem] * 3 + [hbm] * 4,
        out_specs=pl.BlockSpec(memory_space=pl.ANY),
        scratch_shapes=[
            pltpu.VMEM((rows, width), jnp.bfloat16),
            pltpu.VMEM(out_weight.shape, jnp.bfloat16),
            pltpu.VMEM((count, rows, width), jnp.bfloat16),
            pltpu.VMEM((count, rows, width), jnp.bfloat16),
            pltpu.VMEM((heads, rows, HEAD), jnp.float32),
            pltpu.VMEM((heads, rows, HEAD), jnp.float32),
            pltpu.VMEM((heads, rows, HEAD), jnp.float32),
            pltpu.VMEM((rows, width), jnp.bfloat16),
            pltpu.VMEM((rows, width), jnp.bfloat16),
            pltpu.VMEM((rows, out_width), jnp.float32),
            pltpu.VMEM((rows, out_width), jnp.bfloat16),
            pltpu.SemaphoreType.DMA((5,)),
            pltpu.SemaphoreType.DMA((4, count)),
            pltpu.SemaphoreType.DMA((4, count)),
            pltpu.SemaphoreType.DMA((2, heads)),
            pltpu.SemaphoreType.DMA((2, heads)),
            pltpu.SemaphoreType.DMA((heads // 2,)),
            pltpu.SemaphoreType.DMA((heads // 2,)),
        ],
        compiler_params=pltpu.CompilerParams(
            collective_id=1, has_side_effects=True, vmem_limit_bytes=60 << 20
        ),
    )(random_blocks.T, window_blocks, global_blocks, queries, keys, values, out_weight)


def solution(mesh):
    placed = (
        P(("groups", "ctx"), "head"),
        P(("groups", "ctx"), "head"),
        P(("groups", "ctx"), "head"),
        P(None, "head"),
        P("groups", None),
        P(("groups", "ctx")),
        P("groups"),
    )
    return jax.shard_map(
        per_device,
        mesh=mesh,
        in_specs=placed,
        out_specs=P(("groups", "ctx"), "head"),
        check_vma=False,
    )
```

```python
import functools
import math

import jax
import jax.numpy as jnp
from jax import lax
from jax.experimental import pallas as pl
from jax.experimental.pallas import tpu as pltpu
from jax.sharding import PartitionSpec as P

HEAD = 128
BLOCK = 128
WMAX = 1
GLOB = 2
RAND = 3

LARGE_NEG = -1e30
MESH = pl.DeviceIdType.MESH

K_FWD, V_FWD, K_BWD, V_BWD = range(4)


GRID_DEPTH = 4
GRID_WIDTH = 2
OWN, NEAR, CROSS, FAR = range(4)
PARTNER, BELOW, BELOW_PARTNER = 1, 2, 3
SCALE = math.log2(math.e) / math.sqrt(HEAD)


def grid_kernel(
    table_ref,
    q_hbm,
    k_hbm,
    v_hbm,
    w_hbm,
    out_ref,
    q_all,
    k_all,
    v_all,
    w_ref,
    win_all,
    bias_ref,
    peak_ref,
    total_ref,
    acc_ref,
    up_part,
    up_stat,
    up_part_in,
    up_stat_in,
    side_part,
    side_stat,
    side_part_in,
    side_stat_in,
    own_ref,
    other_ref,
    sum_ref,
    load_sem,
    kv_send,
    kv_recv,
    q_send,
    q_recv,
    win_send,
    win_recv,
    up_send,
    up_recv,
    side_send,
    side_recv,
    pair_send,
    pair_recv,
    ready,
):
    rows, width = q_hbm.shape
    heads = width // HEAD
    half = heads // 2
    dev_blocks = rows // BLOCK
    position = lax.axis_index("ctx")
    side = lax.axis_index("head")
    depth, column = position // GRID_WIDTH, position % GRID_WIDTH
    inner = (depth > 0) & (depth < GRID_DEPTH - 1)

    def mate(level):
        return level + 1 - 2 * (level % 2)

    cross_depth = GRID_DEPTH - 1 - depth
    partner = depth * GRID_WIDTH + 1 - column
    near = mate(depth) * GRID_WIDTH + column
    near_partner = mate(depth) * GRID_WIDTH + 1 - column
    cross = cross_depth * GRID_WIDTH + column
    far = mate(cross_depth) * GRID_WIDTH + column

    def at(h):
        if isinstance(h, int):
            return pl.ds(h * HEAD, HEAD)
        return pl.ds(pl.multiple_of(h * HEAD, HEAD), HEAD)

    def send(src, dst, send_sem, recv_sem, target):
        return pltpu.make_async_remote_copy(
            src_ref=src,
            dst_ref=dst,
            send_sem=send_sem,
            recv_sem=recv_sem,
            device_id=target,
            device_id_type=MESH,
        )

    def key_value(kind, slot, h):
        source = {
            NEAR: (k_hbm, v_hbm)[kind],
            CROSS: (k_hbm, v_hbm)[kind],
            FAR: (k_all, v_all)[kind].at[NEAR],
        }[slot]
        return send(
            source.at[:, at(h)],
            (k_all, v_all)[kind].at[slot, :, at(h)],
            kv_send.at[slot, kind, h],
            kv_recv.at[slot, kind, h],
            {"ctx": near if slot == NEAR else cross},
        )

    def query(slot):
        source = q_all.at[BELOW] if slot == BELOW_PARTNER else q_hbm
        return send(
            source,
            q_all.at[slot],
            q_send.at[slot],
            q_recv.at[slot],
            {"ctx": near if slot == BELOW else partner},
        )

    def reach(slot):
        return send(
            win_all.at[BELOW if slot == BELOW_PARTNER else OWN],
            win_all.at[slot],
            win_send.at[slot],
            win_recv.at[slot],
            {"ctx": near if slot == BELOW else partner},
        )

    def upward(which, h):
        target = {"ctx": near_partner if which else near}
        return (
            send(up_stat.at[which, h, 0:1], up_stat_in.at[which, h, 0:1], up_send.at[1, which, h], up_recv.at[1, which, h], target),
            send(up_part.at[which, h], up_part_in.at[which, h], up_send.at[0, which, h], up_recv.at[0, which, h], target),
        )

    def sideways(h):
        target = {"ctx": partner}
        return (
            send(side_stat.at[h, 0:1], side_stat_in.at[h, 0:1], side_send.at[1, h], side_recv.at[1, h], target),
            send(side_part.at[h], side_part_in.at[h], side_send.at[0, h], side_recv.at[0, h], target),
        )

    load_q = pltpu.make_async_copy(q_hbm, q_all.at[OWN], load_sem.at[0])
    load_k = pltpu.make_async_copy(k_hbm, k_all.at[OWN], load_sem.at[1])
    load_v = pltpu.make_async_copy(v_hbm, v_all.at[OWN], load_sem.at[2])
    load_w = pltpu.make_async_copy(w_hbm, w_ref, load_sem.at[3])
    barrier = pltpu.get_barrier_semaphore()

    def greet(semaphore, target):
        pl.semaphore_signal(semaphore, inc=1, device_id=target, device_id_type=MESH)

    @pl.when(inner)
    def _():
        greet(barrier, {"ctx": cross})
        greet(barrier, {"ctx": near})
        greet(barrier, {"ctx": near_partner})

    greet(barrier, {"ctx": partner})
    greet(barrier, {"head": 1 - side})
    load_q.start()
    load_k.start()
    load_v.start()
    for a in range(dev_blocks):
        win_all[OWN, a] = jnp.full((8, HEAD), table_ref[RAND, a], jnp.int32)

    def use_bias(q, query_chip, pairs):
        for k, key_chip in pairs:
            for a in range(dev_blocks):
                query_block = query_chip * dev_blocks + a
                for b in range(dev_blocks):
                    key_block = key_chip * dev_blocks + b
                    offset = jnp.abs(key_block - query_block)
                    needed = jnp.where(offset <= WMAX, offset, 1 << 30)
                    used = table_ref[RAND + 1, 0] == key_block
                    for g in range(1, GLOB):
                        used = used | (table_ref[RAND + 1, g] == key_block)
                    for r in range(RAND):
                        used = used | (table_ref[r, query_block] == key_block)
                    bias = jnp.where(used, 0.0, LARGE_NEG)
                    bias = jnp.where(win_all[q, a] >= needed, 0.0, bias)
                    bias_ref[q, k, a, :, b * BLOCK : (b + 1) * BLOCK] = bias

    def steps(pairs, h, first=False):
        cols = at(h)
        every = [
            lax.dot_general(
                q_all[q, :, cols],
                k_all[k, :, cols],
                (((1,), (1,)), ((), ())),
                preferred_element_type=jnp.float32,
            )
            for q, k in pairs
        ]
        held = []
        for (q, k), scores in zip(pairs, every):
            for a in range(dev_blocks):
                span = slice(a * BLOCK, (a + 1) * BLOCK)
                block = scores[span] * SCALE + bias_ref[q, k, a, 0:1, :]
                best = jnp.max(block, axis=1, keepdims=True)
                old = None
                if first:
                    best = jnp.broadcast_to(best, (BLOCK, HEAD))
                else:
                    old = peak_ref[q, h, span]
                    best = jnp.maximum(old, best)
                weights = [
                    jnp.exp2(block[:, b * BLOCK : (b + 1) * BLOCK] - best) for b in range(dev_blocks)
                ]
                total = functools.reduce(jnp.add, weights)
                rounded = jnp.concatenate([w.astype(jnp.bfloat16) for w in weights], axis=1)
                held.append((old, best, total, rounded))
        for i, (q, k) in enumerate(pairs):
            mine = held[i * dev_blocks : (i + 1) * dev_blocks]
            part = jnp.dot(
                jnp.concatenate([m[3] for m in mine], axis=0),
                v_all[k, :, cols],
                preferred_element_type=jnp.float32,
            )
            for a, (old, best, total, _) in enumerate(mine):
                span = slice(a * BLOCK, (a + 1) * BLOCK)
                acc = part[span]
                if not first:
                    fade = jnp.exp2(old - best)
                    total = total + total_ref[q, h, span] * fade
                    acc = acc + acc_ref[q, h, span] * fade
                peak_ref[q, h, span] = best
                total_ref[q, h, span] = total
                acc_ref[q, h, span] = acc

    def step(q, k, h, first=False):
        steps([(q, k)], h, first)

    def pack(q, h, part, stat):
        total = jnp.sum(total_ref[q, h], axis=1, keepdims=True)
        part[...] = (acc_ref[q, h] / total).astype(jnp.bfloat16)
        level = peak_ref[q, h] + jnp.log2(total)
        stat[...] = level.T[:8]

    def merge(q, h, incoming):
        old = peak_ref[q, h]
        levels = [jnp.broadcast_to(stat[0:1, :], (HEAD, rows)).T for _, stat in incoming]
        best = functools.reduce(jnp.maximum, levels, old)
        fade = jnp.exp2(old - best)
        total = total_ref[q, h] * fade
        acc = acc_ref[q, h] * fade
        for level, (part, _) in zip(levels, incoming):
            gain = jnp.exp2(level - best)
            total = total + gain * (1.0 / HEAD)
            acc = acc + part[...].astype(jnp.float32) * gain
        return best, total, acc

    def keep(q, h, state):
        peak_ref[q, h], total_ref[q, h], acc_ref[q, h] = state

    group = 2 * HEAD
    groups = width // group
    tiles = 2
    tile = out_ref.shape[1] // tiles

    def group_cols(g):
        if isinstance(g, int):
            return pl.ds(g * group, group)
        return pl.ds(pl.multiple_of(g * group, group), group)

    def exchange(g):
        return send(
            own_ref.at[:, group_cols(g)],
            other_ref.at[:, group_cols(g)],
            pair_send.at[g],
            pair_recv.at[g],
            {"head": 1 - side},
        )

    def project(source, which, g):
        w_rows = pl.ds(pl.multiple_of(which * width + g * group, group), group)
        return jnp.dot(source[:, group_cols(g)], w_ref[w_rows, :], preferred_element_type=jnp.float32)

    def finish(h, *incoming):
        _, total, acc = merge(OWN, h, incoming)
        total = jnp.sum(total, axis=1, keepdims=True)
        own_ref[:, at(h)] = (acc / total).astype(jnp.bfloat16)

        @pl.when(h % 2 == 1)
        def _():
            g = h // 2
            exchange(g).start()

            @pl.when(g == 0)
            def _():
                sum_ref[...] = project(own_ref, side, g)

            @pl.when(g > 0)
            def _():
                exchange(g - 1).wait_recv()
                sum_ref[...] += project(own_ref, side, g) + project(other_ref, 1 - side, g - 1)

    def loop(lower, upper, body):
        def run(h, carry):
            body(h)
            return carry

        lax.fori_loop(lower, upper, run, 0)

    def wait_key_value(slot, h):
        key_value(0, slot, h).wait_recv()
        key_value(1, slot, h).wait_recv()

    @pl.when(inner)
    def _():
        pl.semaphore_wait(barrier, 3)

        def start_own(slot, h):
            for kind in (0, 1):
                key_value(kind, slot, h).start()

        start_own(CROSS, 0)
        query(PARTNER).start()
        reach(PARTNER).start()
        loop(1, heads, lambda h: start_own(CROSS, h))
        pl.semaphore_wait(ready, 2)
        loop(0, heads, lambda h: start_own(NEAR, h))
        load_w.start()
        pairs = ((OWN, position), (NEAR, near), (CROSS, cross), (FAR, far))
        use_bias(OWN, position, pairs)
        load_q.wait()
        load_k.wait()
        load_v.wait()
        loop(0, heads, lambda h: step(OWN, OWN, h, first=True))

        query(BELOW).wait_recv()
        reach(BELOW).wait_recv()
        query(BELOW_PARTNER).start()
        reach(BELOW_PARTNER).start()
        query(PARTNER).wait_recv()
        reach(PARTNER).wait_recv()
        use_bias(PARTNER, partner, pairs)
        use_bias(BELOW, near, pairs[2:])
        loop(0, heads, lambda h: step(PARTNER, OWN, h, first=True))

        def pass_on(h):
            wait_key_value(NEAR, h)
            for kind in (0, 1):
                key_value(kind, FAR, h).start()

        def early(h):
            @pl.when(h >= half)
            def _():
                pass_on(h - half)
                steps([(PARTNER, NEAR), (OWN, NEAR)], h - half)

            wait_key_value(CROSS, h)
            steps([(OWN, CROSS), (PARTNER, CROSS)], h)
            step(BELOW, CROSS, h, first=True)

        loop(0, heads, early)
        query(BELOW_PARTNER).wait_recv()
        reach(BELOW_PARTNER).wait_recv()
        use_bias(BELOW_PARTNER, near_partner, pairs[2:])

        def ship(which, q, h):
            pack(q, h, up_part.at[which, h], up_stat.at[which, h])
            for copy in upward(which, h):
                copy.start()

        def close(h):
            for copy in sideways(h):
                copy.wait_recv()
            finish(h, (side_part_in.at[h], side_stat_in.at[h]))

        def ship_side(h):
            pack(PARTNER, h, side_part.at[h], side_stat.at[h])
            for copy in sideways(h):
                copy.start()

        def late(h):
            @pl.when(h < half)
            def _():
                pass_on(h + half)
                steps([(PARTNER, NEAR), (OWN, NEAR)], h + half)

            step(BELOW_PARTNER, CROSS, h, first=True)
            wait_key_value(FAR, h)
            step(BELOW_PARTNER, FAR, h)
            ship(1, BELOW_PARTNER, h)
            steps([(PARTNER, FAR), (BELOW, FAR)], h)
            ship_side(h)
            ship(0, BELOW, h)
            step(OWN, FAR, h)

        def drain(h):
            for slot in (NEAR, CROSS, FAR):
                for kind in (0, 1):
                    key_value(kind, slot, h).wait_send()

        def late_or_drain(h):
            @pl.when(h < heads)
            def _():
                late(h)

            @pl.when(h == 0)
            def _():
                load_w.wait()

            @pl.when(h == heads)
            def _():
                loop(0, heads, drain)
                for slot in (PARTNER, BELOW_PARTNER):
                    query(slot).wait_send()
                    reach(slot).wait_send()

            @pl.when(h > 0)
            def _():
                close(h - 1)

        loop(0, heads + 1, late_or_drain)

    @pl.when(jnp.logical_not(inner))
    def _():
        pl.semaphore_wait(barrier, 4)
        greet(ready, {"ctx": near})
        greet(ready, {"ctx": near_partner})
        query(BELOW).start()
        reach(BELOW).start()
        query(PARTNER).start()
        reach(PARTNER).start()

        def start_own(h):
            for kind in (0, 1):
                key_value(kind, NEAR, h).start()

        loop(0, heads, start_own)
        load_w.start()
        pairs = ((OWN, position), (NEAR, near))
        use_bias(OWN, position, pairs)
        load_q.wait()
        load_k.wait()
        load_v.wait()
        loop(0, heads, lambda h: step(OWN, OWN, h, first=True))
        query(PARTNER).wait_recv()
        reach(PARTNER).wait_recv()
        use_bias(PARTNER, partner, pairs)
        loop(0, heads, lambda h: step(PARTNER, OWN, h, first=True))

        def early(h):
            wait_key_value(NEAR, h)
            step(PARTNER, NEAR, h)
            pack(PARTNER, h, side_part.at[h], side_stat.at[h])
            for copy in sideways(h):
                copy.start()
            step(OWN, NEAR, h)

        loop(0, heads, early)
        load_w.wait()

        def side_merge(h):
            for copy in sideways(h):
                copy.wait_recv()
            keep(OWN, h, merge(OWN, h, [(side_part_in.at[h], side_stat_in.at[h])]))

        loop(0, heads, side_merge)

        def drain(h):
            for kind in (0, 1):
                key_value(kind, NEAR, h).wait_send()

        loop(0, heads, drain)
        for slot in (PARTNER, BELOW):
            query(slot).wait_send()
            reach(slot).wait_send()

        def late(h):
            for which in (1, 0):
                for copy in upward(which, h):
                    copy.wait_recv()
            finish(h, *[(up_part_in.at[which, h], up_stat_in.at[which, h]) for which in (1, 0)])

        loop(0, heads, late)

    exchange(groups - 1).wait_recv()
    out_ref[...] = (sum_ref[...] + project(other_ref, 1 - side, groups - 1)).astype(out_ref.dtype)

    def drain_side(h):
        for copy in sideways(h):
            copy.wait_send()

    loop(0, heads, drain_side)
    loop(0, groups, lambda g: exchange(g).wait_send())

    @pl.when(inner)
    def _():
        def drain_up(h):
            for which in (0, 1):
                for copy in upward(which, h):
                    copy.wait_send()

        loop(0, heads, drain_up)


def grid_call(queries, keys, values, out_weight, random_blocks, window_blocks, global_blocks):
    rows, width = queries.shape
    heads = width // HEAD
    dev_blocks = rows // BLOCK
    out_width = out_weight.shape[1]
    smem = pl.BlockSpec(memory_space=pltpu.SMEM)
    hbm = pl.BlockSpec(memory_space=pltpu.HBM)
    state = pltpu.VMEM((4, heads, rows, HEAD), jnp.float32)
    dma = pltpu.SemaphoreType.DMA
    blocks = random_blocks.shape[0]
    table = (
        jnp.pad(random_blocks.T, ((0, 2), (0, 0)))
        + jnp.pad(window_blocks[None], ((RAND, 1), (0, blocks - dev_blocks)))
        + jnp.pad(global_blocks[None], ((RAND + 1, 0), (0, blocks - GLOB)))
    )
    return pl.pallas_call(
        grid_kernel,
        out_shape=jax.ShapeDtypeStruct((rows, out_width), jnp.bfloat16),
        in_specs=[smem] + [hbm] * 4,
        out_specs=pl.BlockSpec(memory_space=pltpu.VMEM),
        scratch_shapes=[
            pltpu.VMEM((4, rows, width), jnp.bfloat16),
            pltpu.VMEM((4, rows, width), jnp.bfloat16),
            pltpu.VMEM((4, rows, width), jnp.bfloat16),
            pltpu.VMEM(out_weight.shape, jnp.bfloat16),
            pltpu.VMEM((4, dev_blocks, 8, HEAD), jnp.int32),
            pltpu.VMEM((4, 4, dev_blocks, 8, rows), jnp.float32),
            state,
            state,
            state,
            pltpu.VMEM((2, heads, rows, HEAD), jnp.bfloat16),
            pltpu.VMEM((2, heads, 8, rows), jnp.float32),
            pltpu.VMEM((2, heads, rows, HEAD), jnp.bfloat16),
            pltpu.VMEM((2, heads, 8, rows), jnp.float32),
            pltpu.VMEM((heads, rows, HEAD), jnp.bfloat16),
            pltpu.VMEM((heads, 8, rows), jnp.float32),
            pltpu.VMEM((heads, rows, HEAD), jnp.bfloat16),
            pltpu.VMEM((heads, 8, rows), jnp.float32),
            pltpu.VMEM((rows, width), jnp.bfloat16),
            pltpu.VMEM((rows, width), jnp.bfloat16),
            pltpu.VMEM((rows, out_width), jnp.float32),
            dma((4,)),
            dma((4, 2, heads)),
            dma((4, 2, heads)),
            dma((4,)),
            dma((4,)),
            dma((4,)),
            dma((4,)),
            dma((2, 2, heads)),
            dma((2, 2, heads)),
            dma((2, heads)),
            dma((2, heads)),
            dma((heads // 2,)),
            dma((heads // 2,)),
            pltpu.SemaphoreType.REGULAR,
        ],
        compiler_params=pltpu.CompilerParams(
            collective_id=0, has_side_effects=True, vmem_limit_bytes=53 << 20
        ),
    )(table, queries, keys, values, out_weight)


def per_device(*arguments):
    if lax.axis_size("ctx") == GRID_DEPTH * GRID_WIDTH:
        return grid_call(*arguments)
    return ring_call(*arguments)


def ring_place(index, count):
    odd = index % 2
    return (1 - odd) * (index // 2) + odd * (count - 1 - index // 2)


def ring_index(place, count):
    late = place // (count // 2)
    return (1 - late) * (2 * place) + late * (2 * (count - 1 - place) + 1)


def ring_kernel(
    count,
    random_ref,
    window_ref,
    global_ref,
    q_hbm,
    k_hbm,
    v_hbm,
    w_hbm,
    out_any,
    q_ref,
    w_ref,
    k_all,
    v_all,
    peak_ref,
    total_ref,
    acc_ref,
    own_ref,
    other_ref,
    sum_ref,
    out_ref,
    load_sem,
    send_sem,
    recv_sem,
    last_send,
    last_recv,
    pair_send,
    pair_recv,
):
    rows, width = q_ref.shape
    heads = width // HEAD
    dev_blocks = rows // BLOCK
    half = count // 2
    position = lax.axis_index("ctx")
    side = lax.axis_index("head")
    place = ring_place(position, count)
    right = ring_index((place + 1) % count, count)
    left = ring_index((place + count - 1) % count, count)

    load_k = pltpu.make_async_copy(k_hbm, k_all.at[0], load_sem.at[0])
    load_v = pltpu.make_async_copy(v_hbm, v_all.at[0], load_sem.at[1])
    load_q = pltpu.make_async_copy(q_hbm, q_ref, load_sem.at[2])
    load_w = pltpu.make_async_copy(w_hbm, w_ref, load_sem.at[3])
    load_k.start()
    load_v.start()
    load_q.start()

    barrier = pltpu.get_barrier_semaphore()
    pl.semaphore_signal(barrier, inc=1, device_id={"ctx": left}, device_id_type=MESH)
    pl.semaphore_signal(barrier, inc=1, device_id={"ctx": right}, device_id_type=MESH)
    pl.semaphore_signal(barrier, inc=1, device_id={"head": 1 - side}, device_id_type=MESH)
    pl.semaphore_wait(barrier, 3)

    def hop(stream, slot):
        buffer = k_all if stream in (K_FWD, K_BWD) else v_all
        forward = stream in (K_FWD, V_FWD)
        source = slot - 1 if forward else (slot + 1) % count
        return pltpu.make_async_remote_copy(
            src_ref=buffer.at[source],
            dst_ref=buffer.at[slot],
            send_sem=send_sem.at[stream, slot],
            recv_sem=recv_sem.at[stream, slot],
            device_id={"ctx": right if forward else left},
            device_id_type=MESH,
        )

    load_k.wait()
    hop(K_FWD, 1).start()
    hop(K_BWD, count - 1).start()
    load_v.wait()
    hop(V_FWD, 1).start()
    hop(V_BWD, count - 1).start()
    load_q.wait()
    load_w.start()

    peak_ref[...] = jnp.full_like(peak_ref, LARGE_NEG)
    total_ref[...] = jnp.zeros_like(total_ref)
    acc_ref[...] = jnp.zeros_like(acc_ref)
    scale = math.log2(math.e) / math.sqrt(HEAD)

    def use_bias(slot):
        owner = ring_index((place + count - slot) % count, count)
        row_block = lax.broadcasted_iota(jnp.int32, (rows, HEAD), 0) // BLOCK
        biases = []
        for b in range(dev_blocks):
            key_block = owner * dev_blocks + b
            bias = jnp.full((rows, HEAD), LARGE_NEG, jnp.float32)
            for a in range(dev_blocks):
                query_block = position * dev_blocks + a
                offset = jnp.abs(key_block - query_block)
                used = (offset <= window_ref[a]) & (offset <= WMAX)
                for g in range(GLOB):
                    used = used | (global_ref[g] == key_block)
                for r in range(RAND):
                    used = used | (random_ref[r, query_block] == key_block)
                bias = jnp.where(row_block == a, jnp.where(used, 0.0, LARGE_NEG), bias)
            biases.append(bias)
        return biases

    def attend_head(slot, h, biases):
        cols = pl.ds(h * HEAD, HEAD)
        if not isinstance(h, int):
            cols = pl.ds(pl.multiple_of(h * HEAD, HEAD), HEAD)
        scores = lax.dot_general(
            q_ref[:, cols],
            k_all[slot, :, cols],
            (((1,), (1,)), ((), ())),
            preferred_element_type=jnp.float32,
        )
        scores = scores * scale
        old_peak = peak_ref[h]
        best_peak = old_peak
        parts = []
        for b, bias in enumerate(biases):
            block = scores[:, b * BLOCK : (b + 1) * BLOCK]
            row_peak = jnp.max(block, axis=1, keepdims=True)
            weights = jnp.exp2(block - row_peak)
            part = jnp.dot(
                weights.astype(jnp.bfloat16),
                v_all[slot, b * BLOCK : (b + 1) * BLOCK, cols],
                preferred_element_type=jnp.float32,
            )
            used_peak = row_peak + bias
            best_peak = jnp.maximum(best_peak, used_peak)
            parts.append((used_peak, weights, part))
        fade = jnp.exp2(old_peak - best_peak)
        total = total_ref[h] * fade
        acc = acc_ref[h] * fade
        for used_peak, weights, part in parts:
            factor = jnp.exp2(used_peak - best_peak)
            total = total + weights * factor
            acc = acc + part * factor
        return best_peak, total, acc

    def attend(slot):
        biases = use_bias(slot)

        def one_head(h, carry):
            peak_ref[h], total_ref[h], acc_ref[h] = attend_head(slot, h, biases)
            return carry

        lax.fori_loop(0, heads, one_head, 0, unroll=2)

    def last_hop(stream, h):
        buffer = k_all if stream == K_FWD else v_all
        forward = h % 2 == 0
        cols = pl.ds(h * HEAD, HEAD)
        return pltpu.make_async_remote_copy(
            src_ref=buffer.at[half - 1 if forward else half + 1, :, cols],
            dst_ref=buffer.at[half, :, cols],
            send_sem=last_send.at[stream, h],
            recv_sem=last_recv.at[stream, h],
            device_id={"ctx": right if forward else left},
            device_id_type=MESH,
        )

    attend(0)

    def middle(step, carry):
        back = count - step
        hop(K_FWD, step).wait_recv()
        hop(K_FWD, step + 1).start()
        hop(K_BWD, back).wait_recv()
        hop(K_BWD, back - 1).start()
        hop(V_FWD, step).wait_recv()
        hop(V_FWD, step + 1).start()
        hop(V_BWD, back).wait_recv()
        hop(V_BWD, back - 1).start()
        attend(step)
        attend(back)
        return carry

    lax.fori_loop(1, half - 1, middle, 0)

    for side_of, key_stream in ((0, K_FWD), (1, K_BWD)):
        hop(key_stream, half + 1 if side_of else half - 1).wait_recv()
        for pair in range(min(2, heads // 2)):
            last_hop(K_FWD, 2 * pair + side_of).start()
    for side_of, value_stream in ((0, V_FWD), (1, V_BWD)):
        hop(value_stream, half + 1 if side_of else half - 1).wait_recv()
        for pair in range(heads // 2):
            last_hop(V_FWD, 2 * pair + side_of).start()
            if pair + 2 < heads // 2:
                last_hop(K_FWD, 2 * (pair + 2) + side_of).start()
    attend(half - 1)
    attend(half + 1)
    load_w.wait()
    biases = use_bias(half)
    group = 2 * HEAD

    def exchange(g):
        cols = pl.ds(g * group, group)
        return pltpu.make_async_remote_copy(
            src_ref=own_ref.at[:, cols],
            dst_ref=other_ref.at[:, cols],
            send_sem=pair_send.at[g],
            recv_sem=pair_recv.at[g],
            device_id={"head": 1 - side},
            device_id_type=MESH,
        )

    def project(source, which, g):
        w_rows = pl.ds(pl.multiple_of(which * width + g * group, group), group)
        return jnp.dot(
            source[:, g * group : (g + 1) * group],
            w_ref[w_rows, :],
            preferred_element_type=jnp.float32,
        )

    groups = width // group
    for g in range(groups):
        for h in (2 * g, 2 * g + 1):
            last_hop(K_FWD, h).wait_recv()
            last_hop(V_FWD, h).wait_recv()
            _, total, acc = attend_head(half, h, biases)
            total = jnp.sum(total, axis=1, keepdims=True)
            own_ref[:, h * HEAD : (h + 1) * HEAD] = (acc / total).astype(jnp.bfloat16)
        exchange(g).start()
        if g == 0:
            sum_ref[...] = project(own_ref, side, g)
        else:
            exchange(g - 1).wait_recv()
            sum_ref[...] += project(other_ref, 1 - side, g - 1) + project(own_ref, side, g)
    exchange(groups - 1).wait_recv()
    out_ref[...] = (sum_ref[...] + project(other_ref, 1 - side, groups - 1)).astype(out_ref.dtype)

    store = pltpu.make_async_copy(out_ref, out_any, load_sem.at[4])
    store.start()
    for g in range(groups):
        exchange(g).wait_send()
    for h in range(heads):
        last_hop(K_FWD, h).wait_send()
        last_hop(V_FWD, h).wait_send()

    def drain(step, carry):
        hop(K_FWD, step).wait_send()
        hop(V_FWD, step).wait_send()
        hop(K_BWD, count - step).wait_send()
        hop(V_BWD, count - step).wait_send()
        return carry

    lax.fori_loop(1, half, drain, 0)
    store.wait()


def ring_call(queries, keys, values, out_weight, random_blocks, window_blocks, global_blocks):
    count = lax.axis_size("ctx")
    rows, width = queries.shape
    heads = width // HEAD
    out_width = out_weight.shape[1]
    smem = pl.BlockSpec(memory_space=pltpu.SMEM)
    hbm = pl.BlockSpec(memory_space=pltpu.HBM)
    return pl.pallas_call(
        functools.partial(ring_kernel, count),
        out_shape=jax.ShapeDtypeStruct((rows, out_width), jnp.bfloat16),
        in_specs=[smem] * 3 + [hbm] * 4,
        out_specs=pl.BlockSpec(memory_space=pl.ANY),
        scratch_shapes=[
            pltpu.VMEM((rows, width), jnp.bfloat16),
            pltpu.VMEM(out_weight.shape, jnp.bfloat16),
            pltpu.VMEM((count, rows, width), jnp.bfloat16),
            pltpu.VMEM((count, rows, width), jnp.bfloat16),
            pltpu.VMEM((heads, rows, HEAD), jnp.float32),
            pltpu.VMEM((heads, rows, HEAD), jnp.float32),
            pltpu.VMEM((heads, rows, HEAD), jnp.float32),
            pltpu.VMEM((rows, width), jnp.bfloat16),
            pltpu.VMEM((rows, width), jnp.bfloat16),
            pltpu.VMEM((rows, out_width), jnp.float32),
            pltpu.VMEM((rows, out_width), jnp.bfloat16),
            pltpu.SemaphoreType.DMA((5,)),
            pltpu.SemaphoreType.DMA((4, count)),
            pltpu.SemaphoreType.DMA((4, count)),
            pltpu.SemaphoreType.DMA((2, heads)),
            pltpu.SemaphoreType.DMA((2, heads)),
            pltpu.SemaphoreType.DMA((heads // 2,)),
            pltpu.SemaphoreType.DMA((heads // 2,)),
        ],
        compiler_params=pltpu.CompilerParams(
            collective_id=1, has_side_effects=True, vmem_limit_bytes=60 << 20
        ),
    )(random_blocks.T, window_blocks, global_blocks, queries, keys, values, out_weight)


def solution(mesh):
    placed = (
        P(("groups", "ctx"), "head"),
        P(("groups", "ctx"), "head"),
        P(("groups", "ctx"), "head"),
        P(None, "head"),
        P("groups", None),
        P(("groups", "ctx")),
        P("groups"),
    )
    return jax.shard_map(
        per_device,
        mesh=mesh,
        in_specs=placed,
        out_specs=P(("groups", "ctx"), "head"),
        check_vma=False,
    )
```

```python
import functools
import math

import jax
import jax.numpy as jnp
from jax import lax
from jax.experimental import pallas as pl
from jax.experimental.pallas import tpu as pltpu
from jax.sharding import PartitionSpec as P

HEAD = 128
BLOCK = 128
WMAX = 1
GLOB = 2
RAND = 3

LARGE_NEG = -1e30
MESH = pl.DeviceIdType.MESH

K_FWD, V_FWD, K_BWD, V_BWD = range(4)


GRID_DEPTH = 4
GRID_WIDTH = 2
OWN, NEAR, CROSS, FAR = range(4)
PARTNER, BELOW, BELOW_PARTNER = 1, 2, 3
SCALE = math.log2(math.e) / math.sqrt(HEAD)


def grid_kernel(
    table_ref,
    q_hbm,
    k_hbm,
    v_hbm,
    w_hbm,
    out_ref,
    q_all,
    k_all,
    v_all,
    w_ref,
    win_all,
    bias_ref,
    peak_ref,
    total_ref,
    acc_ref,
    weight_ref,
    inverse_ref,
    gain_ref,
    up_part,
    up_stat,
    up_part_in,
    up_stat_in,
    side_part,
    side_stat,
    side_part_in,
    side_stat_in,
    own_ref,
    other_ref,
    sum_ref,
    load_sem,
    kv_send,
    kv_recv,
    q_send,
    q_recv,
    win_send,
    win_recv,
    up_send,
    up_recv,
    side_send,
    side_recv,
    pair_send,
    pair_recv,
    ready,
):
    rows, width = q_hbm.shape
    heads = width // HEAD
    half = heads // 2
    dev_blocks = rows // BLOCK
    position = lax.axis_index("ctx")
    side = lax.axis_index("head")
    depth, column = position // GRID_WIDTH, position % GRID_WIDTH
    inner = (depth > 0) & (depth < GRID_DEPTH - 1)

    def mate(level):
        return level + 1 - 2 * (level % 2)

    cross_depth = GRID_DEPTH - 1 - depth
    partner = depth * GRID_WIDTH + 1 - column
    near = mate(depth) * GRID_WIDTH + column
    near_partner = mate(depth) * GRID_WIDTH + 1 - column
    cross = cross_depth * GRID_WIDTH + column
    far = mate(cross_depth) * GRID_WIDTH + column

    def at(h):
        if isinstance(h, int):
            return pl.ds(h * HEAD, HEAD)
        return pl.ds(pl.multiple_of(h * HEAD, HEAD), HEAD)

    def send(src, dst, send_sem, recv_sem, target):
        return pltpu.make_async_remote_copy(
            src_ref=src,
            dst_ref=dst,
            send_sem=send_sem,
            recv_sem=recv_sem,
            device_id=target,
            device_id_type=MESH,
        )

    def key_value(kind, slot, h):
        source = {
            NEAR: (k_hbm, v_hbm)[kind],
            CROSS: (k_hbm, v_hbm)[kind],
            FAR: (k_all, v_all)[kind].at[NEAR],
        }[slot]
        return send(
            source.at[:, at(h)],
            (k_all, v_all)[kind].at[slot, :, at(h)],
            kv_send.at[slot, kind, h],
            kv_recv.at[slot, kind, h],
            {"ctx": near if slot == NEAR else cross},
        )

    def query(slot):
        source = q_all.at[BELOW] if slot == BELOW_PARTNER else q_hbm
        return send(
            source,
            q_all.at[slot],
            q_send.at[slot],
            q_recv.at[slot],
            {"ctx": near if slot == BELOW else partner},
        )

    def reach(slot):
        return send(
            win_all.at[BELOW if slot == BELOW_PARTNER else OWN],
            win_all.at[slot],
            win_send.at[slot],
            win_recv.at[slot],
            {"ctx": near if slot == BELOW else partner},
        )

    def upward(which, h):
        target = {"ctx": near_partner if which else near}
        return (
            send(up_stat.at[which, h, 0:1], up_stat_in.at[which, h, 0:1], up_send.at[1, which, h], up_recv.at[1, which, h], target),
            send(up_part.at[which, h], up_part_in.at[which, h], up_send.at[0, which, h], up_recv.at[0, which, h], target),
        )

    def sideways(h):
        target = {"ctx": partner}
        return (
            send(side_stat.at[h, 0:1], side_stat_in.at[h, 0:1], side_send.at[1, h], side_recv.at[1, h], target),
            send(side_part.at[h], side_part_in.at[h], side_send.at[0, h], side_recv.at[0, h], target),
        )

    load_q = pltpu.make_async_copy(q_hbm, q_all.at[OWN], load_sem.at[0])
    load_k = pltpu.make_async_copy(k_hbm, k_all.at[OWN], load_sem.at[1])
    load_v = pltpu.make_async_copy(v_hbm, v_all.at[OWN], load_sem.at[2])
    load_w = pltpu.make_async_copy(w_hbm, w_ref, load_sem.at[3])
    barrier = pltpu.get_barrier_semaphore()

    def greet(semaphore, target):
        pl.semaphore_signal(semaphore, inc=1, device_id=target, device_id_type=MESH)

    @pl.when(inner)
    def _():
        greet(barrier, {"ctx": cross})
        greet(barrier, {"ctx": near})
        greet(barrier, {"ctx": near_partner})

    greet(barrier, {"ctx": partner})
    greet(barrier, {"head": 1 - side})
    load_q.start()
    load_k.start()
    load_v.start()
    for a in range(dev_blocks):
        win_all[OWN, a] = jnp.full((8, HEAD), table_ref[RAND, a], jnp.int32)

    def use_bias(q, query_chip, pairs):
        for k, key_chip in pairs:
            for a in range(dev_blocks):
                query_block = query_chip * dev_blocks + a
                for b in range(dev_blocks):
                    key_block = key_chip * dev_blocks + b
                    offset = jnp.abs(key_block - query_block)
                    needed = jnp.where(offset <= WMAX, offset, 1 << 30)
                    used = table_ref[RAND + 1, 0] == key_block
                    for g in range(1, GLOB):
                        used = used | (table_ref[RAND + 1, g] == key_block)
                    for r in range(RAND):
                        used = used | (table_ref[r, query_block] == key_block)
                    bias = jnp.where(used, 0.0, LARGE_NEG)
                    bias = jnp.where(win_all[q, a] >= needed, 0.0, bias)
                    bias_ref[q, k, a, :, b * BLOCK : (b + 1) * BLOCK] = bias

    def steps(pairs, h, first=False):
        cols = at(h)
        every = [
            lax.dot_general(
                q_all[q, :, cols],
                k_all[k, :, cols],
                (((1,), (1,)), ((), ())),
                preferred_element_type=jnp.float32,
            )
            for q, k in pairs
        ]
        held = []
        for (q, k), scores in zip(pairs, every):
            for a in range(dev_blocks):
                span = slice(a * BLOCK, (a + 1) * BLOCK)
                block = scores[span] * SCALE + bias_ref[q, k, a, 0:1, :]
                best = jnp.max(block, axis=1, keepdims=True)
                old = None
                if first:
                    best = jnp.broadcast_to(best, (BLOCK, HEAD))
                else:
                    old = peak_ref[q, h, span]
                    best = jnp.maximum(old, best)
                weights = [
                    jnp.exp2(block[:, b * BLOCK : (b + 1) * BLOCK] - best) for b in range(dev_blocks)
                ]
                total = functools.reduce(jnp.add, weights)
                rounded = jnp.concatenate([w.astype(jnp.bfloat16) for w in weights], axis=1)
                held.append((old, best, total, rounded))
        for i, (q, k) in enumerate(pairs):
            mine = held[i * dev_blocks : (i + 1) * dev_blocks]
            part = jnp.dot(
                jnp.concatenate([m[3] for m in mine], axis=0),
                v_all[k, :, cols],
                preferred_element_type=jnp.float32,
            )
            for a, (old, best, total, _) in enumerate(mine):
                span = slice(a * BLOCK, (a + 1) * BLOCK)
                acc = part[span]
                if not first:
                    fade = jnp.exp2(old - best)
                    total = total + total_ref[q, h, span] * fade
                    acc = acc + acc_ref[q, h, span] * fade
                peak_ref[q, h, span] = best
                total_ref[q, h, span] = total
                acc_ref[q, h, span] = acc

    def step(q, k, h, first=False):
        steps([(q, k)], h, first)

    def score(pairs, h):
        cols = at(h)
        every = [
            lax.dot_general(
                q_all[q, :, cols],
                k_all[k, :, cols],
                (((1,), (1,)), ((), ())),
                preferred_element_type=jnp.float32,
            )
            for q, k in pairs
        ]
        for (q, k), scores in zip(pairs, every):
            for a in range(dev_blocks):
                span = slice(a * BLOCK, (a + 1) * BLOCK)
                block = scores[span] * SCALE + bias_ref[q, k, a, 0:1, :]
                old = peak_ref[q, h, span]
                best = jnp.maximum(old, jnp.max(block, axis=1, keepdims=True))
                weights = [
                    jnp.exp2(block[:, b * BLOCK : (b + 1) * BLOCK] - best) for b in range(dev_blocks)
                ]
                fade = jnp.exp2(old - best)
                weight_ref[q, span] = jnp.concatenate([w.astype(jnp.bfloat16) for w in weights], axis=1)
                peak_ref[q, h, span] = best
                total_ref[q, h, span] = functools.reduce(jnp.add, weights, total_ref[q, h, span] * fade)
                acc_ref[q, h, span] = acc_ref[q, h, span] * fade

    def value(q, k, h):
        return acc_ref[q, h] + jnp.dot(weight_ref[q], v_all[k, :, at(h)], preferred_element_type=jnp.float32)

    def level(q, h, stat):
        total = jnp.sum(total_ref[q, h], axis=1, keepdims=True)
        inverse_ref[q] = jnp.broadcast_to(1.0 / total, (rows, HEAD))
        stat[...] = (peak_ref[q, h] + jnp.log2(total)).T[:8]

    def pack(q, h, part, stat):
        level(q, h, stat)
        part[...] = (acc_ref[q, h] * inverse_ref[q]).astype(jnp.bfloat16)

    def merge(q, h, incoming):
        old = peak_ref[q, h]
        levels = [jnp.broadcast_to(stat[0:1, :], (HEAD, rows)).T for _, stat in incoming]
        best = functools.reduce(jnp.maximum, levels, old)
        fade = jnp.exp2(old - best)
        total = total_ref[q, h] * fade
        acc = acc_ref[q, h] * fade
        for level, (part, _) in zip(levels, incoming):
            gain = jnp.exp2(level - best)
            total = total + gain * (1.0 / HEAD)
            acc = acc + part[...].astype(jnp.float32) * gain
        return best, total, acc

    def keep(q, h, state):
        peak_ref[q, h], total_ref[q, h], acc_ref[q, h] = state

    group = 2 * HEAD
    groups = width // group
    tiles = 2
    tile = out_ref.shape[1] // tiles

    def group_cols(g):
        if isinstance(g, int):
            return pl.ds(g * group, group)
        return pl.ds(pl.multiple_of(g * group, group), group)

    def exchange(g):
        return send(
            own_ref.at[:, group_cols(g)],
            other_ref.at[:, group_cols(g)],
            pair_send.at[g],
            pair_recv.at[g],
            {"head": 1 - side},
        )

    def project(source, which, g):
        w_rows = pl.ds(pl.multiple_of(which * width + g * group, group), group)
        return jnp.dot(source[:, group_cols(g)], w_ref[w_rows, :], preferred_element_type=jnp.float32)

    def finish(h, *incoming):
        for (stat_copy, _), _, _ in incoming:
            stat_copy.wait_recv()
        old = peak_ref[OWN, h]
        levels = [jnp.broadcast_to(stat[0:1, :], (HEAD, rows)).T for _, _, stat in incoming]
        best = functools.reduce(jnp.maximum, levels, old)
        fade = jnp.exp2(old - best)
        gains = [jnp.exp2(level - best) for level in levels]
        total = jnp.sum(total_ref[OWN, h] * fade, axis=1, keepdims=True)
        inverse = 1.0 / functools.reduce(jnp.add, gains, total)
        acc = acc_ref[OWN, h] * (fade * inverse)
        for i, gain in enumerate(gains):
            gain_ref[i] = gain * inverse
        acc_ref[OWN, h] = acc
        for (_, part_copy), _, _ in incoming:
            part_copy.wait_recv()
        acc = acc_ref[OWN, h]
        for i, (_, part, _) in enumerate(incoming):
            acc = acc + part[...].astype(jnp.float32) * gain_ref[i]
        own_ref[:, at(h)] = acc.astype(jnp.bfloat16)

        @pl.when(h % 2 == 1)
        def _():
            g = h // 2
            exchange(g).start()

            @pl.when(g == 0)
            def _():
                sum_ref[...] = project(own_ref, side, g)

            @pl.when(g > 0)
            def _():
                exchange(g - 1).wait_recv()
                sum_ref[...] += project(own_ref, side, g) + project(other_ref, 1 - side, g - 1)

    def loop(lower, upper, body):
        def run(h, carry):
            body(h)
            return carry

        lax.fori_loop(lower, upper, run, 0)

    def wait_key_value(slot, h):
        key_value(0, slot, h).wait_recv()
        key_value(1, slot, h).wait_recv()

    @pl.when(inner)
    def _():
        pl.semaphore_wait(barrier, 3)

        def start_own(slot, h):
            for kind in (0, 1):
                key_value(kind, slot, h).start()

        start_own(CROSS, 0)
        query(PARTNER).start()
        reach(PARTNER).start()
        loop(1, heads, lambda h: start_own(CROSS, h))
        pl.semaphore_wait(ready, 2)
        loop(0, heads, lambda h: start_own(NEAR, h))
        load_w.start()
        pairs = ((OWN, position), (NEAR, near), (CROSS, cross), (FAR, far))
        use_bias(OWN, position, pairs)
        load_q.wait()
        load_k.wait()
        load_v.wait()
        loop(0, heads, lambda h: step(OWN, OWN, h, first=True))

        query(BELOW).wait_recv()
        reach(BELOW).wait_recv()
        query(BELOW_PARTNER).start()
        reach(BELOW_PARTNER).start()
        query(PARTNER).wait_recv()
        reach(PARTNER).wait_recv()
        use_bias(PARTNER, partner, pairs)
        use_bias(BELOW, near, pairs[2:])
        loop(0, heads, lambda h: step(PARTNER, OWN, h, first=True))

        def pass_on(h):
            wait_key_value(NEAR, h)
            for kind in (0, 1):
                key_value(kind, FAR, h).start()

        def early(h):
            @pl.when(h >= half)
            def _():
                pass_on(h - half)
                steps([(PARTNER, NEAR), (OWN, NEAR)], h - half)

            wait_key_value(CROSS, h)
            steps([(OWN, CROSS), (PARTNER, CROSS)], h)
            step(BELOW, CROSS, h, first=True)

        loop(0, heads, early)
        query(BELOW_PARTNER).wait_recv()
        reach(BELOW_PARTNER).wait_recv()
        use_bias(BELOW_PARTNER, near_partner, pairs[2:])

        def close(h):
            finish(h, (sideways(h), side_part_in.at[h], side_stat_in.at[h]))

        def late(h):
            @pl.when(h < half)
            def _():
                pass_on(h + half)

            key_value(0, FAR, h).wait_recv()
            score([(BELOW_PARTNER, FAR), (PARTNER, FAR)], h)
            score([(BELOW, FAR), (OWN, FAR)], h)
            shipped = (
                (BELOW_PARTNER, up_part.at[1, h], up_stat.at[1, h], upward(1, h)),
                (PARTNER, side_part.at[h], side_stat.at[h], sideways(h)),
                (BELOW, up_part.at[0, h], up_stat.at[0, h], upward(0, h)),
            )
            for q, _, stat, _ in shipped:
                level(q, h, stat)
            for _, _, _, (stat_copy, _) in shipped:
                stat_copy.start()
            key_value(1, FAR, h).wait_recv()
            for q, part, _, (_, part_copy) in shipped:
                part[...] = (value(q, FAR, h) * inverse_ref[q]).astype(jnp.bfloat16)
                part_copy.start()
            acc_ref[OWN, h] = value(OWN, FAR, h)

            @pl.when(h < half)
            def _():
                steps([(PARTNER, NEAR), (OWN, NEAR)], h + half)

            @pl.when(h < heads - 1)
            def _():
                step(BELOW_PARTNER, CROSS, h + 1, first=True)

        step(BELOW_PARTNER, CROSS, 0, first=True)

        def drain(h):
            for slot in (NEAR, CROSS, FAR):
                for kind in (0, 1):
                    key_value(kind, slot, h).wait_send()

        def late_or_drain(h):
            @pl.when(h < heads)
            def _():
                late(h)

            @pl.when(h == 0)
            def _():
                load_w.wait()

            @pl.when(h == heads)
            def _():
                loop(0, heads, drain)
                for slot in (PARTNER, BELOW_PARTNER):
                    query(slot).wait_send()
                    reach(slot).wait_send()

            @pl.when(h > 0)
            def _():
                close(h - 1)

        loop(0, heads + 1, late_or_drain)

    @pl.when(jnp.logical_not(inner))
    def _():
        pl.semaphore_wait(barrier, 4)
        greet(ready, {"ctx": near})
        greet(ready, {"ctx": near_partner})
        query(BELOW).start()
        reach(BELOW).start()
        query(PARTNER).start()
        reach(PARTNER).start()

        def start_own(h):
            for kind in (0, 1):
                key_value(kind, NEAR, h).start()

        loop(0, heads, start_own)
        load_w.start()
        pairs = ((OWN, position), (NEAR, near))
        use_bias(OWN, position, pairs)
        load_q.wait()
        load_k.wait()
        load_v.wait()
        loop(0, heads, lambda h: step(OWN, OWN, h, first=True))
        query(PARTNER).wait_recv()
        reach(PARTNER).wait_recv()
        use_bias(PARTNER, partner, pairs)
        loop(0, heads, lambda h: step(PARTNER, OWN, h, first=True))

        def early(h):
            wait_key_value(NEAR, h)
            step(PARTNER, NEAR, h)
            pack(PARTNER, h, side_part.at[h], side_stat.at[h])
            for copy in sideways(h):
                copy.start()
            step(OWN, NEAR, h)

        loop(0, heads, early)
        load_w.wait()

        def side_merge(h):
            for copy in sideways(h):
                copy.wait_recv()
            keep(OWN, h, merge(OWN, h, [(side_part_in.at[h], side_stat_in.at[h])]))

        loop(0, heads, side_merge)

        def drain(h):
            for kind in (0, 1):
                key_value(kind, NEAR, h).wait_send()

        loop(0, heads, drain)
        for slot in (PARTNER, BELOW):
            query(slot).wait_send()
            reach(slot).wait_send()

        def late(h):
            incoming = [(upward(which, h), up_part_in.at[which, h], up_stat_in.at[which, h]) for which in (1, 0)]

            finish(h, *incoming)

        loop(0, heads, late)

    exchange(groups - 1).wait_recv()
    out_ref[...] = (sum_ref[...] + project(other_ref, 1 - side, groups - 1)).astype(out_ref.dtype)

    def drain_side(h):
        for copy in sideways(h):
            copy.wait_send()

    loop(0, heads, drain_side)
    loop(0, groups, lambda g: exchange(g).wait_send())

    @pl.when(inner)
    def _():
        def drain_up(h):
            for which in (0, 1):
                for copy in upward(which, h):
                    copy.wait_send()

        loop(0, heads, drain_up)


def grid_call(queries, keys, values, out_weight, random_blocks, window_blocks, global_blocks):
    rows, width = queries.shape
    heads = width // HEAD
    dev_blocks = rows // BLOCK
    out_width = out_weight.shape[1]
    smem = pl.BlockSpec(memory_space=pltpu.SMEM)
    hbm = pl.BlockSpec(memory_space=pltpu.HBM)
    state = pltpu.VMEM((4, heads, rows, HEAD), jnp.float32)
    dma = pltpu.SemaphoreType.DMA
    blocks = random_blocks.shape[0]
    table = (
        jnp.pad(random_blocks.T, ((0, 2), (0, 0)))
        + jnp.pad(window_blocks[None], ((RAND, 1), (0, blocks - dev_blocks)))
        + jnp.pad(global_blocks[None], ((RAND + 1, 0), (0, blocks - GLOB)))
    )
    return pl.pallas_call(
        grid_kernel,
        out_shape=jax.ShapeDtypeStruct((rows, out_width), jnp.bfloat16),
        in_specs=[smem] + [hbm] * 4,
        out_specs=pl.BlockSpec(memory_space=pltpu.VMEM),
        scratch_shapes=[
            pltpu.VMEM((4, rows, width), jnp.bfloat16),
            pltpu.VMEM((4, rows, width), jnp.bfloat16),
            pltpu.VMEM((4, rows, width), jnp.bfloat16),
            pltpu.VMEM(out_weight.shape, jnp.bfloat16),
            pltpu.VMEM((4, dev_blocks, 8, HEAD), jnp.int32),
            pltpu.VMEM((4, 4, dev_blocks, 8, rows), jnp.float32),
            state,
            state,
            state,
            pltpu.VMEM((4, rows, rows), jnp.bfloat16),
            pltpu.VMEM((4, rows, HEAD), jnp.float32),
            pltpu.VMEM((2, rows, HEAD), jnp.float32),
            pltpu.VMEM((2, heads, rows, HEAD), jnp.bfloat16),
            pltpu.VMEM((2, heads, 8, rows), jnp.float32),
            pltpu.VMEM((2, heads, rows, HEAD), jnp.bfloat16),
            pltpu.VMEM((2, heads, 8, rows), jnp.float32),
            pltpu.VMEM((heads, rows, HEAD), jnp.bfloat16),
            pltpu.VMEM((heads, 8, rows), jnp.float32),
            pltpu.VMEM((heads, rows, HEAD), jnp.bfloat16),
            pltpu.VMEM((heads, 8, rows), jnp.float32),
            pltpu.VMEM((rows, width), jnp.bfloat16),
            pltpu.VMEM((rows, width), jnp.bfloat16),
            pltpu.VMEM((rows, out_width), jnp.float32),
            dma((4,)),
            dma((4, 2, heads)),
            dma((4, 2, heads)),
            dma((4,)),
            dma((4,)),
            dma((4,)),
            dma((4,)),
            dma((2, 2, heads)),
            dma((2, 2, heads)),
            dma((2, heads)),
            dma((2, heads)),
            dma((heads // 2,)),
            dma((heads // 2,)),
            pltpu.SemaphoreType.REGULAR,
        ],
        compiler_params=pltpu.CompilerParams(
            collective_id=0, has_side_effects=True, vmem_limit_bytes=53 << 20
        ),
    )(table, queries, keys, values, out_weight)


def per_device(*arguments):
    if lax.axis_size("ctx") == GRID_DEPTH * GRID_WIDTH:
        return grid_call(*arguments)
    return ring_call(*arguments)


def ring_place(index, count):
    odd = index % 2
    return (1 - odd) * (index // 2) + odd * (count - 1 - index // 2)


def ring_index(place, count):
    late = place // (count // 2)
    return (1 - late) * (2 * place) + late * (2 * (count - 1 - place) + 1)


def ring_kernel(
    count,
    random_ref,
    window_ref,
    global_ref,
    q_hbm,
    k_hbm,
    v_hbm,
    w_hbm,
    out_any,
    q_ref,
    w_ref,
    k_all,
    v_all,
    peak_ref,
    total_ref,
    acc_ref,
    own_ref,
    other_ref,
    sum_ref,
    out_ref,
    load_sem,
    send_sem,
    recv_sem,
    last_send,
    last_recv,
    pair_send,
    pair_recv,
):
    rows, width = q_ref.shape
    heads = width // HEAD
    dev_blocks = rows // BLOCK
    half = count // 2
    position = lax.axis_index("ctx")
    side = lax.axis_index("head")
    place = ring_place(position, count)
    right = ring_index((place + 1) % count, count)
    left = ring_index((place + count - 1) % count, count)

    load_k = pltpu.make_async_copy(k_hbm, k_all.at[0], load_sem.at[0])
    load_v = pltpu.make_async_copy(v_hbm, v_all.at[0], load_sem.at[1])
    load_q = pltpu.make_async_copy(q_hbm, q_ref, load_sem.at[2])
    load_w = pltpu.make_async_copy(w_hbm, w_ref, load_sem.at[3])
    load_k.start()
    load_v.start()
    load_q.start()

    barrier = pltpu.get_barrier_semaphore()
    pl.semaphore_signal(barrier, inc=1, device_id={"ctx": left}, device_id_type=MESH)
    pl.semaphore_signal(barrier, inc=1, device_id={"ctx": right}, device_id_type=MESH)
    pl.semaphore_signal(barrier, inc=1, device_id={"head": 1 - side}, device_id_type=MESH)
    pl.semaphore_wait(barrier, 3)

    def hop(stream, slot):
        buffer = k_all if stream in (K_FWD, K_BWD) else v_all
        forward = stream in (K_FWD, V_FWD)
        source = slot - 1 if forward else (slot + 1) % count
        return pltpu.make_async_remote_copy(
            src_ref=buffer.at[source],
            dst_ref=buffer.at[slot],
            send_sem=send_sem.at[stream, slot],
            recv_sem=recv_sem.at[stream, slot],
            device_id={"ctx": right if forward else left},
            device_id_type=MESH,
        )

    load_k.wait()
    hop(K_FWD, 1).start()
    hop(K_BWD, count - 1).start()
    load_v.wait()
    hop(V_FWD, 1).start()
    hop(V_BWD, count - 1).start()
    load_q.wait()
    load_w.start()

    peak_ref[...] = jnp.full_like(peak_ref, LARGE_NEG)
    total_ref[...] = jnp.zeros_like(total_ref)
    acc_ref[...] = jnp.zeros_like(acc_ref)
    scale = math.log2(math.e) / math.sqrt(HEAD)

    def use_bias(slot):
        owner = ring_index((place + count - slot) % count, count)
        row_block = lax.broadcasted_iota(jnp.int32, (rows, HEAD), 0) // BLOCK
        biases = []
        for b in range(dev_blocks):
            key_block = owner * dev_blocks + b
            bias = jnp.full((rows, HEAD), LARGE_NEG, jnp.float32)
            for a in range(dev_blocks):
                query_block = position * dev_blocks + a
                offset = jnp.abs(key_block - query_block)
                used = (offset <= window_ref[a]) & (offset <= WMAX)
                for g in range(GLOB):
                    used = used | (global_ref[g] == key_block)
                for r in range(RAND):
                    used = used | (random_ref[r, query_block] == key_block)
                bias = jnp.where(row_block == a, jnp.where(used, 0.0, LARGE_NEG), bias)
            biases.append(bias)
        return biases

    def attend_head(slot, h, biases):
        cols = pl.ds(h * HEAD, HEAD)
        if not isinstance(h, int):
            cols = pl.ds(pl.multiple_of(h * HEAD, HEAD), HEAD)
        scores = lax.dot_general(
            q_ref[:, cols],
            k_all[slot, :, cols],
            (((1,), (1,)), ((), ())),
            preferred_element_type=jnp.float32,
        )
        scores = scores * scale
        old_peak = peak_ref[h]
        best_peak = old_peak
        parts = []
        for b, bias in enumerate(biases):
            block = scores[:, b * BLOCK : (b + 1) * BLOCK]
            row_peak = jnp.max(block, axis=1, keepdims=True)
            weights = jnp.exp2(block - row_peak)
            part = jnp.dot(
                weights.astype(jnp.bfloat16),
                v_all[slot, b * BLOCK : (b + 1) * BLOCK, cols],
                preferred_element_type=jnp.float32,
            )
            used_peak = row_peak + bias
            best_peak = jnp.maximum(best_peak, used_peak)
            parts.append((used_peak, weights, part))
        fade = jnp.exp2(old_peak - best_peak)
        total = total_ref[h] * fade
        acc = acc_ref[h] * fade
        for used_peak, weights, part in parts:
            factor = jnp.exp2(used_peak - best_peak)
            total = total + weights * factor
            acc = acc + part * factor
        return best_peak, total, acc

    def attend(slot):
        biases = use_bias(slot)

        def one_head(h, carry):
            peak_ref[h], total_ref[h], acc_ref[h] = attend_head(slot, h, biases)
            return carry

        lax.fori_loop(0, heads, one_head, 0, unroll=2)

    def last_hop(stream, h):
        buffer = k_all if stream == K_FWD else v_all
        forward = h % 2 == 0
        cols = pl.ds(h * HEAD, HEAD)
        return pltpu.make_async_remote_copy(
            src_ref=buffer.at[half - 1 if forward else half + 1, :, cols],
            dst_ref=buffer.at[half, :, cols],
            send_sem=last_send.at[stream, h],
            recv_sem=last_recv.at[stream, h],
            device_id={"ctx": right if forward else left},
            device_id_type=MESH,
        )

    attend(0)

    def middle(step, carry):
        back = count - step
        hop(K_FWD, step).wait_recv()
        hop(K_FWD, step + 1).start()
        hop(K_BWD, back).wait_recv()
        hop(K_BWD, back - 1).start()
        hop(V_FWD, step).wait_recv()
        hop(V_FWD, step + 1).start()
        hop(V_BWD, back).wait_recv()
        hop(V_BWD, back - 1).start()
        attend(step)
        attend(back)
        return carry

    lax.fori_loop(1, half - 1, middle, 0)

    for side_of, key_stream in ((0, K_FWD), (1, K_BWD)):
        hop(key_stream, half + 1 if side_of else half - 1).wait_recv()
        for pair in range(min(2, heads // 2)):
            last_hop(K_FWD, 2 * pair + side_of).start()
    for side_of, value_stream in ((0, V_FWD), (1, V_BWD)):
        hop(value_stream, half + 1 if side_of else half - 1).wait_recv()
        for pair in range(heads // 2):
            last_hop(V_FWD, 2 * pair + side_of).start()
            if pair + 2 < heads // 2:
                last_hop(K_FWD, 2 * (pair + 2) + side_of).start()
    attend(half - 1)
    attend(half + 1)
    load_w.wait()
    biases = use_bias(half)
    group = 2 * HEAD

    def exchange(g):
        cols = pl.ds(g * group, group)
        return pltpu.make_async_remote_copy(
            src_ref=own_ref.at[:, cols],
            dst_ref=other_ref.at[:, cols],
            send_sem=pair_send.at[g],
            recv_sem=pair_recv.at[g],
            device_id={"head": 1 - side},
            device_id_type=MESH,
        )

    def project(source, which, g):
        w_rows = pl.ds(pl.multiple_of(which * width + g * group, group), group)
        return jnp.dot(
            source[:, g * group : (g + 1) * group],
            w_ref[w_rows, :],
            preferred_element_type=jnp.float32,
        )

    groups = width // group
    for g in range(groups):
        for h in (2 * g, 2 * g + 1):
            last_hop(K_FWD, h).wait_recv()
            last_hop(V_FWD, h).wait_recv()
            _, total, acc = attend_head(half, h, biases)
            total = jnp.sum(total, axis=1, keepdims=True)
            own_ref[:, h * HEAD : (h + 1) * HEAD] = (acc / total).astype(jnp.bfloat16)
        exchange(g).start()
        if g == 0:
            sum_ref[...] = project(own_ref, side, g)
        else:
            exchange(g - 1).wait_recv()
            sum_ref[...] += project(other_ref, 1 - side, g - 1) + project(own_ref, side, g)
    exchange(groups - 1).wait_recv()
    out_ref[...] = (sum_ref[...] + project(other_ref, 1 - side, groups - 1)).astype(out_ref.dtype)

    store = pltpu.make_async_copy(out_ref, out_any, load_sem.at[4])
    store.start()
    for g in range(groups):
        exchange(g).wait_send()
    for h in range(heads):
        last_hop(K_FWD, h).wait_send()
        last_hop(V_FWD, h).wait_send()

    def drain(step, carry):
        hop(K_FWD, step).wait_send()
        hop(V_FWD, step).wait_send()
        hop(K_BWD, count - step).wait_send()
        hop(V_BWD, count - step).wait_send()
        return carry

    lax.fori_loop(1, half, drain, 0)
    store.wait()


def ring_call(queries, keys, values, out_weight, random_blocks, window_blocks, global_blocks):
    count = lax.axis_size("ctx")
    rows, width = queries.shape
    heads = width // HEAD
    out_width = out_weight.shape[1]
    smem = pl.BlockSpec(memory_space=pltpu.SMEM)
    hbm = pl.BlockSpec(memory_space=pltpu.HBM)
    return pl.pallas_call(
        functools.partial(ring_kernel, count),
        out_shape=jax.ShapeDtypeStruct((rows, out_width), jnp.bfloat16),
        in_specs=[smem] * 3 + [hbm] * 4,
        out_specs=pl.BlockSpec(memory_space=pl.ANY),
        scratch_shapes=[
            pltpu.VMEM((rows, width), jnp.bfloat16),
            pltpu.VMEM(out_weight.shape, jnp.bfloat16),
            pltpu.VMEM((count, rows, width), jnp.bfloat16),
            pltpu.VMEM((count, rows, width), jnp.bfloat16),
            pltpu.VMEM((heads, rows, HEAD), jnp.float32),
            pltpu.VMEM((heads, rows, HEAD), jnp.float32),
            pltpu.VMEM((heads, rows, HEAD), jnp.float32),
            pltpu.VMEM((rows, width), jnp.bfloat16),
            pltpu.VMEM((rows, width), jnp.bfloat16),
            pltpu.VMEM((rows, out_width), jnp.float32),
            pltpu.VMEM((rows, out_width), jnp.bfloat16),
            pltpu.SemaphoreType.DMA((5,)),
            pltpu.SemaphoreType.DMA((4, count)),
            pltpu.SemaphoreType.DMA((4, count)),
            pltpu.SemaphoreType.DMA((2, heads)),
            pltpu.SemaphoreType.DMA((2, heads)),
            pltpu.SemaphoreType.DMA((heads // 2,)),
            pltpu.SemaphoreType.DMA((heads // 2,)),
        ],
        compiler_params=pltpu.CompilerParams(
            collective_id=1, has_side_effects=True, vmem_limit_bytes=60 << 20
        ),
    )(random_blocks.T, window_blocks, global_blocks, queries, keys, values, out_weight)


def solution(mesh):
    placed = (
        P(("groups", "ctx"), "head"),
        P(("groups", "ctx"), "head"),
        P(("groups", "ctx"), "head"),
        P(None, "head"),
        P("groups", None),
        P(("groups", "ctx")),
        P("groups"),
    )
    return jax.shard_map(
        per_device,
        mesh=mesh,
        in_specs=placed,
        out_specs=P(("groups", "ctx"), "head"),
        check_vma=False,
    )
```

```python
import functools
import math

import jax
import jax.numpy as jnp
from jax import lax
from jax.experimental import pallas as pl
from jax.experimental.pallas import tpu as pltpu
from jax.sharding import PartitionSpec as P

HEAD = 128
BLOCK = 128
WMAX = 1
GLOB = 2
RAND = 3

LARGE_NEG = -1e30
MESH = pl.DeviceIdType.MESH

K_FWD, V_FWD, K_BWD, V_BWD = range(4)


GRID_DEPTH = 4
GRID_WIDTH = 2
OWN, PARTNER, NEAR, NEAR_P, CROSS, CROSS_P, FAR, FAR_P = range(8)
BELOW, BELOW_P = 2, 3
SCALE = math.log2(math.e) / math.sqrt(HEAD)


def grid_kernel(
    table_ref,
    q_hbm,
    k_hbm,
    v_hbm,
    w_hbm,
    out_ref,
    q_all,
    k_all,
    v_all,
    w_ref,
    win_all,
    bias_ref,
    peak_ref,
    total_ref,
    acc_ref,
    weight_ref,
    inverse_ref,
    up_part,
    up_stat,
    up_part_in,
    up_stat_in,
    side_part,
    side_stat,
    side_part_in,
    side_stat_in,
    own_ref,
    other_ref,
    sum_ref,
    load_sem,
    w_sem,
    kv_send,
    kv_recv,
    q_send,
    q_recv,
    win_send,
    win_recv,
    up_send,
    up_recv,
    side_send,
    side_recv,
    pair_send,
    pair_recv,
    ready,
):
    rows, width = q_hbm.shape
    heads = width // HEAD // 2
    span_width = heads * HEAD
    half = heads // 2
    dev_blocks = rows // BLOCK
    position = lax.axis_index("ctx")
    side = lax.axis_index("head")
    depth, column = position // GRID_WIDTH, position % GRID_WIDTH
    inner = (depth > 0) & (depth < GRID_DEPTH - 1)

    def mate(level):
        return level + 1 - 2 * (level % 2)

    def chip(level, col):
        return level * GRID_WIDTH + col

    cross_depth = GRID_DEPTH - 1 - depth
    partner = chip(depth, 1 - column)
    near = chip(mate(depth), column)
    near_partner = chip(mate(depth), 1 - column)
    cross = chip(cross_depth, column)
    cross_partner = chip(cross_depth, 1 - column)
    far = chip(mate(cross_depth), column)
    far_partner = chip(mate(cross_depth), 1 - column)

    def at(h):
        if isinstance(h, int):
            return pl.ds(h * HEAD, HEAD)
        return pl.ds(pl.multiple_of(h * HEAD, HEAD), HEAD)

    def held(col, h):
        return pl.ds(pl.multiple_of((col * heads + h) * HEAD, HEAD), HEAD)

    def share(col):
        return pl.ds(pl.multiple_of(col * span_width, span_width), span_width)

    def spot(col, h):
        return pl.ds(pl.multiple_of((2 * h + col) * HEAD, HEAD), HEAD)

    def send(src, dst, send_sem, recv_sem, target):
        return pltpu.make_async_remote_copy(
            src_ref=src,
            dst_ref=dst,
            send_sem=send_sem,
            recv_sem=recv_sem,
            device_id=target,
            device_id_type=MESH,
        )

    def key_value(kind, slot, h):
        whole, kept = (k_hbm, v_hbm)[kind], (k_all, v_all)[kind]
        if slot == PARTNER:
            source = whole.at[:, held(1 - column, h)]
        elif slot in (NEAR, CROSS):
            source = whole.at[:, held(column, h)]
        else:
            source = kept.at[{NEAR_P: PARTNER, CROSS_P: PARTNER, FAR: NEAR, FAR_P: NEAR_P}[slot], :, at(h)]
        target = {PARTNER: partner, NEAR: near, NEAR_P: near}.get(slot, cross)
        return send(
            source,
            kept.at[slot, :, at(h)],
            kv_send.at[slot, kind, h],
            kv_recv.at[slot, kind, h],
            {"ctx": target},
        )

    def start_key_value(slot, h):
        for kind in (0, 1):
            key_value(kind, slot, h).start()

    def wait_key_value(slot, h):
        for kind in (0, 1):
            key_value(kind, slot, h).wait_recv()

    def query(slot):
        source = {
            PARTNER: q_hbm.at[:, share(1 - column)],
            BELOW: q_hbm.at[:, share(column)],
            BELOW_P: q_all.at[PARTNER],
        }[slot]
        target = {"ctx": partner if slot == PARTNER else near}
        return (
            send(source, q_all.at[slot], q_send.at[slot], q_recv.at[slot], target),
            send(
                win_all.at[PARTNER if slot == BELOW_P else OWN],
                win_all.at[slot],
                win_send.at[slot],
                win_recv.at[slot],
                target,
            ),
        )

    def start_query(slot):
        for copy in query(slot):
            copy.start()

    def wait_query(slot):
        for copy in query(slot):
            copy.wait_recv()

    def upward(which, h):
        target = {"ctx": near_partner if which else near}
        return (
            send(up_stat.at[which, h, 0:1], up_stat_in.at[which, h, 0:1], up_send.at[1, which, h], up_recv.at[1, which, h], target),
            send(up_part.at[which, h], up_part_in.at[which, h], up_send.at[0, which, h], up_recv.at[0, which, h], target),
        )

    def sideways(h):
        target = {"ctx": partner}
        return (
            send(side_stat.at[h, 0:1], side_stat_in.at[h, 0:1], side_send.at[1, h], side_recv.at[1, h], target),
            send(side_part.at[h], side_part_in.at[h], side_send.at[0, h], side_recv.at[0, h], target),
        )

    def swap(h):
        return send(
            side_part.at[h],
            own_ref.at[:, spot(column, h)],
            side_send.at[0, h],
            side_recv.at[0, h],
            {"ctx": partner},
        )

    loads = [
        pltpu.make_async_copy(whole.at[:, share(column)], kept.at[OWN], load_sem.at[i])
        for i, (whole, kept) in enumerate(((q_hbm, q_all), (k_hbm, k_all), (v_hbm, v_all)))
    ]

    def load_w(core, h, col):
        source = pl.multiple_of(core * width + (col * heads + h) * HEAD, HEAD)
        target = pl.multiple_of(core * width + (2 * h + col) * HEAD, HEAD)
        return pltpu.make_async_copy(
            w_hbm.at[pl.ds(source, HEAD)], w_ref.at[pl.ds(target, HEAD)], w_sem.at[core, h, col]
        )

    barrier = pltpu.get_barrier_semaphore()

    def greet(semaphore, target):
        pl.semaphore_signal(semaphore, inc=1, device_id=target, device_id_type=MESH)

    @pl.when(inner)
    def _():
        greet(barrier, {"ctx": cross})
        greet(barrier, {"ctx": near})
        greet(barrier, {"ctx": near_partner})

    greet(barrier, {"ctx": partner})
    greet(barrier, {"head": 1 - side})
    for load in loads:
        load.start()
    for a in range(dev_blocks):
        win_all[OWN, a] = jnp.full((8, HEAD), table_ref[RAND, a], jnp.int32)

    def use_bias(q, query_chip, pairs):
        for k, key_chip in pairs:
            for a in range(dev_blocks):
                query_block = query_chip * dev_blocks + a
                for b in range(dev_blocks):
                    key_block = key_chip * dev_blocks + b
                    offset = jnp.abs(key_block - query_block)
                    needed = jnp.where(offset <= WMAX, offset, 1 << 30)
                    used = table_ref[RAND + 1, 0] == key_block
                    for g in range(1, GLOB):
                        used = used | (table_ref[RAND + 1, g] == key_block)
                    for r in range(RAND):
                        used = used | (table_ref[r, query_block] == key_block)
                    bias = jnp.where(used, 0.0, LARGE_NEG)
                    bias = jnp.where(win_all[q, a] >= needed, 0.0, bias)
                    bias_ref[q, k, a, :, b * BLOCK : (b + 1) * BLOCK] = bias

    def steps(pairs, h, first=False):
        cols = at(h)
        every = [
            lax.dot_general(
                q_all[q, :, cols],
                k_all[k, :, cols],
                (((1,), (1,)), ((), ())),
                preferred_element_type=jnp.float32,
            )
            for q, k in pairs
        ]
        held = []
        for (q, k), scores in zip(pairs, every):
            for a in range(dev_blocks):
                span = slice(a * BLOCK, (a + 1) * BLOCK)
                block = scores[span] * SCALE + bias_ref[q, k, a, 0:1, :]
                best = jnp.max(block, axis=1, keepdims=True)
                old = None
                if first:
                    best = jnp.broadcast_to(best, (BLOCK, HEAD))
                else:
                    old = peak_ref[q, h, span]
                    best = jnp.maximum(old, best)
                weights = [
                    jnp.exp2(block[:, b * BLOCK : (b + 1) * BLOCK] - best) for b in range(dev_blocks)
                ]
                total = functools.reduce(jnp.add, weights)
                rounded = jnp.concatenate([w.astype(jnp.bfloat16) for w in weights], axis=1)
                held.append((old, best, total, rounded))
        for i, (q, k) in enumerate(pairs):
            mine = held[i * dev_blocks : (i + 1) * dev_blocks]
            part = jnp.dot(
                jnp.concatenate([m[3] for m in mine], axis=0),
                v_all[k, :, cols],
                preferred_element_type=jnp.float32,
            )
            for a, (old, best, total, _) in enumerate(mine):
                span = slice(a * BLOCK, (a + 1) * BLOCK)
                acc = part[span]
                if not first:
                    fade = jnp.exp2(old - best)
                    total = total + total_ref[q, h, span] * fade
                    acc = acc + acc_ref[q, h, span] * fade
                peak_ref[q, h, span] = best
                total_ref[q, h, span] = total
                acc_ref[q, h, span] = acc

    def step(q, k, h, first=False):
        steps([(q, k)], h, first)

    def score(pairs, h):
        cols = at(h)
        every = [
            lax.dot_general(
                q_all[q, :, cols],
                k_all[k, :, cols],
                (((1,), (1,)), ((), ())),
                preferred_element_type=jnp.float32,
            )
            for q, k in pairs
        ]
        for (q, k), scores in zip(pairs, every):
            for a in range(dev_blocks):
                span = slice(a * BLOCK, (a + 1) * BLOCK)
                block = scores[span] * SCALE + bias_ref[q, k, a, 0:1, :]
                old = peak_ref[q, h, span]
                best = jnp.maximum(old, jnp.max(block, axis=1, keepdims=True))
                weights = [
                    jnp.exp2(block[:, b * BLOCK : (b + 1) * BLOCK] - best) for b in range(dev_blocks)
                ]
                fade = jnp.exp2(old - best)
                weight_ref[q, span] = jnp.concatenate([w.astype(jnp.bfloat16) for w in weights], axis=1)
                peak_ref[q, h, span] = best
                total_ref[q, h, span] = functools.reduce(jnp.add, weights, total_ref[q, h, span] * fade)
                acc_ref[q, h, span] = acc_ref[q, h, span] * fade

    def value(q, k, h):
        return acc_ref[q, h] + jnp.dot(weight_ref[q], v_all[k, :, at(h)], preferred_element_type=jnp.float32)

    def level(q, h, stat):
        total = jnp.sum(total_ref[q, h], axis=1, keepdims=True)
        inverse_ref[q] = jnp.broadcast_to(1.0 / total, (rows, HEAD))
        stat[...] = (peak_ref[q, h] + jnp.log2(total)).T[:8]

    def pack(q, h, part, stat):
        level(q, h, stat)
        part[...] = (acc_ref[q, h] * inverse_ref[q]).astype(jnp.bfloat16)

    group = 2 * HEAD

    def group_cols(g):
        if isinstance(g, int):
            return pl.ds(g * group, group)
        return pl.ds(pl.multiple_of(g * group, group), group)

    def exchange(g):
        return send(
            own_ref.at[:, group_cols(g)],
            other_ref.at[:, group_cols(g)],
            pair_send.at[g],
            pair_recv.at[g],
            {"head": 1 - side},
        )

    def project(source, which, g):
        w_rows = pl.ds(pl.multiple_of(which * width + g * group, group), group)
        return jnp.dot(source[:, group_cols(g)], w_ref[w_rows, :], preferred_element_type=jnp.float32)

    def finish(h):
        exchange(h).start()

        @pl.when(h == 0)
        def _():
            sum_ref[...] = project(own_ref, side, h)

        @pl.when(h > 0)
        def _():
            exchange(h - 1).wait_recv()
            sum_ref[...] += project(own_ref, side, h) + project(other_ref, 1 - side, h - 1)

    def loop(lower, upper, body):
        def run(h, carry):
            body(h)
            return carry

        lax.fori_loop(lower, upper, run, 0)

    def each_w(action):
        def one(h):
            for core in (0, 1):
                for col in (0, 1):
                    getattr(load_w(core, h, col), action)()

        loop(0, heads, one)

    @pl.when(inner)
    def _():
        pl.semaphore_wait(barrier, 3)
        start_key_value(CROSS, 0)
        for h in range(half):
            start_key_value(PARTNER, h)
        start_query(PARTNER)
        loop(1, heads, lambda h: start_key_value(CROSS, h))
        loop(half, heads, lambda h: start_key_value(PARTNER, h))
        pl.semaphore_wait(ready, 2)
        loop(0, heads, lambda h: start_key_value(NEAR, h))
        each_w("start")
        close_by = ((OWN, position), (PARTNER, partner), (NEAR, near), (NEAR_P, near_partner))
        beyond = ((CROSS, cross), (CROSS_P, cross_partner), (FAR, far), (FAR_P, far_partner))
        use_bias(OWN, position, close_by + beyond)
        for load in loads:
            load.wait()
        loop(0, heads, lambda h: step(OWN, OWN, h, first=True))

        def first_round(h):
            wait_key_value(PARTNER, h)
            start_key_value(CROSS_P, h)
            start_key_value(NEAR_P, h)
            step(OWN, PARTNER, h)

        loop(0, heads, first_round)
        wait_query(PARTNER)
        use_bias(PARTNER, partner, close_by + beyond)
        loop(0, heads, lambda h: step(PARTNER, OWN, h, first=True))
        loop(0, heads, lambda h: step(PARTNER, PARTNER, h))
        wait_query(BELOW)
        use_bias(BELOW, near, beyond)

        def pass_on(h):
            wait_key_value(NEAR, h)
            start_key_value(FAR, h)
            wait_key_value(NEAR_P, h)
            start_key_value(FAR_P, h)

        def meet_near(h):
            steps([(OWN, NEAR), (PARTNER, NEAR)], h)
            steps([(OWN, NEAR_P), (PARTNER, NEAR_P)], h)

        loop(0, half, pass_on)

        def second_round(h):
            wait_key_value(CROSS, h)
            steps([(OWN, CROSS), (PARTNER, CROSS)], h)
            step(BELOW, CROSS, h, first=True)

            @pl.when(h < half)
            def _():
                meet_near(h)

            wait_key_value(CROSS_P, h)
            steps([(OWN, CROSS_P), (PARTNER, CROSS_P)], h)
            step(BELOW, CROSS_P, h)

        loop(0, heads, second_round)
        wait_query(BELOW_P)
        use_bias(BELOW_P, near_partner, beyond)

        def third_round(h):
            step(BELOW_P, CROSS, h, first=True)
            step(BELOW_P, CROSS_P, h)

        loop(0, heads, third_round)
        each_w("wait")

        def close(h):
            swap(h).wait_recv()
            finish(h)

        def late(h):
            wait_key_value(FAR, h)
            steps([(BELOW_P, FAR), (BELOW, FAR)], h)
            steps([(PARTNER, FAR), (OWN, FAR)], h)

            @pl.when(h < half)
            def _():
                pass_on(h + half)

            key_value(0, FAR_P, h).wait_recv()
            score([(BELOW_P, FAR_P), (BELOW, FAR_P)], h)
            score([(PARTNER, FAR_P), (OWN, FAR_P)], h)
            for which, q in ((1, BELOW_P), (0, BELOW)):
                level(q, h, up_stat.at[which, h])
                upward(which, h)[0].start()
            for q in (PARTNER, OWN):
                total = jnp.sum(total_ref[q, h], axis=1, keepdims=True)
                inverse_ref[q] = jnp.broadcast_to(1.0 / total, (rows, HEAD))
            key_value(1, FAR_P, h).wait_recv()
            for which, q in ((1, BELOW_P), (0, BELOW)):
                up_part[which, h] = (value(q, FAR_P, h) * inverse_ref[q]).astype(jnp.bfloat16)
                upward(which, h)[1].start()
            side_part[h] = (value(PARTNER, FAR_P, h) * inverse_ref[PARTNER]).astype(jnp.bfloat16)
            swap(h).start()
            own_ref[:, spot(column, h)] = (value(OWN, FAR_P, h) * inverse_ref[OWN]).astype(jnp.bfloat16)

            @pl.when(h < half)
            def _():
                meet_near(h + half)

        def drain(h):
            for slot in (PARTNER, NEAR, NEAR_P, CROSS, CROSS_P, FAR, FAR_P):
                for kind in (0, 1):
                    key_value(kind, slot, h).wait_send()

        def late_or_drain(h):
            @pl.when(h < heads)
            def _():
                late(h)

            @pl.when(h == heads)
            def _():
                loop(0, heads, drain)
                for copy in query(PARTNER):
                    copy.wait_send()

            @pl.when(h > 0)
            def _():
                close(h - 1)

        loop(0, heads + 1, late_or_drain)

    @pl.when(jnp.logical_not(inner))
    def _():
        pl.semaphore_wait(barrier, 4)
        greet(ready, {"ctx": near})
        greet(ready, {"ctx": near_partner})
        start_query(BELOW)
        for h in range(half):
            start_key_value(PARTNER, h)
        start_query(PARTNER)
        for h in range(half):
            start_key_value(NEAR, h)
        loop(half, heads, lambda h: start_key_value(PARTNER, h))
        each_w("start")
        close_by = ((OWN, position), (PARTNER, partner), (NEAR, near), (NEAR_P, near_partner))
        use_bias(OWN, position, close_by)
        for load in loads:
            load.wait()

        def relay(h):
            @pl.when(h >= half)
            def _():
                start_key_value(NEAR, h)

            wait_key_value(PARTNER, h)
            start_key_value(NEAR_P, h)

        loop(0, half, relay)
        wait_query(PARTNER)
        start_query(BELOW_P)
        loop(half, heads, relay)
        use_bias(PARTNER, partner, close_by)

        def early(h):
            step(OWN, OWN, h, first=True)
            step(PARTNER, OWN, h, first=True)
            steps([(PARTNER, PARTNER), (OWN, PARTNER)], h)

        loop(0, heads, early)

        def middle(h):
            wait_key_value(NEAR, h)
            steps([(PARTNER, NEAR), (OWN, NEAR)], h)

        loop(0, heads, middle)

        def side_round(h):
            wait_key_value(NEAR_P, h)
            steps([(PARTNER, NEAR_P), (OWN, NEAR_P)], h)
            pack(PARTNER, h, side_part.at[h], side_stat.at[h])
            for copy in sideways(h):
                copy.start()

        loop(0, heads, side_round)
        each_w("wait")

        def drain(h):
            for slot in (PARTNER, NEAR, NEAR_P):
                for kind in (0, 1):
                    key_value(kind, slot, h).wait_send()
            for copy in sideways(h):
                copy.wait_send()

        loop(0, heads, drain)
        for slot in (PARTNER, BELOW, BELOW_P):
            for copy in query(slot):
                copy.wait_send()

        def column_of(stat):
            return jnp.broadcast_to(stat[0:1, :], (HEAD, rows)).T

        def late(h):
            for copy in sideways(h):
                copy.wait_recv()
            upward(1, h)[0].wait_recv()
            upward(0, h)[0].wait_recv()
            mine, theirs = column_of(side_stat_in[h]), column_of(up_stat_in[1, h])
            best = jnp.maximum(mine, theirs)
            mine, theirs = jnp.exp2(mine - best), jnp.exp2(theirs - best)
            inverse = 1.0 / (mine + theirs)
            inverse_ref[0] = theirs * inverse
            part = side_part_in[h].astype(jnp.float32) * (mine * inverse)
            old, theirs = peak_ref[OWN, h], column_of(up_stat_in[0, h])
            best = jnp.maximum(old, theirs)
            fade, theirs = jnp.exp2(old - best), jnp.exp2(theirs - best)
            inverse = 1.0 / (jnp.sum(total_ref[OWN, h] * fade, axis=1, keepdims=True) + theirs)
            inverse_ref[1] = theirs * inverse
            acc_ref[OWN, h] = acc_ref[OWN, h] * (fade * inverse)
            acc_ref[PARTNER, h] = part
            for which, q, col in ((1, PARTNER, 1 - column), (0, OWN, column)):
                upward(which, h)[1].wait_recv()
                total = acc_ref[q, h] + up_part_in[which, h].astype(jnp.float32) * inverse_ref[1 - which]
                own_ref[:, spot(col, h)] = total.astype(jnp.bfloat16)
            finish(h)

        loop(0, heads, late)

    exchange(heads - 1).wait_recv()
    out_ref[...] = (sum_ref[...] + project(other_ref, 1 - side, heads - 1)).astype(out_ref.dtype)
    loop(0, heads, lambda g: exchange(g).wait_send())

    @pl.when(inner)
    def _():
        def drain_late(h):
            swap(h).wait_send()
            for which in (0, 1):
                for copy in upward(which, h):
                    copy.wait_send()

        loop(0, heads, drain_late)


def grid_call(queries, keys, values, out_weight, random_blocks, window_blocks, global_blocks):
    rows, width = queries.shape
    heads = width // HEAD // 2
    dev_blocks = rows // BLOCK
    out_width = out_weight.shape[1]
    hbm = pl.BlockSpec(memory_space=pltpu.HBM)
    state = pltpu.VMEM((4, heads, rows, HEAD), jnp.float32)
    dma = pltpu.SemaphoreType.DMA
    blocks = random_blocks.shape[0]
    table = (
        jnp.pad(random_blocks.T, ((0, 2), (0, 0)))
        + jnp.pad(window_blocks[None], ((RAND, 1), (0, blocks - dev_blocks)))
        + jnp.pad(global_blocks[None], ((RAND + 1, 0), (0, blocks - GLOB)))
    )
    return pl.pallas_call(
        grid_kernel,
        out_shape=jax.ShapeDtypeStruct((rows, out_width), jnp.bfloat16),
        in_specs=[pl.BlockSpec(memory_space=pltpu.SMEM)] + [hbm] * 4,
        out_specs=pl.BlockSpec(memory_space=pltpu.VMEM),
        scratch_shapes=[
            pltpu.VMEM((4, rows, width // 2), jnp.bfloat16),
            pltpu.VMEM((8, rows, width // 2), jnp.bfloat16),
            pltpu.VMEM((8, rows, width // 2), jnp.bfloat16),
            pltpu.VMEM(out_weight.shape, jnp.bfloat16),
            pltpu.VMEM((4, dev_blocks, 8, HEAD), jnp.int32),
            pltpu.VMEM((4, 8, dev_blocks, 8, rows), jnp.float32),
            state,
            state,
            state,
            pltpu.VMEM((4, rows, rows), jnp.bfloat16),
            pltpu.VMEM((4, rows, HEAD), jnp.float32),
            pltpu.VMEM((2, heads, rows, HEAD), jnp.bfloat16),
            pltpu.VMEM((2, heads, 8, rows), jnp.float32),
            pltpu.VMEM((2, heads, rows, HEAD), jnp.bfloat16),
            pltpu.VMEM((2, heads, 8, rows), jnp.float32),
            pltpu.VMEM((heads, rows, HEAD), jnp.bfloat16),
            pltpu.VMEM((heads, 8, rows), jnp.float32),
            pltpu.VMEM((heads, rows, HEAD), jnp.bfloat16),
            pltpu.VMEM((heads, 8, rows), jnp.float32),
            pltpu.VMEM((rows, width), jnp.bfloat16),
            pltpu.VMEM((rows, width), jnp.bfloat16),
            pltpu.VMEM((rows, out_width), jnp.float32),
            dma((3,)),
            dma((2, heads, 2)),
            dma((8, 2, heads)),
            dma((8, 2, heads)),
            dma((4,)),
            dma((4,)),
            dma((4,)),
            dma((4,)),
            dma((2, 2, heads)),
            dma((2, 2, heads)),
            dma((2, heads)),
            dma((2, heads)),
            dma((heads,)),
            dma((heads,)),
            pltpu.SemaphoreType.REGULAR,
        ],
        compiler_params=pltpu.CompilerParams(
            collective_id=0, has_side_effects=True, vmem_limit_bytes=53 << 20
        ),
    )(table, queries, keys, values, out_weight)


def per_device(*arguments):
    if lax.axis_size("ctx") == GRID_DEPTH * GRID_WIDTH:
        return grid_call(*arguments)
    return ring_call(*arguments)


def ring_place(index, count):
    odd = index % 2
    return (1 - odd) * (index // 2) + odd * (count - 1 - index // 2)


def ring_index(place, count):
    late = place // (count // 2)
    return (1 - late) * (2 * place) + late * (2 * (count - 1 - place) + 1)


def ring_kernel(
    count,
    random_ref,
    window_ref,
    global_ref,
    q_hbm,
    k_hbm,
    v_hbm,
    w_hbm,
    out_any,
    q_ref,
    w_ref,
    k_all,
    v_all,
    peak_ref,
    total_ref,
    acc_ref,
    own_ref,
    other_ref,
    sum_ref,
    out_ref,
    load_sem,
    send_sem,
    recv_sem,
    last_send,
    last_recv,
    pair_send,
    pair_recv,
):
    rows, width = q_ref.shape
    heads = width // HEAD
    dev_blocks = rows // BLOCK
    half = count // 2
    position = lax.axis_index("ctx")
    side = lax.axis_index("head")
    place = ring_place(position, count)
    right = ring_index((place + 1) % count, count)
    left = ring_index((place + count - 1) % count, count)

    load_k = pltpu.make_async_copy(k_hbm, k_all.at[0], load_sem.at[0])
    load_v = pltpu.make_async_copy(v_hbm, v_all.at[0], load_sem.at[1])
    load_q = pltpu.make_async_copy(q_hbm, q_ref, load_sem.at[2])
    load_w = pltpu.make_async_copy(w_hbm, w_ref, load_sem.at[3])
    load_k.start()
    load_v.start()
    load_q.start()

    barrier = pltpu.get_barrier_semaphore()
    pl.semaphore_signal(barrier, inc=1, device_id={"ctx": left}, device_id_type=MESH)
    pl.semaphore_signal(barrier, inc=1, device_id={"ctx": right}, device_id_type=MESH)
    pl.semaphore_signal(barrier, inc=1, device_id={"head": 1 - side}, device_id_type=MESH)
    pl.semaphore_wait(barrier, 3)

    def hop(stream, slot):
        buffer = k_all if stream in (K_FWD, K_BWD) else v_all
        forward = stream in (K_FWD, V_FWD)
        source = slot - 1 if forward else (slot + 1) % count
        return pltpu.make_async_remote_copy(
            src_ref=buffer.at[source],
            dst_ref=buffer.at[slot],
            send_sem=send_sem.at[stream, slot],
            recv_sem=recv_sem.at[stream, slot],
            device_id={"ctx": right if forward else left},
            device_id_type=MESH,
        )

    load_k.wait()
    hop(K_FWD, 1).start()
    hop(K_BWD, count - 1).start()
    load_v.wait()
    hop(V_FWD, 1).start()
    hop(V_BWD, count - 1).start()
    load_q.wait()
    load_w.start()

    peak_ref[...] = jnp.full_like(peak_ref, LARGE_NEG)
    total_ref[...] = jnp.zeros_like(total_ref)
    acc_ref[...] = jnp.zeros_like(acc_ref)
    scale = math.log2(math.e) / math.sqrt(HEAD)

    def use_bias(slot):
        owner = ring_index((place + count - slot) % count, count)
        row_block = lax.broadcasted_iota(jnp.int32, (rows, HEAD), 0) // BLOCK
        biases = []
        for b in range(dev_blocks):
            key_block = owner * dev_blocks + b
            bias = jnp.full((rows, HEAD), LARGE_NEG, jnp.float32)
            for a in range(dev_blocks):
                query_block = position * dev_blocks + a
                offset = jnp.abs(key_block - query_block)
                used = (offset <= window_ref[a]) & (offset <= WMAX)
                for g in range(GLOB):
                    used = used | (global_ref[g] == key_block)
                for r in range(RAND):
                    used = used | (random_ref[r, query_block] == key_block)
                bias = jnp.where(row_block == a, jnp.where(used, 0.0, LARGE_NEG), bias)
            biases.append(bias)
        return biases

    def attend_head(slot, h, biases):
        cols = pl.ds(h * HEAD, HEAD)
        if not isinstance(h, int):
            cols = pl.ds(pl.multiple_of(h * HEAD, HEAD), HEAD)
        scores = lax.dot_general(
            q_ref[:, cols],
            k_all[slot, :, cols],
            (((1,), (1,)), ((), ())),
            preferred_element_type=jnp.float32,
        )
        scores = scores * scale
        old_peak = peak_ref[h]
        best_peak = old_peak
        parts = []
        for b, bias in enumerate(biases):
            block = scores[:, b * BLOCK : (b + 1) * BLOCK]
            row_peak = jnp.max(block, axis=1, keepdims=True)
            weights = jnp.exp2(block - row_peak)
            part = jnp.dot(
                weights.astype(jnp.bfloat16),
                v_all[slot, b * BLOCK : (b + 1) * BLOCK, cols],
                preferred_element_type=jnp.float32,
            )
            used_peak = row_peak + bias
            best_peak = jnp.maximum(best_peak, used_peak)
            parts.append((used_peak, weights, part))
        fade = jnp.exp2(old_peak - best_peak)
        total = total_ref[h] * fade
        acc = acc_ref[h] * fade
        for used_peak, weights, part in parts:
            factor = jnp.exp2(used_peak - best_peak)
            total = total + weights * factor
            acc = acc + part * factor
        return best_peak, total, acc

    def attend(slot):
        biases = use_bias(slot)

        def one_head(h, carry):
            peak_ref[h], total_ref[h], acc_ref[h] = attend_head(slot, h, biases)
            return carry

        lax.fori_loop(0, heads, one_head, 0, unroll=2)

    def last_hop(stream, h):
        buffer = k_all if stream == K_FWD else v_all
        forward = h % 2 == 0
        cols = pl.ds(h * HEAD, HEAD)
        return pltpu.make_async_remote_copy(
            src_ref=buffer.at[half - 1 if forward else half + 1, :, cols],
            dst_ref=buffer.at[half, :, cols],
            send_sem=last_send.at[stream, h],
            recv_sem=last_recv.at[stream, h],
            device_id={"ctx": right if forward else left},
            device_id_type=MESH,
        )

    attend(0)

    def middle(step, carry):
        back = count - step
        hop(K_FWD, step).wait_recv()
        hop(K_FWD, step + 1).start()
        hop(K_BWD, back).wait_recv()
        hop(K_BWD, back - 1).start()
        hop(V_FWD, step).wait_recv()
        hop(V_FWD, step + 1).start()
        hop(V_BWD, back).wait_recv()
        hop(V_BWD, back - 1).start()
        attend(step)
        attend(back)
        return carry

    lax.fori_loop(1, half - 1, middle, 0)

    for side_of, key_stream in ((0, K_FWD), (1, K_BWD)):
        hop(key_stream, half + 1 if side_of else half - 1).wait_recv()
        for pair in range(min(2, heads // 2)):
            last_hop(K_FWD, 2 * pair + side_of).start()
    for side_of, value_stream in ((0, V_FWD), (1, V_BWD)):
        hop(value_stream, half + 1 if side_of else half - 1).wait_recv()
        for pair in range(heads // 2):
            last_hop(V_FWD, 2 * pair + side_of).start()
            if pair + 2 < heads // 2:
                last_hop(K_FWD, 2 * (pair + 2) + side_of).start()
    attend(half - 1)
    attend(half + 1)
    load_w.wait()
    biases = use_bias(half)
    group = 2 * HEAD

    def exchange(g):
        cols = pl.ds(g * group, group)
        return pltpu.make_async_remote_copy(
            src_ref=own_ref.at[:, cols],
            dst_ref=other_ref.at[:, cols],
            send_sem=pair_send.at[g],
            recv_sem=pair_recv.at[g],
            device_id={"head": 1 - side},
            device_id_type=MESH,
        )

    def project(source, which, g):
        w_rows = pl.ds(pl.multiple_of(which * width + g * group, group), group)
        return jnp.dot(
            source[:, g * group : (g + 1) * group],
            w_ref[w_rows, :],
            preferred_element_type=jnp.float32,
        )

    groups = width // group
    for g in range(groups):
        for h in (2 * g, 2 * g + 1):
            last_hop(K_FWD, h).wait_recv()
            last_hop(V_FWD, h).wait_recv()
            _, total, acc = attend_head(half, h, biases)
            total = jnp.sum(total, axis=1, keepdims=True)
            own_ref[:, h * HEAD : (h + 1) * HEAD] = (acc / total).astype(jnp.bfloat16)
        exchange(g).start()
        if g == 0:
            sum_ref[...] = project(own_ref, side, g)
        else:
            exchange(g - 1).wait_recv()
            sum_ref[...] += project(other_ref, 1 - side, g - 1) + project(own_ref, side, g)
    exchange(groups - 1).wait_recv()
    out_ref[...] = (sum_ref[...] + project(other_ref, 1 - side, groups - 1)).astype(out_ref.dtype)

    store = pltpu.make_async_copy(out_ref, out_any, load_sem.at[4])
    store.start()
    for g in range(groups):
        exchange(g).wait_send()
    for h in range(heads):
        last_hop(K_FWD, h).wait_send()
        last_hop(V_FWD, h).wait_send()

    def drain(step, carry):
        hop(K_FWD, step).wait_send()
        hop(V_FWD, step).wait_send()
        hop(K_BWD, count - step).wait_send()
        hop(V_BWD, count - step).wait_send()
        return carry

    lax.fori_loop(1, half, drain, 0)
    store.wait()


def ring_call(queries, keys, values, out_weight, random_blocks, window_blocks, global_blocks):
    count = lax.axis_size("ctx")
    rows, width = queries.shape
    heads = width // HEAD
    out_width = out_weight.shape[1]
    smem = pl.BlockSpec(memory_space=pltpu.SMEM)
    hbm = pl.BlockSpec(memory_space=pltpu.HBM)
    return pl.pallas_call(
        functools.partial(ring_kernel, count),
        out_shape=jax.ShapeDtypeStruct((rows, out_width), jnp.bfloat16),
        in_specs=[smem] * 3 + [hbm] * 4,
        out_specs=pl.BlockSpec(memory_space=pl.ANY),
        scratch_shapes=[
            pltpu.VMEM((rows, width), jnp.bfloat16),
            pltpu.VMEM(out_weight.shape, jnp.bfloat16),
            pltpu.VMEM((count, rows, width), jnp.bfloat16),
            pltpu.VMEM((count, rows, width), jnp.bfloat16),
            pltpu.VMEM((heads, rows, HEAD), jnp.float32),
            pltpu.VMEM((heads, rows, HEAD), jnp.float32),
            pltpu.VMEM((heads, rows, HEAD), jnp.float32),
            pltpu.VMEM((rows, width), jnp.bfloat16),
            pltpu.VMEM((rows, width), jnp.bfloat16),
            pltpu.VMEM((rows, out_width), jnp.float32),
            pltpu.VMEM((rows, out_width), jnp.bfloat16),
            pltpu.SemaphoreType.DMA((5,)),
            pltpu.SemaphoreType.DMA((4, count)),
            pltpu.SemaphoreType.DMA((4, count)),
            pltpu.SemaphoreType.DMA((2, heads)),
            pltpu.SemaphoreType.DMA((2, heads)),
            pltpu.SemaphoreType.DMA((heads // 2,)),
            pltpu.SemaphoreType.DMA((heads // 2,)),
        ],
        compiler_params=pltpu.CompilerParams(
            collective_id=1, has_side_effects=True, vmem_limit_bytes=60 << 20
        ),
    )(random_blocks.T, window_blocks, global_blocks, queries, keys, values, out_weight)


def solution(mesh):
    placed = (
        P(("groups", "ctx"), "head"),
        P(("groups", "ctx"), "head"),
        P(("groups", "ctx"), "head"),
        P(None, "head"),
        P("groups", None),
        P(("groups", "ctx")),
        P("groups"),
    )
    return jax.shard_map(
        per_device,
        mesh=mesh,
        in_specs=placed,
        out_specs=P(("groups", "ctx"), "head"),
        check_vma=False,
    )
```

```python
import functools
import math

import jax
import jax.numpy as jnp
from jax import lax
from jax.experimental import pallas as pl
from jax.experimental.pallas import tpu as pltpu
from jax.sharding import PartitionSpec as P

HEAD = 128
BLOCK = 128
WMAX = 1
GLOB = 2
RAND = 3

LARGE_NEG = -1e30
MESH = pl.DeviceIdType.MESH

K_FWD, V_FWD, K_BWD, V_BWD = range(4)


GRID_DEPTH = 4
GRID_WIDTH = 2
OWN, PARTNER, NEAR, NEAR_P, CROSS, CROSS_P, FAR, FAR_P = range(8)
BELOW, BELOW_P = 2, 3
SCALE = math.log2(math.e) / math.sqrt(HEAD)


def grid_kernel(
    table_ref,
    q_hbm,
    k_hbm,
    v_hbm,
    w_hbm,
    out_ref,
    q_all,
    k_all,
    v_all,
    w_ref,
    win_all,
    bias_ref,
    peak_ref,
    total_ref,
    acc_ref,
    weight_ref,
    inverse_ref,
    up_part,
    up_stat,
    up_part_in,
    up_stat_in,
    side_part,
    side_stat,
    side_part_in,
    side_stat_in,
    own_ref,
    other_ref,
    sum_ref,
    load_sem,
    w_sem,
    kv_send,
    kv_recv,
    q_send,
    q_recv,
    win_send,
    win_recv,
    up_send,
    up_recv,
    side_send,
    side_recv,
    pair_send,
    pair_recv,
    ready,
    back_part,
    back_stat,
    back_send,
    ask_send,
    ask_recv,
):
    rows, width = q_hbm.shape
    heads = width // HEAD // 2
    span_width = heads * HEAD
    half = heads // 2
    last = heads - 1
    dev_blocks = rows // BLOCK
    position = lax.axis_index("ctx")
    side = lax.axis_index("head")
    depth, column = position // GRID_WIDTH, position % GRID_WIDTH
    inner = (depth > 0) & (depth < GRID_DEPTH - 1)

    def mate(level):
        return level + 1 - 2 * (level % 2)

    def chip(level, col):
        return level * GRID_WIDTH + col

    cross_depth = GRID_DEPTH - 1 - depth
    partner = chip(depth, 1 - column)
    near = chip(mate(depth), column)
    near_partner = chip(mate(depth), 1 - column)
    cross = chip(cross_depth, column)
    cross_partner = chip(cross_depth, 1 - column)
    far = chip(mate(cross_depth), column)
    far_inner = chip(mate(cross_depth), column)
    far_inner_partner = chip(mate(cross_depth), 1 - column)
    far_partner = chip(mate(cross_depth), 1 - column)

    def at(h):
        if isinstance(h, int):
            return pl.ds(h * HEAD, HEAD)
        return pl.ds(pl.multiple_of(h * HEAD, HEAD), HEAD)

    def held(col, h):
        return pl.ds(pl.multiple_of((col * heads + h) * HEAD, HEAD), HEAD)

    def share(col):
        return pl.ds(pl.multiple_of(col * span_width, span_width), span_width)

    def spot(col, h):
        return pl.ds(pl.multiple_of((2 * h + col) * HEAD, HEAD), HEAD)

    def send(src, dst, send_sem, recv_sem, target):
        return pltpu.make_async_remote_copy(
            src_ref=src,
            dst_ref=dst,
            send_sem=send_sem,
            recv_sem=recv_sem,
            device_id=target,
            device_id_type=MESH,
        )

    def key_value(kind, slot, h):
        whole, kept = (k_hbm, v_hbm)[kind], (k_all, v_all)[kind]
        if slot == PARTNER:
            source = whole.at[:, held(1 - column, h)]
        elif slot in (NEAR, CROSS):
            source = whole.at[:, held(column, h)]
        else:
            source = kept.at[{NEAR_P: PARTNER, CROSS_P: PARTNER, FAR: NEAR, FAR_P: NEAR_P}[slot], :, at(h)]
        target = {PARTNER: partner, NEAR: near, NEAR_P: near}.get(slot, cross)
        return send(
            source,
            kept.at[slot, :, at(h)],
            kv_send.at[slot, kind, h],
            kv_recv.at[slot, kind, h],
            {"ctx": target},
        )

    def start_key_value(slot, h):
        for kind in (0, 1):
            key_value(kind, slot, h).start()

    def wait_key_value(slot, h):
        for kind in (0, 1):
            key_value(kind, slot, h).wait_recv()

    def query(slot):
        source = {
            PARTNER: q_hbm.at[:, share(1 - column)],
            BELOW: q_hbm.at[:, share(column)],
            BELOW_P: q_all.at[PARTNER],
        }[slot]
        target = {"ctx": partner if slot == PARTNER else near}
        return (
            send(source, q_all.at[slot], q_send.at[slot], q_recv.at[slot], target),
            send(
                win_all.at[PARTNER if slot == BELOW_P else OWN],
                win_all.at[slot],
                win_send.at[slot],
                win_recv.at[slot],
                target,
            ),
        )

    def start_query(slot):
        for copy in query(slot):
            copy.start()

    def wait_query(slot):
        for copy in query(slot):
            copy.wait_recv()

    def upward(which, h):
        target = {"ctx": near_partner if which else near}
        return (
            send(up_stat.at[which, h, 0:1], up_stat_in.at[which, h, 0:1], up_send.at[1, which, h], up_recv.at[1, which, h], target),
            send(up_part.at[which, h], up_part_in.at[which, h], up_send.at[0, which, h], up_recv.at[0, which, h], target),
        )

    def ask(slot):
        source = q_hbm.at[:, held(column, last)] if slot == OWN else q_all.at[slot, :, at(last)]
        return send(
            source, q_all.at[CROSS + slot, :, at(last)], ask_send.at[slot], ask_recv.at[slot], {"ctx": cross}
        )

    def ask_reach(slot):
        return send(
            win_all.at[slot], win_all.at[CROSS + slot], win_send.at[CROSS + slot], win_recv.at[CROSS + slot], {"ctx": cross}
        )

    def answer(slot):
        which = slot % 2
        target = {"ctx": {CROSS: cross, CROSS_P: cross_partner, FAR: far, FAR_P: far_partner}[slot]}
        i = slot - CROSS
        return (
            send(back_stat.at[i, 0:1], up_stat_in.at[which, last, 0:1], back_send.at[1, i], up_recv.at[1, which, last], target),
            send(back_part.at[i], up_part_in.at[which, last], back_send.at[0, i], up_recv.at[0, which, last], target),
        )

    def sideways(h):
        target = {"ctx": partner}
        return (
            send(side_stat.at[h, 0:1], side_stat_in.at[h, 0:1], side_send.at[1, h], side_recv.at[1, h], target),
            send(side_part.at[h], side_part_in.at[h], side_send.at[0, h], side_recv.at[0, h], target),
        )

    def swap(h):
        return send(
            side_part.at[h],
            own_ref.at[:, spot(column, h)],
            side_send.at[0, h],
            side_recv.at[0, h],
            {"ctx": partner},
        )

    loads = [
        pltpu.make_async_copy(whole.at[:, share(column)], kept.at[OWN], load_sem.at[i])
        for i, (whole, kept) in enumerate(((q_hbm, q_all), (k_hbm, k_all), (v_hbm, v_all)))
    ]

    def load_w(core, h, col):
        source = pl.multiple_of(core * width + (col * heads + h) * HEAD, HEAD)
        target = pl.multiple_of(core * width + (2 * h + col) * HEAD, HEAD)
        return pltpu.make_async_copy(
            w_hbm.at[pl.ds(source, HEAD)], w_ref.at[pl.ds(target, HEAD)], w_sem.at[core, h, col]
        )

    barrier = pltpu.get_barrier_semaphore()

    def greet(semaphore, target):
        pl.semaphore_signal(semaphore, inc=1, device_id=target, device_id_type=MESH)

    @pl.when(inner)
    def _():
        for target in (cross, near, near_partner, cross_partner, far, far_partner):
            greet(barrier, {"ctx": target})

    greet(barrier, {"ctx": partner})
    greet(barrier, {"head": 1 - side})
    for load in loads:
        load.start()
    for a in range(dev_blocks):
        win_all[OWN, a] = jnp.full((8, HEAD), table_ref[RAND, a], jnp.int32)

    def use_bias(q, query_chip, pairs, win=None):
        win = q if win is None else win
        for k, key_chip in pairs:
            for a in range(dev_blocks):
                query_block = query_chip * dev_blocks + a
                for b in range(dev_blocks):
                    key_block = key_chip * dev_blocks + b
                    offset = jnp.abs(key_block - query_block)
                    needed = jnp.where(offset <= WMAX, offset, 1 << 30)
                    used = table_ref[RAND + 1, 0] == key_block
                    for g in range(1, GLOB):
                        used = used | (table_ref[RAND + 1, g] == key_block)
                    for r in range(RAND):
                        used = used | (table_ref[r, query_block] == key_block)
                    bias = jnp.where(used, 0.0, LARGE_NEG)
                    bias = jnp.where(win_all[win, a] >= needed, 0.0, bias)
                    bias_ref[q, k, a, :, b * BLOCK : (b + 1) * BLOCK] = bias

    def steps(pairs, h, first=False):
        cols = at(h)
        every = [
            lax.dot_general(
                q_all[q, :, cols],
                k_all[k, :, cols],
                (((1,), (1,)), ((), ())),
                preferred_element_type=jnp.float32,
            )
            for q, k in pairs
        ]
        held = []
        for (q, k), scores in zip(pairs, every):
            for a in range(dev_blocks):
                span = slice(a * BLOCK, (a + 1) * BLOCK)
                block = scores[span] * SCALE + bias_ref[q, k, a, 0:1, :]
                best = jnp.max(block, axis=1, keepdims=True)
                old = None
                if first:
                    best = jnp.broadcast_to(best, (BLOCK, HEAD))
                else:
                    old = peak_ref[q, h, span]
                    best = jnp.maximum(old, best)
                weights = [
                    jnp.exp2(block[:, b * BLOCK : (b + 1) * BLOCK] - best) for b in range(dev_blocks)
                ]
                total = functools.reduce(jnp.add, weights)
                rounded = jnp.concatenate([w.astype(jnp.bfloat16) for w in weights], axis=1)
                held.append((old, best, total, rounded))
        for i, (q, k) in enumerate(pairs):
            mine = held[i * dev_blocks : (i + 1) * dev_blocks]
            part = jnp.dot(
                jnp.concatenate([m[3] for m in mine], axis=0),
                v_all[k, :, cols],
                preferred_element_type=jnp.float32,
            )
            for a, (old, best, total, _) in enumerate(mine):
                span = slice(a * BLOCK, (a + 1) * BLOCK)
                acc = part[span]
                if not first:
                    fade = jnp.exp2(old - best)
                    total = total + total_ref[q, h, span] * fade
                    acc = acc + acc_ref[q, h, span] * fade
                peak_ref[q, h, span] = best
                total_ref[q, h, span] = total
                acc_ref[q, h, span] = acc

    def step(q, k, h, first=False):
        steps([(q, k)], h, first)

    def score(pairs, h):
        cols = at(h)
        every = [
            lax.dot_general(
                q_all[q, :, cols],
                k_all[k, :, cols],
                (((1,), (1,)), ((), ())),
                preferred_element_type=jnp.float32,
            )
            for q, k in pairs
        ]
        for (q, k), scores in zip(pairs, every):
            for a in range(dev_blocks):
                span = slice(a * BLOCK, (a + 1) * BLOCK)
                block = scores[span] * SCALE + bias_ref[q, k, a, 0:1, :]
                old = peak_ref[q, h, span]
                best = jnp.maximum(old, jnp.max(block, axis=1, keepdims=True))
                weights = [
                    jnp.exp2(block[:, b * BLOCK : (b + 1) * BLOCK] - best) for b in range(dev_blocks)
                ]
                fade = jnp.exp2(old - best)
                weight_ref[q, span] = jnp.concatenate([w.astype(jnp.bfloat16) for w in weights], axis=1)
                peak_ref[q, h, span] = best
                total_ref[q, h, span] = functools.reduce(jnp.add, weights, total_ref[q, h, span] * fade)
                acc_ref[q, h, span] = acc_ref[q, h, span] * fade

    def value(q, k, h):
        return acc_ref[q, h] + jnp.dot(weight_ref[q], v_all[k, :, at(h)], preferred_element_type=jnp.float32)

    def level(q, h, stat):
        total = jnp.sum(total_ref[q, h], axis=1, keepdims=True)
        inverse_ref[q] = jnp.broadcast_to(1.0 / total, (rows, HEAD))
        stat[...] = (peak_ref[q, h] + jnp.log2(total)).T[:8]

    def pack(q, h, part, stat):
        level(q, h, stat)
        part[...] = (acc_ref[q, h] * inverse_ref[q]).astype(jnp.bfloat16)

    group = 2 * HEAD

    def group_cols(g):
        if isinstance(g, int):
            return pl.ds(g * group, group)
        return pl.ds(pl.multiple_of(g * group, group), group)

    def exchange(g):
        return send(
            own_ref.at[:, group_cols(g)],
            other_ref.at[:, group_cols(g)],
            pair_send.at[g],
            pair_recv.at[g],
            {"head": 1 - side},
        )

    def project(source, which, g):
        w_rows = pl.ds(pl.multiple_of(which * width + g * group, group), group)
        return jnp.dot(source[:, group_cols(g)], w_ref[w_rows, :], preferred_element_type=jnp.float32)

    def finish(h):
        exchange(h).start()

        @pl.when(h == 0)
        def _():
            sum_ref[...] = project(own_ref, side, h)

        @pl.when(h > 0)
        def _():
            exchange(h - 1).wait_recv()
            sum_ref[...] += project(own_ref, side, h) + project(other_ref, 1 - side, h - 1)

    def loop(lower, upper, body):
        def run(h, carry):
            body(h)
            return carry

        lax.fori_loop(lower, upper, run, 0)

    def column_of(stat):
        return jnp.broadcast_to(stat[0:1, :], (HEAD, rows)).T

    def join(h):
        for copy in sideways(h):
            copy.wait_recv()
        upward(1, h)[0].wait_recv()
        upward(0, h)[0].wait_recv()
        mine, theirs = column_of(side_stat_in[h]), column_of(up_stat_in[1, h])
        best = jnp.maximum(mine, theirs)
        mine, theirs = jnp.exp2(mine - best), jnp.exp2(theirs - best)
        inverse = 1.0 / (mine + theirs)
        inverse_ref[0] = theirs * inverse
        part = side_part_in[h].astype(jnp.float32) * (mine * inverse)
        old, theirs = peak_ref[OWN, h], column_of(up_stat_in[0, h])
        best = jnp.maximum(old, theirs)
        fade, theirs = jnp.exp2(old - best), jnp.exp2(theirs - best)
        inverse = 1.0 / (jnp.sum(total_ref[OWN, h] * fade, axis=1, keepdims=True) + theirs)
        inverse_ref[1] = theirs * inverse
        acc_ref[OWN, h] = acc_ref[OWN, h] * (fade * inverse)
        acc_ref[PARTNER, h] = part
        for which, q, col in ((1, PARTNER, 1 - column), (0, OWN, column)):
            upward(which, h)[1].wait_recv()
            total = acc_ref[q, h] + up_part_in[which, h].astype(jnp.float32) * inverse_ref[1 - which]
            own_ref[:, spot(col, h)] = total.astype(jnp.bfloat16)
        finish(h)

    def each_w(action):
        def one(h):
            for core in (0, 1):
                for col in (0, 1):
                    getattr(load_w(core, h, col), action)()

        loop(0, heads, one)

    @pl.when(inner)
    def _():
        pl.semaphore_wait(barrier, 4)
        start_key_value(CROSS, 0)
        for h in range(half):
            start_key_value(PARTNER, h)
        start_query(PARTNER)
        loop(1, last, lambda h: start_key_value(CROSS, h))
        ask(OWN).start()
        ask_reach(OWN).start()
        loop(half, heads, lambda h: start_key_value(PARTNER, h))
        pl.semaphore_wait(ready, 4)
        loop(0, heads, lambda h: start_key_value(NEAR, h))
        each_w("start")
        close_by = ((OWN, position), (PARTNER, partner), (NEAR, near), (NEAR_P, near_partner))
        beyond = ((CROSS, cross), (CROSS_P, cross_partner), (FAR, far), (FAR_P, far_partner))
        use_bias(OWN, position, close_by + beyond)
        for load in loads:
            load.wait()
        loop(0, heads, lambda h: step(OWN, OWN, h, first=True))

        def first_round(h):
            wait_key_value(PARTNER, h)
            start_key_value(NEAR_P, h)

            @pl.when(h < last)
            def _():
                start_key_value(CROSS_P, h)

            step(OWN, PARTNER, h)

        loop(0, heads, first_round)
        wait_query(PARTNER)
        ask(PARTNER).start()
        ask_reach(PARTNER).start()
        use_bias(PARTNER, partner, close_by + beyond)
        loop(0, heads, lambda h: step(PARTNER, OWN, h, first=True))
        loop(0, heads, lambda h: step(PARTNER, PARTNER, h))
        wait_query(BELOW)
        ask(BELOW).start()
        use_bias(BELOW, near, beyond)

        def pass_on(h):
            wait_key_value(NEAR, h)
            start_key_value(FAR, h)
            wait_key_value(NEAR_P, h)
            start_key_value(FAR_P, h)

        def meet_near(h):
            steps([(OWN, NEAR), (PARTNER, NEAR)], h)
            steps([(OWN, NEAR_P), (PARTNER, NEAR_P)], h)

        loop(0, half, pass_on)

        def second_round(h):
            wait_key_value(CROSS, h)
            steps([(OWN, CROSS), (PARTNER, CROSS)], h)
            step(BELOW, CROSS, h, first=True)

            @pl.when(h < half)
            def _():
                meet_near(h)

            wait_key_value(CROSS_P, h)
            steps([(OWN, CROSS_P), (PARTNER, CROSS_P)], h)
            step(BELOW, CROSS_P, h)

        loop(0, last, second_round)
        wait_query(BELOW_P)
        ask(BELOW_P).start()
        use_bias(BELOW_P, near_partner, beyond)

        def third_round(h):
            step(BELOW_P, CROSS, h, first=True)
            step(BELOW_P, CROSS_P, h)

        loop(0, last, third_round)

        ask_reach(OWN).wait_recv()
        ask_reach(PARTNER).wait_recv()
        chips = {CROSS: cross, CROSS_P: cross_partner, FAR: far, FAR_P: far_partner}
        for slot in (CROSS, CROSS_P):
            use_bias(slot, chips[slot], close_by)
        for slot in (FAR, FAR_P):
            use_bias(slot, chips[slot], close_by, OWN)

        def reply():
            wait_key_value(NEAR, last)
            wait_key_value(NEAR_P, last)
            for slot in (OWN, PARTNER, BELOW, BELOW_P):
                ask(slot).wait_recv()
            for pair in ((FAR_P, FAR), (CROSS_P, CROSS)):
                steps([(q, OWN) for q in pair], last, first=True)
                for k in (PARTNER, NEAR, NEAR_P):
                    steps([(q, k) for q in pair], last)
                for q in pair:
                    pack(q, last, back_part.at[q - CROSS], back_stat.at[q - CROSS])
                    for copy in answer(q):
                        copy.start()

        def settle():
            meet_near(last)
            pack(PARTNER, last, side_part.at[last], side_stat.at[last])
            for copy in sideways(last):
                copy.start()

        each_w("wait")

        def close(h):
            swap(h).wait_recv()
            finish(h)

        def late(h):
            wait_key_value(FAR, h)
            steps([(BELOW_P, FAR), (BELOW, FAR)], h)
            steps([(PARTNER, FAR), (OWN, FAR)], h)

            @pl.when(h < last - half)
            def _():
                pass_on(h + half)

            key_value(0, FAR_P, h).wait_recv()
            score([(BELOW_P, FAR_P), (BELOW, FAR_P)], h)
            score([(PARTNER, FAR_P), (OWN, FAR_P)], h)
            for which, q in ((1, BELOW_P), (0, BELOW)):
                level(q, h, up_stat.at[which, h])
                upward(which, h)[0].start()
            for q in (PARTNER, OWN):
                total = jnp.sum(total_ref[q, h], axis=1, keepdims=True)
                inverse_ref[q] = jnp.broadcast_to(1.0 / total, (rows, HEAD))
            key_value(1, FAR_P, h).wait_recv()
            def lift(which, q):
                up_part[which, h] = (value(q, FAR_P, h) * inverse_ref[q]).astype(jnp.bfloat16)
                upward(which, h)[1].start()

            lift(1, BELOW_P)
            side_part[h] = (value(PARTNER, FAR_P, h) * inverse_ref[PARTNER]).astype(jnp.bfloat16)
            swap(h).start()
            lift(0, BELOW)
            own_ref[:, spot(column, h)] = (value(OWN, FAR_P, h) * inverse_ref[OWN]).astype(jnp.bfloat16)

            @pl.when(h < last - half)
            def _():
                meet_near(h + half)

        def drain(h):
            for slot in (PARTNER, NEAR, NEAR_P):
                for kind in (0, 1):
                    key_value(kind, slot, h).wait_send()

            @pl.when(h < last)
            def _():
                for slot in (CROSS, CROSS_P, FAR, FAR_P):
                    for kind in (0, 1):
                        key_value(kind, slot, h).wait_send()

        def late_round(h):
            @pl.when(h == last - 1)
            def _():
                reply()

            @pl.when(h < last)
            def _():
                late(h)

            @pl.when(h == last - 1)
            def _():
                settle()

            @pl.when(h > 0)
            def _():
                close(h - 1)

        loop(0, last + 1, late_round)
        loop(0, heads, drain)
        for copy in query(PARTNER):
            copy.wait_send()
        for slot in (OWN, PARTNER, BELOW, BELOW_P):
            ask(slot).wait_send()
        for slot in (OWN, PARTNER):
            ask_reach(slot).wait_send()
        for copy in sideways(last):
            copy.wait_send()
        join(jnp.int32(last))

    @pl.when(jnp.logical_not(inner))
    def _():
        pl.semaphore_wait(barrier, 6)
        for target in (near, near_partner, far_inner, far_inner_partner):
            greet(ready, {"ctx": target})
        start_query(BELOW)
        for h in range(half):
            start_key_value(PARTNER, h)
        start_query(PARTNER)
        for h in range(half):
            start_key_value(NEAR, h)
        loop(half, heads, lambda h: start_key_value(PARTNER, h))
        each_w("start")
        close_by = ((OWN, position), (PARTNER, partner), (NEAR, near), (NEAR_P, near_partner))
        use_bias(OWN, position, close_by)
        for load in loads:
            load.wait()

        def relay(h):
            @pl.when(h >= half)
            def _():
                start_key_value(NEAR, h)

            wait_key_value(PARTNER, h)
            start_key_value(NEAR_P, h)

        loop(0, half, relay)
        wait_query(PARTNER)
        start_query(BELOW_P)
        loop(half, heads, relay)
        use_bias(PARTNER, partner, close_by)

        def early(h):
            step(OWN, OWN, h, first=True)
            step(PARTNER, OWN, h, first=True)
            steps([(PARTNER, PARTNER), (OWN, PARTNER)], h)

        loop(0, heads, early)

        def middle(h):
            wait_key_value(NEAR, h)
            steps([(PARTNER, NEAR), (OWN, NEAR)], h)

        loop(0, heads, middle)

        def side_round(h):
            wait_key_value(NEAR_P, h)
            steps([(PARTNER, NEAR_P), (OWN, NEAR_P)], h)
            pack(PARTNER, h, side_part.at[h], side_stat.at[h])
            for copy in sideways(h):
                copy.start()

        loop(0, heads, side_round)
        each_w("wait")

        def drain(h):
            for slot in (PARTNER, NEAR, NEAR_P):
                for kind in (0, 1):
                    key_value(kind, slot, h).wait_send()
            for copy in sideways(h):
                copy.wait_send()

        loop(0, heads, drain)
        for slot in (PARTNER, BELOW, BELOW_P):
            for copy in query(slot):
                copy.wait_send()

        loop(0, heads, join)

    exchange(heads - 1).wait_recv()
    out_ref[...] = (sum_ref[...] + project(other_ref, 1 - side, heads - 1)).astype(out_ref.dtype)
    loop(0, heads, lambda g: exchange(g).wait_send())

    @pl.when(inner)
    def _():
        def drain_late(h):
            swap(h).wait_send()
            for which in (0, 1):
                for copy in upward(which, h):
                    copy.wait_send()

        loop(0, last, drain_late)
        for slot in (CROSS, CROSS_P, FAR, FAR_P):
            for copy in answer(slot):
                copy.wait_send()


def grid_call(queries, keys, values, out_weight, random_blocks, window_blocks, global_blocks):
    rows, width = queries.shape
    heads = width // HEAD // 2
    dev_blocks = rows // BLOCK
    out_width = out_weight.shape[1]
    hbm = pl.BlockSpec(memory_space=pltpu.HBM)
    state = pltpu.VMEM((8, heads, rows, HEAD), jnp.float32)
    dma = pltpu.SemaphoreType.DMA
    blocks = random_blocks.shape[0]
    table = (
        jnp.pad(random_blocks.T, ((0, 2), (0, 0)))
        + jnp.pad(window_blocks[None], ((RAND, 1), (0, blocks - dev_blocks)))
        + jnp.pad(global_blocks[None], ((RAND + 1, 0), (0, blocks - GLOB)))
    )
    return pl.pallas_call(
        grid_kernel,
        out_shape=jax.ShapeDtypeStruct((rows, out_width), jnp.bfloat16),
        in_specs=[pl.BlockSpec(memory_space=pltpu.SMEM)] + [hbm] * 4,
        out_specs=pl.BlockSpec(memory_space=pltpu.VMEM),
        scratch_shapes=[
            pltpu.VMEM((8, rows, width // 2), jnp.bfloat16),
            pltpu.VMEM((8, rows, width // 2), jnp.bfloat16),
            pltpu.VMEM((8, rows, width // 2), jnp.bfloat16),
            pltpu.VMEM(out_weight.shape, jnp.bfloat16),
            pltpu.VMEM((8, dev_blocks, 8, HEAD), jnp.int32),
            pltpu.VMEM((8, 8, dev_blocks, 8, rows), jnp.float32),
            state,
            state,
            state,
            pltpu.VMEM((4, rows, rows), jnp.bfloat16),
            pltpu.VMEM((8, rows, HEAD), jnp.float32),
            pltpu.VMEM((2, heads, rows, HEAD), jnp.bfloat16),
            pltpu.VMEM((2, heads, 8, rows), jnp.float32),
            pltpu.VMEM((2, heads, rows, HEAD), jnp.bfloat16),
            pltpu.VMEM((2, heads, 8, rows), jnp.float32),
            pltpu.VMEM((heads, rows, HEAD), jnp.bfloat16),
            pltpu.VMEM((heads, 8, rows), jnp.float32),
            pltpu.VMEM((heads, rows, HEAD), jnp.bfloat16),
            pltpu.VMEM((heads, 8, rows), jnp.float32),
            pltpu.VMEM((rows, width), jnp.bfloat16),
            pltpu.VMEM((rows, width), jnp.bfloat16),
            pltpu.VMEM((rows, out_width), jnp.float32),
            dma((3,)),
            dma((2, heads, 2)),
            dma((8, 2, heads)),
            dma((8, 2, heads)),
            dma((4,)),
            dma((4,)),
            dma((8,)),
            dma((8,)),
            dma((2, 2, heads)),
            dma((2, 2, heads)),
            dma((2, heads)),
            dma((2, heads)),
            dma((heads,)),
            dma((heads,)),
            pltpu.SemaphoreType.REGULAR,
            pltpu.VMEM((4, rows, HEAD), jnp.bfloat16),
            pltpu.VMEM((4, 8, rows), jnp.float32),
            dma((2, 4)),
            dma((4,)),
            dma((4,)),
        ],
        compiler_params=pltpu.CompilerParams(
            collective_id=0, has_side_effects=True, vmem_limit_bytes=53 << 20
        ),
    )(table, queries, keys, values, out_weight)


def per_device(*arguments):
    if lax.axis_size("ctx") == GRID_DEPTH * GRID_WIDTH:
        return grid_call(*arguments)
    return ring_call(*arguments)


def ring_place(index, count):
    odd = index % 2
    return (1 - odd) * (index // 2) + odd * (count - 1 - index // 2)


def ring_index(place, count):
    late = place // (count // 2)
    return (1 - late) * (2 * place) + late * (2 * (count - 1 - place) + 1)


def ring_kernel(
    count,
    random_ref,
    window_ref,
    global_ref,
    q_hbm,
    k_hbm,
    v_hbm,
    w_hbm,
    out_any,
    q_ref,
    w_ref,
    k_all,
    v_all,
    peak_ref,
    total_ref,
    acc_ref,
    own_ref,
    other_ref,
    sum_ref,
    out_ref,
    load_sem,
    send_sem,
    recv_sem,
    last_send,
    last_recv,
    pair_send,
    pair_recv,
):
    rows, width = q_ref.shape
    heads = width // HEAD
    dev_blocks = rows // BLOCK
    half = count // 2
    position = lax.axis_index("ctx")
    side = lax.axis_index("head")
    place = ring_place(position, count)
    right = ring_index((place + 1) % count, count)
    left = ring_index((place + count - 1) % count, count)

    load_k = pltpu.make_async_copy(k_hbm, k_all.at[0], load_sem.at[0])
    load_v = pltpu.make_async_copy(v_hbm, v_all.at[0], load_sem.at[1])
    load_q = pltpu.make_async_copy(q_hbm, q_ref, load_sem.at[2])
    load_w = pltpu.make_async_copy(w_hbm, w_ref, load_sem.at[3])
    load_k.start()
    load_v.start()
    load_q.start()

    barrier = pltpu.get_barrier_semaphore()
    pl.semaphore_signal(barrier, inc=1, device_id={"ctx": left}, device_id_type=MESH)
    pl.semaphore_signal(barrier, inc=1, device_id={"ctx": right}, device_id_type=MESH)
    pl.semaphore_signal(barrier, inc=1, device_id={"head": 1 - side}, device_id_type=MESH)
    pl.semaphore_wait(barrier, 3)

    def hop(stream, slot):
        buffer = k_all if stream in (K_FWD, K_BWD) else v_all
        forward = stream in (K_FWD, V_FWD)
        source = slot - 1 if forward else (slot + 1) % count
        return pltpu.make_async_remote_copy(
            src_ref=buffer.at[source],
            dst_ref=buffer.at[slot],
            send_sem=send_sem.at[stream, slot],
            recv_sem=recv_sem.at[stream, slot],
            device_id={"ctx": right if forward else left},
            device_id_type=MESH,
        )

    load_k.wait()
    hop(K_FWD, 1).start()
    hop(K_BWD, count - 1).start()
    load_v.wait()
    hop(V_FWD, 1).start()
    hop(V_BWD, count - 1).start()
    load_q.wait()
    load_w.start()

    peak_ref[...] = jnp.full_like(peak_ref, LARGE_NEG)
    total_ref[...] = jnp.zeros_like(total_ref)
    acc_ref[...] = jnp.zeros_like(acc_ref)
    scale = math.log2(math.e) / math.sqrt(HEAD)

    def use_bias(slot):
        owner = ring_index((place + count - slot) % count, count)
        row_block = lax.broadcasted_iota(jnp.int32, (rows, HEAD), 0) // BLOCK
        biases = []
        for b in range(dev_blocks):
            key_block = owner * dev_blocks + b
            bias = jnp.full((rows, HEAD), LARGE_NEG, jnp.float32)
            for a in range(dev_blocks):
                query_block = position * dev_blocks + a
                offset = jnp.abs(key_block - query_block)
                used = (offset <= window_ref[a]) & (offset <= WMAX)
                for g in range(GLOB):
                    used = used | (global_ref[g] == key_block)
                for r in range(RAND):
                    used = used | (random_ref[r, query_block] == key_block)
                bias = jnp.where(row_block == a, jnp.where(used, 0.0, LARGE_NEG), bias)
            biases.append(bias)
        return biases

    def attend_head(slot, h, biases):
        cols = pl.ds(h * HEAD, HEAD)
        if not isinstance(h, int):
            cols = pl.ds(pl.multiple_of(h * HEAD, HEAD), HEAD)
        scores = lax.dot_general(
            q_ref[:, cols],
            k_all[slot, :, cols],
            (((1,), (1,)), ((), ())),
            preferred_element_type=jnp.float32,
        )
        scores = scores * scale
        old_peak = peak_ref[h]
        best_peak = old_peak
        parts = []
        for b, bias in enumerate(biases):
            block = scores[:, b * BLOCK : (b + 1) * BLOCK]
            row_peak = jnp.max(block, axis=1, keepdims=True)
            weights = jnp.exp2(block - row_peak)
            part = jnp.dot(
                weights.astype(jnp.bfloat16),
                v_all[slot, b * BLOCK : (b + 1) * BLOCK, cols],
                preferred_element_type=jnp.float32,
            )
            used_peak = row_peak + bias
            best_peak = jnp.maximum(best_peak, used_peak)
            parts.append((used_peak, weights, part))
        fade = jnp.exp2(old_peak - best_peak)
        total = total_ref[h] * fade
        acc = acc_ref[h] * fade
        for used_peak, weights, part in parts:
            factor = jnp.exp2(used_peak - best_peak)
            total = total + weights * factor
            acc = acc + part * factor
        return best_peak, total, acc

    def attend(slot):
        biases = use_bias(slot)

        def one_head(h, carry):
            peak_ref[h], total_ref[h], acc_ref[h] = attend_head(slot, h, biases)
            return carry

        lax.fori_loop(0, heads, one_head, 0, unroll=2)

    def last_hop(stream, h):
        buffer = k_all if stream == K_FWD else v_all
        forward = h % 2 == 0
        cols = pl.ds(h * HEAD, HEAD)
        return pltpu.make_async_remote_copy(
            src_ref=buffer.at[half - 1 if forward else half + 1, :, cols],
            dst_ref=buffer.at[half, :, cols],
            send_sem=last_send.at[stream, h],
            recv_sem=last_recv.at[stream, h],
            device_id={"ctx": right if forward else left},
            device_id_type=MESH,
        )

    attend(0)

    def middle(step, carry):
        back = count - step
        hop(K_FWD, step).wait_recv()
        hop(K_FWD, step + 1).start()
        hop(K_BWD, back).wait_recv()
        hop(K_BWD, back - 1).start()
        hop(V_FWD, step).wait_recv()
        hop(V_FWD, step + 1).start()
        hop(V_BWD, back).wait_recv()
        hop(V_BWD, back - 1).start()
        attend(step)
        attend(back)
        return carry

    lax.fori_loop(1, half - 1, middle, 0)

    for side_of, key_stream in ((0, K_FWD), (1, K_BWD)):
        hop(key_stream, half + 1 if side_of else half - 1).wait_recv()
        for pair in range(min(2, heads // 2)):
            last_hop(K_FWD, 2 * pair + side_of).start()
    for side_of, value_stream in ((0, V_FWD), (1, V_BWD)):
        hop(value_stream, half + 1 if side_of else half - 1).wait_recv()
        for pair in range(heads // 2):
            last_hop(V_FWD, 2 * pair + side_of).start()
            if pair + 2 < heads // 2:
                last_hop(K_FWD, 2 * (pair + 2) + side_of).start()
    attend(half - 1)
    attend(half + 1)
    load_w.wait()
    biases = use_bias(half)
    group = 2 * HEAD

    def exchange(g):
        cols = pl.ds(g * group, group)
        return pltpu.make_async_remote_copy(
            src_ref=own_ref.at[:, cols],
            dst_ref=other_ref.at[:, cols],
            send_sem=pair_send.at[g],
            recv_sem=pair_recv.at[g],
            device_id={"head": 1 - side},
            device_id_type=MESH,
        )

    def project(source, which, g):
        w_rows = pl.ds(pl.multiple_of(which * width + g * group, group), group)
        return jnp.dot(
            source[:, g * group : (g + 1) * group],
            w_ref[w_rows, :],
            preferred_element_type=jnp.float32,
        )

    groups = width // group
    for g in range(groups):
        for h in (2 * g, 2 * g + 1):
            last_hop(K_FWD, h).wait_recv()
            last_hop(V_FWD, h).wait_recv()
            _, total, acc = attend_head(half, h, biases)
            total = jnp.sum(total, axis=1, keepdims=True)
            own_ref[:, h * HEAD : (h + 1) * HEAD] = (acc / total).astype(jnp.bfloat16)
        exchange(g).start()
        if g == 0:
            sum_ref[...] = project(own_ref, side, g)
        else:
            exchange(g - 1).wait_recv()
            sum_ref[...] += project(other_ref, 1 - side, g - 1) + project(own_ref, side, g)
    exchange(groups - 1).wait_recv()
    out_ref[...] = (sum_ref[...] + project(other_ref, 1 - side, groups - 1)).astype(out_ref.dtype)

    store = pltpu.make_async_copy(out_ref, out_any, load_sem.at[4])
    store.start()
    for g in range(groups):
        exchange(g).wait_send()
    for h in range(heads):
        last_hop(K_FWD, h).wait_send()
        last_hop(V_FWD, h).wait_send()

    def drain(step, carry):
        hop(K_FWD, step).wait_send()
        hop(V_FWD, step).wait_send()
        hop(K_BWD, count - step).wait_send()
        hop(V_BWD, count - step).wait_send()
        return carry

    lax.fori_loop(1, half, drain, 0)
    store.wait()


def ring_call(queries, keys, values, out_weight, random_blocks, window_blocks, global_blocks):
    count = lax.axis_size("ctx")
    rows, width = queries.shape
    heads = width // HEAD
    out_width = out_weight.shape[1]
    smem = pl.BlockSpec(memory_space=pltpu.SMEM)
    hbm = pl.BlockSpec(memory_space=pltpu.HBM)
    return pl.pallas_call(
        functools.partial(ring_kernel, count),
        out_shape=jax.ShapeDtypeStruct((rows, out_width), jnp.bfloat16),
        in_specs=[smem] * 3 + [hbm] * 4,
        out_specs=pl.BlockSpec(memory_space=pl.ANY),
        scratch_shapes=[
            pltpu.VMEM((rows, width), jnp.bfloat16),
            pltpu.VMEM(out_weight.shape, jnp.bfloat16),
            pltpu.VMEM((count, rows, width), jnp.bfloat16),
            pltpu.VMEM((count, rows, width), jnp.bfloat16),
            pltpu.VMEM((heads, rows, HEAD), jnp.float32),
            pltpu.VMEM((heads, rows, HEAD), jnp.float32),
            pltpu.VMEM((heads, rows, HEAD), jnp.float32),
            pltpu.VMEM((rows, width), jnp.bfloat16),
            pltpu.VMEM((rows, width), jnp.bfloat16),
            pltpu.VMEM((rows, out_width), jnp.float32),
            pltpu.VMEM((rows, out_width), jnp.bfloat16),
            pltpu.SemaphoreType.DMA((5,)),
            pltpu.SemaphoreType.DMA((4, count)),
            pltpu.SemaphoreType.DMA((4, count)),
            pltpu.SemaphoreType.DMA((2, heads)),
            pltpu.SemaphoreType.DMA((2, heads)),
            pltpu.SemaphoreType.DMA((heads // 2,)),
            pltpu.SemaphoreType.DMA((heads // 2,)),
        ],
        compiler_params=pltpu.CompilerParams(
            collective_id=1, has_side_effects=True, vmem_limit_bytes=60 << 20
        ),
    )(random_blocks.T, window_blocks, global_blocks, queries, keys, values, out_weight)


def solution(mesh):
    placed = (
        P(("groups", "ctx"), "head"),
        P(("groups", "ctx"), "head"),
        P(("groups", "ctx"), "head"),
        P(None, "head"),
        P("groups", None),
        P(("groups", "ctx")),
        P("groups"),
    )
    return jax.shard_map(
        per_device,
        mesh=mesh,
        in_specs=placed,
        out_specs=P(("groups", "ctx"), "head"),
        check_vma=False,
    )
```

```python
import functools
import math

import jax
import jax.numpy as jnp
from jax import lax
from jax.experimental import pallas as pl
from jax.experimental.pallas import tpu as pltpu
from jax.sharding import PartitionSpec as P

HEAD = 128
BLOCK = 128
WMAX = 1
GLOB = 2
RAND = 3

LARGE_NEG = -1e30
MESH = pl.DeviceIdType.MESH

K_FWD, V_FWD, K_BWD, V_BWD = range(4)


GRID_DEPTH = 4
GRID_WIDTH = 2
OWN, PARTNER, NEAR, NEAR_P, CROSS, CROSS_P, FAR, FAR_P = range(8)
BELOW, BELOW_P = 2, 3
SCALE = math.log2(math.e) / math.sqrt(HEAD)


def grid_kernel(
    table_ref,
    q_hbm,
    k_hbm,
    v_hbm,
    w_hbm,
    out_ref,
    q_all,
    k_all,
    v_all,
    w_ref,
    win_all,
    bias_ref,
    peak_ref,
    total_ref,
    acc_ref,
    weight_ref,
    inverse_ref,
    up_part,
    up_stat,
    up_part_in,
    up_stat_in,
    side_part,
    side_stat,
    side_part_in,
    side_stat_in,
    own_ref,
    other_ref,
    sum_ref,
    load_sem,
    w_sem,
    kv_send,
    kv_recv,
    q_send,
    q_recv,
    win_send,
    win_recv,
    up_send,
    up_recv,
    side_send,
    side_recv,
    pair_send,
    pair_recv,
    ready,
    back_part,
    back_stat,
    back_send,
    ask_send,
    ask_recv,
):
    rows, width = q_hbm.shape
    heads = width // HEAD // 2
    span_width = heads * HEAD
    half = heads // 2
    last = heads - 1
    dev_blocks = rows // BLOCK
    position = lax.axis_index("ctx")
    side = lax.axis_index("head")
    depth, column = position // GRID_WIDTH, position % GRID_WIDTH
    inner = (depth > 0) & (depth < GRID_DEPTH - 1)

    def mate(level):
        return level + 1 - 2 * (level % 2)

    def chip(level, col):
        return level * GRID_WIDTH + col

    cross_depth = GRID_DEPTH - 1 - depth
    partner = chip(depth, 1 - column)
    near = chip(mate(depth), column)
    near_partner = chip(mate(depth), 1 - column)
    cross = chip(cross_depth, column)
    cross_partner = chip(cross_depth, 1 - column)
    far = chip(mate(cross_depth), column)
    far_inner = chip(mate(cross_depth), column)
    far_inner_partner = chip(mate(cross_depth), 1 - column)
    far_partner = chip(mate(cross_depth), 1 - column)

    def at(h):
        if isinstance(h, int):
            return pl.ds(h * HEAD, HEAD)
        return pl.ds(pl.multiple_of(h * HEAD, HEAD), HEAD)

    def held(col, h):
        return pl.ds(pl.multiple_of((col * heads + h) * HEAD, HEAD), HEAD)

    def share(col):
        return pl.ds(pl.multiple_of(col * span_width, span_width), span_width)

    def spot(col, h):
        return pl.ds(pl.multiple_of((2 * h + col) * HEAD, HEAD), HEAD)

    def send(src, dst, send_sem, recv_sem, target):
        return pltpu.make_async_remote_copy(
            src_ref=src,
            dst_ref=dst,
            send_sem=send_sem,
            recv_sem=recv_sem,
            device_id=target,
            device_id_type=MESH,
        )

    def key_value(kind, slot, h):
        whole, kept = (k_hbm, v_hbm)[kind], (k_all, v_all)[kind]
        if slot == PARTNER:
            source = whole.at[:, held(1 - column, h)]
        elif slot in (NEAR, CROSS):
            source = whole.at[:, held(column, h)]
        else:
            source = kept.at[{NEAR_P: PARTNER, CROSS_P: PARTNER, FAR: NEAR, FAR_P: NEAR_P}[slot], :, at(h)]
        target = {PARTNER: partner, NEAR: near, NEAR_P: near}.get(slot, cross)
        return send(
            source,
            kept.at[slot, :, at(h)],
            kv_send.at[slot, kind, h],
            kv_recv.at[slot, kind, h],
            {"ctx": target},
        )

    def start_key_value(slot, h):
        for kind in (0, 1):
            key_value(kind, slot, h).start()

    def wait_key_value(slot, h):
        for kind in (0, 1):
            key_value(kind, slot, h).wait_recv()

    def query(slot):
        source = {
            PARTNER: q_hbm.at[:, share(1 - column)],
            BELOW: q_hbm.at[:, share(column)],
            BELOW_P: q_all.at[PARTNER],
        }[slot]
        target = {"ctx": partner if slot == PARTNER else near}
        return (
            send(source, q_all.at[slot], q_send.at[slot], q_recv.at[slot], target),
            send(
                win_all.at[PARTNER if slot == BELOW_P else OWN],
                win_all.at[slot],
                win_send.at[slot],
                win_recv.at[slot],
                target,
            ),
        )

    def start_query(slot):
        for copy in query(slot):
            copy.start()

    def wait_query(slot):
        for copy in query(slot):
            copy.wait_recv()

    def upward(which, h):
        target = {"ctx": near_partner if which else near}
        return (
            send(up_stat.at[which, h, 0:1], up_stat_in.at[which, h, 0:1], up_send.at[1, which, h], up_recv.at[1, which, h], target),
            send(up_part.at[which, h], up_part_in.at[which, h], up_send.at[0, which, h], up_recv.at[0, which, h], target),
        )

    def ask(slot):
        source = q_hbm.at[:, held(column, last)] if slot == OWN else q_all.at[slot, :, at(last)]
        return send(
            source, q_all.at[CROSS + slot, :, at(last)], ask_send.at[slot], ask_recv.at[slot], {"ctx": cross}
        )

    def ask_reach(slot):
        return send(
            win_all.at[slot], win_all.at[CROSS + slot], win_send.at[CROSS + slot], win_recv.at[CROSS + slot], {"ctx": cross}
        )

    def answer(slot):
        which = slot % 2
        target = {"ctx": {CROSS: cross, CROSS_P: cross_partner, FAR: far, FAR_P: far_partner}[slot]}
        i = slot - CROSS
        return (
            send(back_stat.at[i, 0:1], up_stat_in.at[which, last, 0:1], back_send.at[1, i], up_recv.at[1, which, last], target),
            send(back_part.at[i], up_part_in.at[which, last], back_send.at[0, i], up_recv.at[0, which, last], target),
        )

    def sideways(h):
        target = {"ctx": partner}
        return (
            send(side_stat.at[h, 0:1], side_stat_in.at[h, 0:1], side_send.at[1, h], side_recv.at[1, h], target),
            send(side_part.at[h], side_part_in.at[h], side_send.at[0, h], side_recv.at[0, h], target),
        )

    def swap(h):
        return send(
            side_part.at[h],
            own_ref.at[:, spot(column, h)],
            side_send.at[0, h],
            side_recv.at[0, h],
            {"ctx": partner},
        )

    loads = [
        pltpu.make_async_copy(whole.at[:, share(column)], kept.at[OWN], load_sem.at[i])
        for i, (whole, kept) in enumerate(((q_hbm, q_all), (k_hbm, k_all), (v_hbm, v_all)))
    ]

    def load_w(core, h, col):
        source = pl.multiple_of(core * width + (col * heads + h) * HEAD, HEAD)
        target = pl.multiple_of(core * width + (2 * h + col) * HEAD, HEAD)
        return pltpu.make_async_copy(
            w_hbm.at[pl.ds(source, HEAD)], w_ref.at[pl.ds(target, HEAD)], w_sem.at[core, h, col]
        )

    barrier = pltpu.get_barrier_semaphore()

    def greet(semaphore, target):
        pl.semaphore_signal(semaphore, inc=1, device_id=target, device_id_type=MESH)

    @pl.when(inner)
    def _():
        for target in (cross, near, near_partner, cross_partner, far, far_partner):
            greet(barrier, {"ctx": target})

    greet(barrier, {"ctx": partner})
    greet(barrier, {"head": 1 - side})
    for load in loads:
        load.start()
    for a in range(dev_blocks):
        win_all[OWN, a] = jnp.full((8, HEAD), table_ref[RAND, a], jnp.int32)

    def use_bias(q, query_chip, pairs, win=None):
        win = q if win is None else win
        for k, key_chip in pairs:
            for a in range(dev_blocks):
                query_block = query_chip * dev_blocks + a
                for b in range(dev_blocks):
                    key_block = key_chip * dev_blocks + b
                    offset = jnp.abs(key_block - query_block)
                    needed = jnp.where(offset <= WMAX, offset, 1 << 30)
                    used = table_ref[RAND + 1, 0] == key_block
                    for g in range(1, GLOB):
                        used = used | (table_ref[RAND + 1, g] == key_block)
                    for r in range(RAND):
                        used = used | (table_ref[r, query_block] == key_block)
                    bias = jnp.where(used, 0.0, LARGE_NEG)
                    bias = jnp.where(win_all[win, a] >= needed, 0.0, bias)
                    bias_ref[q, k, a, :, b * BLOCK : (b + 1) * BLOCK] = bias

    def steps(pairs, h, first=False):
        cols = at(h)
        every = [
            lax.dot_general(
                q_all[q, :, cols],
                k_all[k, :, cols],
                (((1,), (1,)), ((), ())),
                preferred_element_type=jnp.float32,
            )
            for q, k in pairs
        ]
        held = []
        for (q, k), scores in zip(pairs, every):
            for a in range(dev_blocks):
                span = slice(a * BLOCK, (a + 1) * BLOCK)
                block = scores[span] * SCALE + bias_ref[q, k, a, 0:1, :]
                best = jnp.max(block, axis=1, keepdims=True)
                old = None
                if first:
                    best = jnp.broadcast_to(best, (BLOCK, HEAD))
                else:
                    old = peak_ref[q, h, span]
                    best = jnp.maximum(old, best)
                weights = [
                    jnp.exp2(block[:, b * BLOCK : (b + 1) * BLOCK] - best) for b in range(dev_blocks)
                ]
                total = functools.reduce(jnp.add, weights)
                rounded = jnp.concatenate([w.astype(jnp.bfloat16) for w in weights], axis=1)
                held.append((old, best, total, rounded))
        for i, (q, k) in enumerate(pairs):
            mine = held[i * dev_blocks : (i + 1) * dev_blocks]
            part = jnp.dot(
                jnp.concatenate([m[3] for m in mine], axis=0),
                v_all[k, :, cols],
                preferred_element_type=jnp.float32,
            )
            for a, (old, best, total, _) in enumerate(mine):
                span = slice(a * BLOCK, (a + 1) * BLOCK)
                acc = part[span]
                if not first:
                    fade = jnp.exp2(old - best)
                    total = total + total_ref[q, h, span] * fade
                    acc = acc + acc_ref[q, h, span] * fade
                peak_ref[q, h, span] = best
                total_ref[q, h, span] = total
                acc_ref[q, h, span] = acc

    def step(q, k, h, first=False):
        steps([(q, k)], h, first)

    def score(pairs, h):
        cols = at(h)
        every = [
            lax.dot_general(
                q_all[q, :, cols],
                k_all[k, :, cols],
                (((1,), (1,)), ((), ())),
                preferred_element_type=jnp.float32,
            )
            for q, k in pairs
        ]
        for (q, k), scores in zip(pairs, every):
            for a in range(dev_blocks):
                span = slice(a * BLOCK, (a + 1) * BLOCK)
                block = scores[span] * SCALE + bias_ref[q, k, a, 0:1, :]
                old = peak_ref[q, h, span]
                best = jnp.maximum(old, jnp.max(block, axis=1, keepdims=True))
                weights = [
                    jnp.exp2(block[:, b * BLOCK : (b + 1) * BLOCK] - best) for b in range(dev_blocks)
                ]
                fade = jnp.exp2(old - best)
                weight_ref[q, span] = jnp.concatenate([w.astype(jnp.bfloat16) for w in weights], axis=1)
                peak_ref[q, h, span] = best
                total_ref[q, h, span] = functools.reduce(jnp.add, weights, total_ref[q, h, span] * fade)
                acc_ref[q, h, span] = acc_ref[q, h, span] * fade

    def value(q, k, h):
        return acc_ref[q, h] + jnp.dot(weight_ref[q], v_all[k, :, at(h)], preferred_element_type=jnp.float32)

    def level(q, h, stat):
        total = jnp.sum(total_ref[q, h], axis=1, keepdims=True)
        inverse_ref[q] = jnp.broadcast_to(1.0 / total, (rows, HEAD))
        stat[...] = (peak_ref[q, h] + jnp.log2(total)).T[:8]

    def pack(q, h, part, stat):
        level(q, h, stat)
        part[...] = (acc_ref[q, h] * inverse_ref[q]).astype(jnp.bfloat16)

    group = 2 * HEAD

    def group_cols(g):
        if isinstance(g, int):
            return pl.ds(g * group, group)
        return pl.ds(pl.multiple_of(g * group, group), group)

    def exchange(g):
        return send(
            own_ref.at[:, group_cols(g)],
            other_ref.at[:, group_cols(g)],
            pair_send.at[g],
            pair_recv.at[g],
            {"head": 1 - side},
        )

    def project(source, which, g):
        w_rows = pl.ds(pl.multiple_of(which * width + g * group, group), group)
        return jnp.dot(source[:, group_cols(g)], w_ref[w_rows, :], preferred_element_type=jnp.float32)

    def finish(h):
        exchange(h).start()

        @pl.when(h == 0)
        def _():
            sum_ref[...] = project(own_ref, side, h)

        @pl.when(h > 0)
        def _():
            exchange(h - 1).wait_recv()
            sum_ref[...] += project(own_ref, side, h) + project(other_ref, 1 - side, h - 1)

    def loop(lower, upper, body):
        def run(h, carry):
            body(h)
            return carry

        lax.fori_loop(lower, upper, run, 0)

    def column_of(stat):
        return jnp.broadcast_to(stat[0:1, :], (HEAD, rows)).T

    def join(h):
        for copy in sideways(h):
            copy.wait_recv()
        upward(1, h)[0].wait_recv()
        upward(0, h)[0].wait_recv()
        mine, theirs = column_of(side_stat_in[h]), column_of(up_stat_in[1, h])
        best = jnp.maximum(mine, theirs)
        mine, theirs = jnp.exp2(mine - best), jnp.exp2(theirs - best)
        inverse = 1.0 / (mine + theirs)
        inverse_ref[0] = theirs * inverse
        part = side_part_in[h].astype(jnp.float32) * (mine * inverse)
        old, theirs = peak_ref[OWN, h], column_of(up_stat_in[0, h])
        best = jnp.maximum(old, theirs)
        fade, theirs = jnp.exp2(old - best), jnp.exp2(theirs - best)
        inverse = 1.0 / (jnp.sum(total_ref[OWN, h] * fade, axis=1, keepdims=True) + theirs)
        inverse_ref[1] = theirs * inverse
        acc_ref[OWN, h] = acc_ref[OWN, h] * (fade * inverse)
        acc_ref[PARTNER, h] = part
        for which, q, col in ((1, PARTNER, 1 - column), (0, OWN, column)):
            upward(which, h)[1].wait_recv()
            total = acc_ref[q, h] + up_part_in[which, h].astype(jnp.float32) * inverse_ref[1 - which]
            own_ref[:, spot(col, h)] = total.astype(jnp.bfloat16)
        finish(h)

    def each_w(action):
        def one(h):
            for core in (0, 1):
                for col in (0, 1):
                    getattr(load_w(core, h, col), action)()

        loop(0, heads, one)

    @pl.when(inner)
    def _():
        pl.semaphore_wait(barrier, 4)
        start_key_value(CROSS, 0)
        for h in range(half):
            start_key_value(PARTNER, h)
        start_query(PARTNER)
        loop(1, last, lambda h: start_key_value(CROSS, h))
        ask(OWN).start()
        ask_reach(OWN).start()
        loop(half, heads, lambda h: start_key_value(PARTNER, h))
        pl.semaphore_wait(ready, 4)
        loop(0, heads, lambda h: start_key_value(NEAR, h))
        each_w("start")
        close_by = ((OWN, position), (PARTNER, partner), (NEAR, near), (NEAR_P, near_partner))
        beyond = ((CROSS, cross), (CROSS_P, cross_partner), (FAR, far), (FAR_P, far_partner))
        use_bias(OWN, position, close_by + beyond)
        for load in loads:
            load.wait()
        loop(0, heads, lambda h: step(OWN, OWN, h, first=True))

        def first_round(h):
            wait_key_value(PARTNER, h)
            start_key_value(NEAR_P, h)

            @pl.when(h < last)
            def _():
                start_key_value(CROSS_P, h)

            step(OWN, PARTNER, h)

        loop(0, heads, first_round)
        wait_query(PARTNER)
        ask(PARTNER).start()
        ask_reach(PARTNER).start()
        use_bias(PARTNER, partner, close_by + beyond)
        loop(0, heads, lambda h: step(PARTNER, OWN, h, first=True))
        loop(0, heads, lambda h: step(PARTNER, PARTNER, h))
        wait_query(BELOW)
        ask(BELOW).start()
        use_bias(BELOW, near, beyond)

        def pass_on(h):
            wait_key_value(NEAR, h)
            start_key_value(FAR, h)
            wait_key_value(NEAR_P, h)
            start_key_value(FAR_P, h)

        def meet_near(h):
            steps([(OWN, NEAR), (PARTNER, NEAR)], h)
            steps([(OWN, NEAR_P), (PARTNER, NEAR_P)], h)

        loop(0, half, pass_on)

        def second_round(h):
            wait_key_value(CROSS, h)
            steps([(OWN, CROSS), (PARTNER, CROSS)], h)
            step(BELOW, CROSS, h, first=True)

            @pl.when(h < half)
            def _():
                meet_near(h)

            wait_key_value(CROSS_P, h)
            steps([(OWN, CROSS_P), (PARTNER, CROSS_P)], h)
            step(BELOW, CROSS_P, h)

        loop(0, last, second_round)
        wait_query(BELOW_P)
        ask(BELOW_P).start()
        use_bias(BELOW_P, near_partner, beyond)

        def third_round(h):
            step(BELOW_P, CROSS, h, first=True)
            step(BELOW_P, CROSS_P, h)

        loop(0, last, third_round)

        ask_reach(OWN).wait_recv()
        ask_reach(PARTNER).wait_recv()
        chips = {CROSS: cross, CROSS_P: cross_partner, FAR: far, FAR_P: far_partner}
        for slot in (CROSS, CROSS_P):
            use_bias(slot, chips[slot], close_by)
        for slot in (FAR, FAR_P):
            use_bias(slot, chips[slot], close_by, OWN)

        def reply():
            pairs = ((FAR_P, FAR), (CROSS_P, CROSS))
            wait_key_value(NEAR, last)
            for slot in (OWN, PARTNER, BELOW, BELOW_P):
                ask(slot).wait_recv()
            for pair in pairs:
                steps([(q, OWN) for q in pair], last, first=True)
                for k in (PARTNER, NEAR):
                    steps([(q, k) for q in pair], last)
            wait_key_value(NEAR_P, last)
            for pair in pairs:
                steps([(q, NEAR_P) for q in pair], last)
                for q in pair:
                    pack(q, last, back_part.at[q - CROSS], back_stat.at[q - CROSS])
                    for copy in answer(q):
                        copy.start()

        def settle():
            meet_near(last)
            pack(PARTNER, last, side_part.at[last], side_stat.at[last])
            for copy in sideways(last):
                copy.start()

        each_w("wait")

        def close(h):
            swap(h).wait_recv()
            finish(h)

        def late(h):
            wait_key_value(FAR, h)
            steps([(BELOW_P, FAR), (BELOW, FAR)], h)
            steps([(PARTNER, FAR), (OWN, FAR)], h)

            @pl.when(h < last - half)
            def _():
                pass_on(h + half)

            key_value(0, FAR_P, h).wait_recv()
            score([(BELOW_P, FAR_P), (BELOW, FAR_P)], h)
            score([(PARTNER, FAR_P), (OWN, FAR_P)], h)
            for which, q in ((1, BELOW_P), (0, BELOW)):
                level(q, h, up_stat.at[which, h])
                upward(which, h)[0].start()
            for q in (PARTNER, OWN):
                total = jnp.sum(total_ref[q, h], axis=1, keepdims=True)
                inverse_ref[q] = jnp.broadcast_to(1.0 / total, (rows, HEAD))
            key_value(1, FAR_P, h).wait_recv()
            def lift(which, q):
                up_part[which, h] = (value(q, FAR_P, h) * inverse_ref[q]).astype(jnp.bfloat16)
                upward(which, h)[1].start()

            lift(1, BELOW_P)
            side_part[h] = (value(PARTNER, FAR_P, h) * inverse_ref[PARTNER]).astype(jnp.bfloat16)
            swap(h).start()
            lift(0, BELOW)
            own_ref[:, spot(column, h)] = (value(OWN, FAR_P, h) * inverse_ref[OWN]).astype(jnp.bfloat16)

            @pl.when(h < last - half)
            def _():
                meet_near(h + half)

        def drain(h):
            for slot in (FAR, FAR_P):
                for kind in (0, 1):
                    key_value(kind, slot, h).wait_send()

        def drain_early(h):
            for slot in (PARTNER, NEAR, NEAR_P):
                for kind in (0, 1):
                    key_value(kind, slot, h).wait_send()

            @pl.when(h < last)
            def _():
                for slot in (CROSS, CROSS_P):
                    for kind in (0, 1):
                        key_value(kind, slot, h).wait_send()

        def late_round(h):
            @pl.when(h == last - 1)
            def _():
                reply()

            @pl.when(h < last)
            def _():
                late(h)

            @pl.when(h == last - 1)
            def _():
                settle()

            @pl.when(h > 0)
            def _():
                close(h - 1)

        loop(0, heads, drain_early)
        loop(0, last + 1, late_round)
        loop(0, last, drain)
        for copy in query(PARTNER):
            copy.wait_send()
        for slot in (OWN, PARTNER, BELOW, BELOW_P):
            ask(slot).wait_send()
        for slot in (OWN, PARTNER):
            ask_reach(slot).wait_send()
        for copy in sideways(last):
            copy.wait_send()
        join(jnp.int32(last))

    @pl.when(jnp.logical_not(inner))
    def _():
        pl.semaphore_wait(barrier, 6)
        for target in (near, near_partner, far_inner, far_inner_partner):
            greet(ready, {"ctx": target})
        start_query(BELOW)
        for h in range(half):
            start_key_value(PARTNER, h)
        start_query(PARTNER)
        for h in range(half):
            start_key_value(NEAR, h)
        loop(half, heads, lambda h: start_key_value(PARTNER, h))
        each_w("start")
        close_by = ((OWN, position), (PARTNER, partner), (NEAR, near), (NEAR_P, near_partner))
        use_bias(OWN, position, close_by)
        for load in loads:
            load.wait()

        def relay(h):
            @pl.when(h >= half)
            def _():
                start_key_value(NEAR, h)

            wait_key_value(PARTNER, h)
            start_key_value(NEAR_P, h)

        loop(0, half, relay)
        wait_query(PARTNER)
        start_query(BELOW_P)
        loop(half, heads, relay)
        use_bias(PARTNER, partner, close_by)

        def early(h):
            step(OWN, OWN, h, first=True)
            step(PARTNER, OWN, h, first=True)
            steps([(PARTNER, PARTNER), (OWN, PARTNER)], h)

        loop(0, heads, early)

        def middle(h):
            wait_key_value(NEAR, h)
            steps([(PARTNER, NEAR), (OWN, NEAR)], h)

        loop(0, heads, middle)

        def side_round(h):
            wait_key_value(NEAR_P, h)
            steps([(PARTNER, NEAR_P), (OWN, NEAR_P)], h)
            pack(PARTNER, h, side_part.at[h], side_stat.at[h])
            for copy in sideways(h):
                copy.start()

        loop(0, heads, side_round)
        each_w("wait")

        def drain(h):
            for slot in (PARTNER, NEAR, NEAR_P):
                for kind in (0, 1):
                    key_value(kind, slot, h).wait_send()
            for copy in sideways(h):
                copy.wait_send()

        loop(0, heads, drain)
        for slot in (PARTNER, BELOW, BELOW_P):
            for copy in query(slot):
                copy.wait_send()

        loop(0, heads, join)

    exchange(heads - 1).wait_recv()
    out_ref[...] = (sum_ref[...] + project(other_ref, 1 - side, heads - 1)).astype(out_ref.dtype)
    loop(0, heads, lambda g: exchange(g).wait_send())

    @pl.when(inner)
    def _():
        def drain_late(h):
            swap(h).wait_send()
            for which in (0, 1):
                for copy in upward(which, h):
                    copy.wait_send()

        loop(0, last, drain_late)
        for slot in (CROSS, CROSS_P, FAR, FAR_P):
            for copy in answer(slot):
                copy.wait_send()


def grid_call(queries, keys, values, out_weight, random_blocks, window_blocks, global_blocks):
    rows, width = queries.shape
    heads = width // HEAD // 2
    dev_blocks = rows // BLOCK
    out_width = out_weight.shape[1]
    hbm = pl.BlockSpec(memory_space=pltpu.HBM)
    state = pltpu.VMEM((8, heads, rows, HEAD), jnp.float32)
    dma = pltpu.SemaphoreType.DMA
    blocks = random_blocks.shape[0]
    table = (
        jnp.pad(random_blocks.T, ((0, 2), (0, 0)))
        + jnp.pad(window_blocks[None], ((RAND, 1), (0, blocks - dev_blocks)))
        + jnp.pad(global_blocks[None], ((RAND + 1, 0), (0, blocks - GLOB)))
    )
    return pl.pallas_call(
        grid_kernel,
        out_shape=jax.ShapeDtypeStruct((rows, out_width), jnp.bfloat16),
        in_specs=[pl.BlockSpec(memory_space=pltpu.SMEM)] + [hbm] * 4,
        out_specs=pl.BlockSpec(memory_space=pltpu.VMEM),
        scratch_shapes=[
            pltpu.VMEM((8, rows, width // 2), jnp.bfloat16),
            pltpu.VMEM((8, rows, width // 2), jnp.bfloat16),
            pltpu.VMEM((8, rows, width // 2), jnp.bfloat16),
            pltpu.VMEM(out_weight.shape, jnp.bfloat16),
            pltpu.VMEM((8, dev_blocks, 8, HEAD), jnp.int32),
            pltpu.VMEM((8, 8, dev_blocks, 8, rows), jnp.float32),
            state,
            state,
            state,
            pltpu.VMEM((4, rows, rows), jnp.bfloat16),
            pltpu.VMEM((8, rows, HEAD), jnp.float32),
            pltpu.VMEM((2, heads, rows, HEAD), jnp.bfloat16),
            pltpu.VMEM((2, heads, 8, rows), jnp.float32),
            pltpu.VMEM((2, heads, rows, HEAD), jnp.bfloat16),
            pltpu.VMEM((2, heads, 8, rows), jnp.float32),
            pltpu.VMEM((heads, rows, HEAD), jnp.bfloat16),
            pltpu.VMEM((heads, 8, rows), jnp.float32),
            pltpu.VMEM((heads, rows, HEAD), jnp.bfloat16),
            pltpu.VMEM((heads, 8, rows), jnp.float32),
            pltpu.VMEM((rows, width), jnp.bfloat16),
            pltpu.VMEM((rows, width), jnp.bfloat16),
            pltpu.VMEM((rows, out_width), jnp.float32),
            dma((3,)),
            dma((2, heads, 2)),
            dma((8, 2, heads)),
            dma((8, 2, heads)),
            dma((4,)),
            dma((4,)),
            dma((8,)),
            dma((8,)),
            dma((2, 2, heads)),
            dma((2, 2, heads)),
            dma((2, heads)),
            dma((2, heads)),
            dma((heads,)),
            dma((heads,)),
            pltpu.SemaphoreType.REGULAR,
            pltpu.VMEM((4, rows, HEAD), jnp.bfloat16),
            pltpu.VMEM((4, 8, rows), jnp.float32),
            dma((2, 4)),
            dma((4,)),
            dma((4,)),
        ],
        compiler_params=pltpu.CompilerParams(
            collective_id=0, has_side_effects=True, vmem_limit_bytes=53 << 20
        ),
    )(table, queries, keys, values, out_weight)


def per_device(*arguments):
    if lax.axis_size("ctx") == GRID_DEPTH * GRID_WIDTH:
        return grid_call(*arguments)
    return ring_call(*arguments)


def ring_place(index, count):
    odd = index % 2
    return (1 - odd) * (index // 2) + odd * (count - 1 - index // 2)


def ring_index(place, count):
    late = place // (count // 2)
    return (1 - late) * (2 * place) + late * (2 * (count - 1 - place) + 1)


def ring_kernel(
    count,
    random_ref,
    window_ref,
    global_ref,
    q_hbm,
    k_hbm,
    v_hbm,
    w_hbm,
    out_any,
    q_ref,
    w_ref,
    k_all,
    v_all,
    peak_ref,
    total_ref,
    acc_ref,
    own_ref,
    other_ref,
    sum_ref,
    out_ref,
    load_sem,
    send_sem,
    recv_sem,
    last_send,
    last_recv,
    pair_send,
    pair_recv,
):
    rows, width = q_ref.shape
    heads = width // HEAD
    dev_blocks = rows // BLOCK
    half = count // 2
    position = lax.axis_index("ctx")
    side = lax.axis_index("head")
    place = ring_place(position, count)
    right = ring_index((place + 1) % count, count)
    left = ring_index((place + count - 1) % count, count)

    load_k = pltpu.make_async_copy(k_hbm, k_all.at[0], load_sem.at[0])
    load_v = pltpu.make_async_copy(v_hbm, v_all.at[0], load_sem.at[1])
    load_q = pltpu.make_async_copy(q_hbm, q_ref, load_sem.at[2])
    load_w = pltpu.make_async_copy(w_hbm, w_ref, load_sem.at[3])
    load_k.start()
    load_v.start()
    load_q.start()

    barrier = pltpu.get_barrier_semaphore()
    pl.semaphore_signal(barrier, inc=1, device_id={"ctx": left}, device_id_type=MESH)
    pl.semaphore_signal(barrier, inc=1, device_id={"ctx": right}, device_id_type=MESH)
    pl.semaphore_signal(barrier, inc=1, device_id={"head": 1 - side}, device_id_type=MESH)
    pl.semaphore_wait(barrier, 3)

    def hop(stream, slot):
        buffer = k_all if stream in (K_FWD, K_BWD) else v_all
        forward = stream in (K_FWD, V_FWD)
        source = slot - 1 if forward else (slot + 1) % count
        return pltpu.make_async_remote_copy(
            src_ref=buffer.at[source],
            dst_ref=buffer.at[slot],
            send_sem=send_sem.at[stream, slot],
            recv_sem=recv_sem.at[stream, slot],
            device_id={"ctx": right if forward else left},
            device_id_type=MESH,
        )

    load_k.wait()
    hop(K_FWD, 1).start()
    hop(K_BWD, count - 1).start()
    load_v.wait()
    hop(V_FWD, 1).start()
    hop(V_BWD, count - 1).start()
    load_q.wait()
    load_w.start()

    peak_ref[...] = jnp.full_like(peak_ref, LARGE_NEG)
    total_ref[...] = jnp.zeros_like(total_ref)
    acc_ref[...] = jnp.zeros_like(acc_ref)
    scale = math.log2(math.e) / math.sqrt(HEAD)

    def use_bias(slot):
        owner = ring_index((place + count - slot) % count, count)
        row_block = lax.broadcasted_iota(jnp.int32, (rows, HEAD), 0) // BLOCK
        biases = []
        for b in range(dev_blocks):
            key_block = owner * dev_blocks + b
            bias = jnp.full((rows, HEAD), LARGE_NEG, jnp.float32)
            for a in range(dev_blocks):
                query_block = position * dev_blocks + a
                offset = jnp.abs(key_block - query_block)
                used = (offset <= window_ref[a]) & (offset <= WMAX)
                for g in range(GLOB):
                    used = used | (global_ref[g] == key_block)
                for r in range(RAND):
                    used = used | (random_ref[r, query_block] == key_block)
                bias = jnp.where(row_block == a, jnp.where(used, 0.0, LARGE_NEG), bias)
            biases.append(bias)
        return biases

    def attend_head(slot, h, biases):
        cols = pl.ds(h * HEAD, HEAD)
        if not isinstance(h, int):
            cols = pl.ds(pl.multiple_of(h * HEAD, HEAD), HEAD)
        scores = lax.dot_general(
            q_ref[:, cols],
            k_all[slot, :, cols],
            (((1,), (1,)), ((), ())),
            preferred_element_type=jnp.float32,
        )
        scores = scores * scale
        old_peak = peak_ref[h]
        best_peak = old_peak
        parts = []
        for b, bias in enumerate(biases):
            block = scores[:, b * BLOCK : (b + 1) * BLOCK]
            row_peak = jnp.max(block, axis=1, keepdims=True)
            weights = jnp.exp2(block - row_peak)
            part = jnp.dot(
                weights.astype(jnp.bfloat16),
                v_all[slot, b * BLOCK : (b + 1) * BLOCK, cols],
                preferred_element_type=jnp.float32,
            )
            used_peak = row_peak + bias
            best_peak = jnp.maximum(best_peak, used_peak)
            parts.append((used_peak, weights, part))
        fade = jnp.exp2(old_peak - best_peak)
        total = total_ref[h] * fade
        acc = acc_ref[h] * fade
        for used_peak, weights, part in parts:
            factor = jnp.exp2(used_peak - best_peak)
            total = total + weights * factor
            acc = acc + part * factor
        return best_peak, total, acc

    def attend(slot):
        biases = use_bias(slot)

        def one_head(h, carry):
            peak_ref[h], total_ref[h], acc_ref[h] = attend_head(slot, h, biases)
            return carry

        lax.fori_loop(0, heads, one_head, 0, unroll=2)

    def last_hop(stream, h):
        buffer = k_all if stream == K_FWD else v_all
        forward = h % 2 == 0
        cols = pl.ds(h * HEAD, HEAD)
        return pltpu.make_async_remote_copy(
            src_ref=buffer.at[half - 1 if forward else half + 1, :, cols],
            dst_ref=buffer.at[half, :, cols],
            send_sem=last_send.at[stream, h],
            recv_sem=last_recv.at[stream, h],
            device_id={"ctx": right if forward else left},
            device_id_type=MESH,
        )

    attend(0)

    def middle(step, carry):
        back = count - step
        hop(K_FWD, step).wait_recv()
        hop(K_FWD, step + 1).start()
        hop(K_BWD, back).wait_recv()
        hop(K_BWD, back - 1).start()
        hop(V_FWD, step).wait_recv()
        hop(V_FWD, step + 1).start()
        hop(V_BWD, back).wait_recv()
        hop(V_BWD, back - 1).start()
        attend(step)
        attend(back)
        return carry

    lax.fori_loop(1, half - 1, middle, 0)

    for side_of, key_stream in ((0, K_FWD), (1, K_BWD)):
        hop(key_stream, half + 1 if side_of else half - 1).wait_recv()
        for pair in range(min(2, heads // 2)):
            last_hop(K_FWD, 2 * pair + side_of).start()
    for side_of, value_stream in ((0, V_FWD), (1, V_BWD)):
        hop(value_stream, half + 1 if side_of else half - 1).wait_recv()
        for pair in range(heads // 2):
            last_hop(V_FWD, 2 * pair + side_of).start()
            if pair + 2 < heads // 2:
                last_hop(K_FWD, 2 * (pair + 2) + side_of).start()
    attend(half - 1)
    attend(half + 1)
    load_w.wait()
    biases = use_bias(half)
    group = 2 * HEAD

    def exchange(g):
        cols = pl.ds(g * group, group)
        return pltpu.make_async_remote_copy(
            src_ref=own_ref.at[:, cols],
            dst_ref=other_ref.at[:, cols],
            send_sem=pair_send.at[g],
            recv_sem=pair_recv.at[g],
            device_id={"head": 1 - side},
            device_id_type=MESH,
        )

    def project(source, which, g):
        w_rows = pl.ds(pl.multiple_of(which * width + g * group, group), group)
        return jnp.dot(
            source[:, g * group : (g + 1) * group],
            w_ref[w_rows, :],
            preferred_element_type=jnp.float32,
        )

    groups = width // group
    for g in range(groups):
        for h in (2 * g, 2 * g + 1):
            last_hop(K_FWD, h).wait_recv()
            last_hop(V_FWD, h).wait_recv()
            _, total, acc = attend_head(half, h, biases)
            total = jnp.sum(total, axis=1, keepdims=True)
            own_ref[:, h * HEAD : (h + 1) * HEAD] = (acc / total).astype(jnp.bfloat16)
        exchange(g).start()
        if g == 0:
            sum_ref[...] = project(own_ref, side, g)
        else:
            exchange(g - 1).wait_recv()
            sum_ref[...] += project(other_ref, 1 - side, g - 1) + project(own_ref, side, g)
    exchange(groups - 1).wait_recv()
    out_ref[...] = (sum_ref[...] + project(other_ref, 1 - side, groups - 1)).astype(out_ref.dtype)

    store = pltpu.make_async_copy(out_ref, out_any, load_sem.at[4])
    store.start()
    for g in range(groups):
        exchange(g).wait_send()
    for h in range(heads):
        last_hop(K_FWD, h).wait_send()
        last_hop(V_FWD, h).wait_send()

    def drain(step, carry):
        hop(K_FWD, step).wait_send()
        hop(V_FWD, step).wait_send()
        hop(K_BWD, count - step).wait_send()
        hop(V_BWD, count - step).wait_send()
        return carry

    lax.fori_loop(1, half, drain, 0)
    store.wait()


def ring_call(queries, keys, values, out_weight, random_blocks, window_blocks, global_blocks):
    count = lax.axis_size("ctx")
    rows, width = queries.shape
    heads = width // HEAD
    out_width = out_weight.shape[1]
    smem = pl.BlockSpec(memory_space=pltpu.SMEM)
    hbm = pl.BlockSpec(memory_space=pltpu.HBM)
    return pl.pallas_call(
        functools.partial(ring_kernel, count),
        out_shape=jax.ShapeDtypeStruct((rows, out_width), jnp.bfloat16),
        in_specs=[smem] * 3 + [hbm] * 4,
        out_specs=pl.BlockSpec(memory_space=pl.ANY),
        scratch_shapes=[
            pltpu.VMEM((rows, width), jnp.bfloat16),
            pltpu.VMEM(out_weight.shape, jnp.bfloat16),
            pltpu.VMEM((count, rows, width), jnp.bfloat16),
            pltpu.VMEM((count, rows, width), jnp.bfloat16),
            pltpu.VMEM((heads, rows, HEAD), jnp.float32),
            pltpu.VMEM((heads, rows, HEAD), jnp.float32),
            pltpu.VMEM((heads, rows, HEAD), jnp.float32),
            pltpu.VMEM((rows, width), jnp.bfloat16),
            pltpu.VMEM((rows, width), jnp.bfloat16),
            pltpu.VMEM((rows, out_width), jnp.float32),
            pltpu.VMEM((rows, out_width), jnp.bfloat16),
            pltpu.SemaphoreType.DMA((5,)),
            pltpu.SemaphoreType.DMA((4, count)),
            pltpu.SemaphoreType.DMA((4, count)),
            pltpu.SemaphoreType.DMA((2, heads)),
            pltpu.SemaphoreType.DMA((2, heads)),
            pltpu.SemaphoreType.DMA((heads // 2,)),
            pltpu.SemaphoreType.DMA((heads // 2,)),
        ],
        compiler_params=pltpu.CompilerParams(
            collective_id=1, has_side_effects=True, vmem_limit_bytes=60 << 20
        ),
    )(random_blocks.T, window_blocks, global_blocks, queries, keys, values, out_weight)


def solution(mesh):
    placed = (
        P(("groups", "ctx"), "head"),
        P(("groups", "ctx"), "head"),
        P(("groups", "ctx"), "head"),
        P(None, "head"),
        P("groups", None),
        P(("groups", "ctx")),
        P("groups"),
    )
    return jax.shard_map(
        per_device,
        mesh=mesh,
        in_specs=placed,
        out_specs=P(("groups", "ctx"), "head"),
        check_vma=False,
    )
```

```python
import functools
import math

import jax
import jax.numpy as jnp
from jax import lax
from jax.experimental import pallas as pl
from jax.experimental.pallas import tpu as pltpu
from jax.sharding import PartitionSpec as P

HEAD = 128
BLOCK = 128
WMAX = 1
GLOB = 2
RAND = 3

LARGE_NEG = -1e30
MESH = pl.DeviceIdType.MESH

K_FWD, V_FWD, K_BWD, V_BWD = range(4)


GRID_DEPTH = 4
GRID_WIDTH = 2
OWN, PARTNER, NEAR, NEAR_P, CROSS, CROSS_P, FAR, FAR_P = range(8)
BELOW, BELOW_P = 2, 3
SCALE = math.log2(math.e) / math.sqrt(HEAD)


def grid_kernel(
    table_ref,
    q_hbm,
    k_hbm,
    v_hbm,
    w_hbm,
    out_ref,
    q_all,
    k_all,
    v_all,
    w_ref,
    win_all,
    bias_ref,
    peak_ref,
    total_ref,
    acc_ref,
    weight_ref,
    inverse_ref,
    up_part,
    up_stat,
    up_part_in,
    up_stat_in,
    side_part,
    side_stat,
    side_part_in,
    side_stat_in,
    own_ref,
    other_ref,
    sum_ref,
    load_sem,
    w_sem,
    kv_send,
    kv_recv,
    q_send,
    q_recv,
    win_send,
    win_recv,
    up_send,
    up_recv,
    side_send,
    side_recv,
    pair_send,
    pair_recv,
    ready,
    back_part,
    back_stat,
    back_send,
    ask_send,
    ask_recv,
):
    rows, width = q_hbm.shape
    heads = width // HEAD // 2
    span_width = heads * HEAD
    half = heads // 2
    last = heads - 1
    dev_blocks = rows // BLOCK
    position = lax.axis_index("ctx")
    side = lax.axis_index("head")
    depth, column = position // GRID_WIDTH, position % GRID_WIDTH
    inner = (depth > 0) & (depth < GRID_DEPTH - 1)

    def mate(level):
        return level + 1 - 2 * (level % 2)

    def chip(level, col):
        return level * GRID_WIDTH + col

    cross_depth = GRID_DEPTH - 1 - depth
    partner = chip(depth, 1 - column)
    near = chip(mate(depth), column)
    near_partner = chip(mate(depth), 1 - column)
    cross = chip(cross_depth, column)
    cross_partner = chip(cross_depth, 1 - column)
    far = chip(mate(cross_depth), column)
    far_inner = chip(mate(cross_depth), column)
    far_inner_partner = chip(mate(cross_depth), 1 - column)
    far_partner = chip(mate(cross_depth), 1 - column)

    def at(h):
        if isinstance(h, int):
            return pl.ds(h * HEAD, HEAD)
        return pl.ds(pl.multiple_of(h * HEAD, HEAD), HEAD)

    def held(col, h):
        return pl.ds(pl.multiple_of((col * heads + h) * HEAD, HEAD), HEAD)

    def share(col):
        return pl.ds(pl.multiple_of(col * span_width, span_width), span_width)

    def spot(col, h):
        return pl.ds(pl.multiple_of((2 * h + col) * HEAD, HEAD), HEAD)

    def send(src, dst, send_sem, recv_sem, target):
        return pltpu.make_async_remote_copy(
            src_ref=src,
            dst_ref=dst,
            send_sem=send_sem,
            recv_sem=recv_sem,
            device_id=target,
            device_id_type=MESH,
        )

    def key_value(kind, slot, h):
        whole, kept = (k_hbm, v_hbm)[kind], (k_all, v_all)[kind]
        if slot == PARTNER:
            source = whole.at[:, held(1 - column, h)]
        elif slot in (NEAR, CROSS):
            source = whole.at[:, held(column, h)]
        else:
            source = kept.at[{NEAR_P: PARTNER, CROSS_P: PARTNER, FAR: NEAR, FAR_P: NEAR_P}[slot], :, at(h)]
        target = {PARTNER: partner, NEAR: near, NEAR_P: near}.get(slot, cross)
        return send(
            source,
            kept.at[slot, :, at(h)],
            kv_send.at[slot, kind, h],
            kv_recv.at[slot, kind, h],
            {"ctx": target},
        )

    def start_key_value(slot, h):
        for kind in (0, 1):
            key_value(kind, slot, h).start()

    def wait_key_value(slot, h):
        for kind in (0, 1):
            key_value(kind, slot, h).wait_recv()

    def query(slot):
        source = {
            PARTNER: q_hbm.at[:, share(1 - column)],
            BELOW: q_hbm.at[:, share(column)],
            BELOW_P: q_all.at[PARTNER],
        }[slot]
        target = {"ctx": partner if slot == PARTNER else near}
        return (
            send(source, q_all.at[slot], q_send.at[slot], q_recv.at[slot], target),
            send(
                win_all.at[PARTNER if slot == BELOW_P else OWN],
                win_all.at[slot],
                win_send.at[slot],
                win_recv.at[slot],
                target,
            ),
        )

    def start_query(slot):
        for copy in query(slot):
            copy.start()

    def wait_query(slot):
        for copy in query(slot):
            copy.wait_recv()

    def upward(which, h):
        target = {"ctx": near_partner if which else near}
        return (
            send(up_stat.at[which, h, 0:1], up_stat_in.at[which, h, 0:1], up_send.at[1, which, h], up_recv.at[1, which, h], target),
            send(up_part.at[which, h], up_part_in.at[which, h], up_send.at[0, which, h], up_recv.at[0, which, h], target),
        )

    def ask(slot):
        source = q_hbm.at[:, held(column, last)] if slot == OWN else q_all.at[slot, :, at(last)]
        return send(
            source, q_all.at[CROSS + slot, :, at(last)], ask_send.at[slot], ask_recv.at[slot], {"ctx": cross}
        )

    def ask_reach(slot):
        return send(
            win_all.at[slot], win_all.at[CROSS + slot], win_send.at[CROSS + slot], win_recv.at[CROSS + slot], {"ctx": cross}
        )

    def answer(slot):
        which = slot % 2
        target = {"ctx": {CROSS: cross, CROSS_P: cross_partner, FAR: far, FAR_P: far_partner}[slot]}
        i = slot - CROSS
        return (
            send(back_stat.at[i, 0:1], up_stat_in.at[which, last, 0:1], back_send.at[1, i], up_recv.at[1, which, last], target),
            send(back_part.at[i], up_part_in.at[which, last], back_send.at[0, i], up_recv.at[0, which, last], target),
        )

    def sideways(h):
        target = {"ctx": partner}
        return (
            send(side_stat.at[h, 0:1], side_stat_in.at[h, 0:1], side_send.at[1, h], side_recv.at[1, h], target),
            send(side_part.at[h], side_part_in.at[h], side_send.at[0, h], side_recv.at[0, h], target),
        )

    def swap(h):
        return send(
            side_part.at[h],
            own_ref.at[:, spot(column, h)],
            side_send.at[0, h],
            side_recv.at[0, h],
            {"ctx": partner},
        )

    loads = [
        pltpu.make_async_copy(whole.at[:, share(column)], kept.at[OWN], load_sem.at[i])
        for i, (whole, kept) in enumerate(((q_hbm, q_all), (k_hbm, k_all), (v_hbm, v_all)))
    ]

    def load_w(core, h, col):
        source = pl.multiple_of(core * width + (col * heads + h) * HEAD, HEAD)
        target = pl.multiple_of(core * width + (2 * h + col) * HEAD, HEAD)
        return pltpu.make_async_copy(
            w_hbm.at[pl.ds(source, HEAD)], w_ref.at[pl.ds(target, HEAD)], w_sem.at[core, h, col]
        )

    barrier = pltpu.get_barrier_semaphore()

    def greet(semaphore, target):
        pl.semaphore_signal(semaphore, inc=1, device_id=target, device_id_type=MESH)

    @pl.when(inner)
    def _():
        for target in (cross, near, near_partner, cross_partner, far, far_partner):
            greet(barrier, {"ctx": target})

    greet(barrier, {"ctx": partner})
    greet(barrier, {"head": 1 - side})
    for load in loads:
        load.start()
    for a in range(dev_blocks):
        win_all[OWN, a] = jnp.full((8, HEAD), table_ref[RAND, a], jnp.int32)

    def use_bias(q, query_chip, pairs, win=None):
        win = q if win is None else win
        for k, key_chip in pairs:
            for a in range(dev_blocks):
                query_block = query_chip * dev_blocks + a
                for b in range(dev_blocks):
                    key_block = key_chip * dev_blocks + b
                    offset = jnp.abs(key_block - query_block)
                    needed = jnp.where(offset <= WMAX, offset, 1 << 30)
                    used = table_ref[RAND + 1, 0] == key_block
                    for g in range(1, GLOB):
                        used = used | (table_ref[RAND + 1, g] == key_block)
                    for r in range(RAND):
                        used = used | (table_ref[r, query_block] == key_block)
                    bias = jnp.where(used, 0.0, LARGE_NEG)
                    bias = jnp.where(win_all[win, a] >= needed, 0.0, bias)
                    bias_ref[q, k, a, :, b * BLOCK : (b + 1) * BLOCK] = bias

    def steps(pairs, h, first=False):
        cols = at(h)
        every = [
            lax.dot_general(
                q_all[q, :, cols],
                k_all[k, :, cols],
                (((1,), (1,)), ((), ())),
                preferred_element_type=jnp.float32,
            )
            for q, k in pairs
        ]
        held = []
        for (q, k), scores in zip(pairs, every):
            for a in range(dev_blocks):
                span = slice(a * BLOCK, (a + 1) * BLOCK)
                block = scores[span] * SCALE + bias_ref[q, k, a, 0:1, :]
                best = jnp.max(block, axis=1, keepdims=True)
                old = None
                if first:
                    best = jnp.broadcast_to(best, (BLOCK, HEAD))
                else:
                    old = peak_ref[q, h, span]
                    best = jnp.maximum(old, best)
                weights = [
                    jnp.exp2(block[:, b * BLOCK : (b + 1) * BLOCK] - best) for b in range(dev_blocks)
                ]
                total = functools.reduce(jnp.add, weights)
                rounded = jnp.concatenate([w.astype(jnp.bfloat16) for w in weights], axis=1)
                held.append((old, best, total, rounded))
        for i, (q, k) in enumerate(pairs):
            mine = held[i * dev_blocks : (i + 1) * dev_blocks]
            part = jnp.dot(
                jnp.concatenate([m[3] for m in mine], axis=0),
                v_all[k, :, cols],
                preferred_element_type=jnp.float32,
            )
            for a, (old, best, total, _) in enumerate(mine):
                span = slice(a * BLOCK, (a + 1) * BLOCK)
                acc = part[span]
                if not first:
                    fade = jnp.exp2(old - best)
                    total = total + total_ref[q, h, span] * fade
                    acc = acc + acc_ref[q, h, span] * fade
                peak_ref[q, h, span] = best
                total_ref[q, h, span] = total
                acc_ref[q, h, span] = acc

    def step(q, k, h, first=False):
        steps([(q, k)], h, first)

    def score(pairs, h):
        cols = at(h)
        every = [
            lax.dot_general(
                q_all[q, :, cols],
                k_all[k, :, cols],
                (((1,), (1,)), ((), ())),
                preferred_element_type=jnp.float32,
            )
            for q, k in pairs
        ]
        for (q, k), scores in zip(pairs, every):
            for a in range(dev_blocks):
                span = slice(a * BLOCK, (a + 1) * BLOCK)
                block = scores[span] * SCALE + bias_ref[q, k, a, 0:1, :]
                old = peak_ref[q, h, span]
                best = jnp.maximum(old, jnp.max(block, axis=1, keepdims=True))
                weights = [
                    jnp.exp2(block[:, b * BLOCK : (b + 1) * BLOCK] - best) for b in range(dev_blocks)
                ]
                fade = jnp.exp2(old - best)
                weight_ref[q, span] = jnp.concatenate([w.astype(jnp.bfloat16) for w in weights], axis=1)
                peak_ref[q, h, span] = best
                total_ref[q, h, span] = functools.reduce(jnp.add, weights, total_ref[q, h, span] * fade)
                acc_ref[q, h, span] = acc_ref[q, h, span] * fade

    def value(q, k, h):
        return acc_ref[q, h] + jnp.dot(weight_ref[q], v_all[k, :, at(h)], preferred_element_type=jnp.float32)

    def level(q, h, stat):
        total = jnp.sum(total_ref[q, h], axis=1, keepdims=True)
        inverse_ref[q] = jnp.broadcast_to(1.0 / total, (rows, HEAD))
        stat[...] = (peak_ref[q, h] + jnp.log2(total)).T[:8]

    def pack(q, h, part, stat):
        level(q, h, stat)
        part[...] = (acc_ref[q, h] * inverse_ref[q]).astype(jnp.bfloat16)

    group = 2 * HEAD

    def group_cols(g):
        if isinstance(g, int):
            return pl.ds(g * group, group)
        return pl.ds(pl.multiple_of(g * group, group), group)

    def exchange(g):
        return send(
            own_ref.at[:, group_cols(g)],
            other_ref.at[:, group_cols(g)],
            pair_send.at[g],
            pair_recv.at[g],
            {"head": 1 - side},
        )

    def project(source, which, g):
        w_rows = pl.ds(pl.multiple_of(which * width + g * group, group), group)
        return jnp.dot(source[:, group_cols(g)], w_ref[w_rows, :], preferred_element_type=jnp.float32)

    def finish(h):
        exchange(h).start()

        @pl.when(h == 0)
        def _():
            sum_ref[...] = project(own_ref, side, h)

        @pl.when(h > 0)
        def _():
            exchange(h - 1).wait_recv()
            sum_ref[...] += project(own_ref, side, h) + project(other_ref, 1 - side, h - 1)

    def loop(lower, upper, body):
        def run(h, carry):
            body(h)
            return carry

        lax.fori_loop(lower, upper, run, 0)

    def column_of(stat):
        return jnp.broadcast_to(stat[0:1, :], (HEAD, rows)).T

    def join(h):
        for copy in sideways(h):
            copy.wait_recv()
        upward(1, h)[0].wait_recv()
        upward(0, h)[0].wait_recv()
        mine, theirs = column_of(side_stat_in[h]), column_of(up_stat_in[1, h])
        best = jnp.maximum(mine, theirs)
        mine, theirs = jnp.exp2(mine - best), jnp.exp2(theirs - best)
        inverse = 1.0 / (mine + theirs)
        inverse_ref[0] = theirs * inverse
        part = side_part_in[h].astype(jnp.float32) * (mine * inverse)
        old, theirs = peak_ref[OWN, h], column_of(up_stat_in[0, h])
        best = jnp.maximum(old, theirs)
        fade, theirs = jnp.exp2(old - best), jnp.exp2(theirs - best)
        inverse = 1.0 / (jnp.sum(total_ref[OWN, h] * fade, axis=1, keepdims=True) + theirs)
        inverse_ref[1] = theirs * inverse
        acc_ref[OWN, h] = acc_ref[OWN, h] * (fade * inverse)
        acc_ref[PARTNER, h] = part
        for which, q, col in ((1, PARTNER, 1 - column), (0, OWN, column)):
            upward(which, h)[1].wait_recv()
            total = acc_ref[q, h] + up_part_in[which, h].astype(jnp.float32) * inverse_ref[1 - which]
            own_ref[:, spot(col, h)] = total.astype(jnp.bfloat16)
        finish(h)

    def each_w(action):
        def one(h):
            for core in (0, 1):
                for col in (0, 1):
                    getattr(load_w(core, h, col), action)()

        loop(0, heads, one)

    @pl.when(inner)
    def _():
        pl.semaphore_wait(barrier, 4)
        start_key_value(CROSS, 0)
        for h in range(half):
            start_key_value(PARTNER, h)
        start_query(PARTNER)
        loop(1, last, lambda h: start_key_value(CROSS, h))
        ask(OWN).start()
        ask_reach(OWN).start()
        loop(half, heads, lambda h: start_key_value(PARTNER, h))
        pl.semaphore_wait(ready, 4)
        loop(0, heads, lambda h: start_key_value(NEAR, h))
        each_w("start")
        close_by = ((OWN, position), (PARTNER, partner), (NEAR, near), (NEAR_P, near_partner))
        beyond = ((CROSS, cross), (CROSS_P, cross_partner), (FAR, far), (FAR_P, far_partner))
        use_bias(OWN, position, close_by + beyond)
        for load in loads:
            load.wait()
        loop(0, heads, lambda h: step(OWN, OWN, h, first=True))

        def first_round(h):
            wait_key_value(PARTNER, h)
            start_key_value(NEAR_P, h)

            @pl.when(h < last)
            def _():
                start_key_value(CROSS_P, h)

            step(OWN, PARTNER, h)

        loop(0, heads, first_round)
        wait_query(PARTNER)
        ask(PARTNER).start()
        ask_reach(PARTNER).start()
        use_bias(PARTNER, partner, close_by + beyond)
        loop(0, heads, lambda h: step(PARTNER, OWN, h, first=True))
        loop(0, heads, lambda h: step(PARTNER, PARTNER, h))
        wait_query(BELOW)
        ask(BELOW).start()
        use_bias(BELOW, near, beyond)

        def pass_on(h):
            wait_key_value(NEAR, h)
            start_key_value(FAR, h)
            wait_key_value(NEAR_P, h)
            start_key_value(FAR_P, h)

        def meet_near(h):
            steps([(OWN, NEAR), (PARTNER, NEAR)], h)
            steps([(OWN, NEAR_P), (PARTNER, NEAR_P)], h)

        loop(0, half, pass_on)

        def second_round(h):
            wait_key_value(CROSS, h)
            steps([(OWN, CROSS), (PARTNER, CROSS)], h)
            step(BELOW, CROSS, h, first=True)

            @pl.when(h < half)
            def _():
                meet_near(h)

            wait_key_value(CROSS_P, h)
            steps([(OWN, CROSS_P), (PARTNER, CROSS_P)], h)
            step(BELOW, CROSS_P, h)

        loop(0, last, second_round)
        wait_query(BELOW_P)
        ask(BELOW_P).start()
        use_bias(BELOW_P, near_partner, beyond)

        def third_round(h):
            step(BELOW_P, CROSS, h, first=True)
            step(BELOW_P, CROSS_P, h)

        loop(0, last, third_round)

        ask_reach(OWN).wait_recv()
        ask_reach(PARTNER).wait_recv()
        chips = {CROSS: cross, CROSS_P: cross_partner, FAR: far, FAR_P: far_partner}
        for slot in (CROSS, CROSS_P):
            use_bias(slot, chips[slot], close_by)
        for slot in (FAR, FAR_P):
            use_bias(slot, chips[slot], close_by, OWN)

        ask(OWN).wait_recv()
        ask(PARTNER).wait_recv()
        steps([(CROSS, OWN), (CROSS_P, OWN)], last, first=True)
        steps([(CROSS, PARTNER), (CROSS_P, PARTNER)], last)

        def reply():
            for slot in (BELOW, BELOW_P):
                ask(slot).wait_recv()
            steps([(FAR, OWN), (FAR_P, OWN)], last, first=True)
            steps([(FAR, PARTNER), (FAR_P, PARTNER)], last)
            wait_key_value(NEAR, last)
            for pair in ((FAR_P, FAR), (CROSS_P, CROSS)):
                steps([(q, NEAR) for q in pair], last)
            wait_key_value(NEAR_P, last)
            for pair in ((FAR_P, FAR), (CROSS_P, CROSS)):
                steps([(q, NEAR_P) for q in pair], last)
                for q in pair:
                    pack(q, last, back_part.at[q - CROSS], back_stat.at[q - CROSS])
                    for copy in answer(q):
                        copy.start()

        def settle():
            meet_near(last)
            pack(PARTNER, last, side_part.at[last], side_stat.at[last])
            for copy in sideways(last):
                copy.start()

        each_w("wait")

        def close(h):
            swap(h).wait_recv()
            finish(h)

        def late(h):
            wait_key_value(FAR, h)
            steps([(BELOW_P, FAR), (BELOW, FAR)], h)
            steps([(PARTNER, FAR), (OWN, FAR)], h)

            @pl.when(h < last - half)
            def _():
                pass_on(h + half)

            key_value(0, FAR_P, h).wait_recv()
            score([(BELOW_P, FAR_P), (BELOW, FAR_P)], h)
            score([(PARTNER, FAR_P), (OWN, FAR_P)], h)
            for which, q in ((1, BELOW_P), (0, BELOW)):
                level(q, h, up_stat.at[which, h])
                upward(which, h)[0].start()
            for q in (PARTNER, OWN):
                total = jnp.sum(total_ref[q, h], axis=1, keepdims=True)
                inverse_ref[q] = jnp.broadcast_to(1.0 / total, (rows, HEAD))
            key_value(1, FAR_P, h).wait_recv()
            def lift(which, q):
                up_part[which, h] = (value(q, FAR_P, h) * inverse_ref[q]).astype(jnp.bfloat16)
                upward(which, h)[1].start()

            lift(1, BELOW_P)
            side_part[h] = (value(PARTNER, FAR_P, h) * inverse_ref[PARTNER]).astype(jnp.bfloat16)
            swap(h).start()
            lift(0, BELOW)
            own_ref[:, spot(column, h)] = (value(OWN, FAR_P, h) * inverse_ref[OWN]).astype(jnp.bfloat16)

            @pl.when(h < last - half)
            def _():
                meet_near(h + half)

        def drain(h):
            for slot in (PARTNER, NEAR, NEAR_P):
                for kind in (0, 1):
                    key_value(kind, slot, h).wait_send()

            @pl.when(h < last)
            def _():
                for slot in (CROSS, CROSS_P, FAR, FAR_P):
                    for kind in (0, 1):
                        key_value(kind, slot, h).wait_send()

        def late_round(h):
            @pl.when(h == last - 1)
            def _():
                reply()

            @pl.when(h < last)
            def _():
                late(h)

            @pl.when(h == last - 1)
            def _():
                settle()

            @pl.when(h > 0)
            def _():
                close(h - 1)

        loop(0, last + 1, late_round)
        loop(0, heads, drain)
        for copy in query(PARTNER):
            copy.wait_send()
        for slot in (OWN, PARTNER, BELOW, BELOW_P):
            ask(slot).wait_send()
        for slot in (OWN, PARTNER):
            ask_reach(slot).wait_send()
        for copy in sideways(last):
            copy.wait_send()
        join(jnp.int32(last))

    @pl.when(jnp.logical_not(inner))
    def _():
        pl.semaphore_wait(barrier, 6)
        for target in (near, near_partner, far_inner, far_inner_partner):
            greet(ready, {"ctx": target})
        start_query(BELOW)
        for h in range(half):
            start_key_value(PARTNER, h)
        start_query(PARTNER)
        for h in range(half):
            start_key_value(NEAR, h)
        loop(half, heads, lambda h: start_key_value(PARTNER, h))
        each_w("start")
        close_by = ((OWN, position), (PARTNER, partner), (NEAR, near), (NEAR_P, near_partner))
        use_bias(OWN, position, close_by)
        for load in loads:
            load.wait()

        def relay(h):
            @pl.when(h >= half)
            def _():
                start_key_value(NEAR, h)

            wait_key_value(PARTNER, h)
            start_key_value(NEAR_P, h)

        loop(0, half, relay)
        wait_query(PARTNER)
        start_query(BELOW_P)
        loop(half, heads, relay)
        use_bias(PARTNER, partner, close_by)

        def early(h):
            step(OWN, OWN, h, first=True)
            step(PARTNER, OWN, h, first=True)
            steps([(PARTNER, PARTNER), (OWN, PARTNER)], h)

        loop(0, heads, early)

        def middle(h):
            wait_key_value(NEAR, h)
            steps([(PARTNER, NEAR), (OWN, NEAR)], h)

        loop(0, heads, middle)

        def side_round(h):
            wait_key_value(NEAR_P, h)
            steps([(PARTNER, NEAR_P), (OWN, NEAR_P)], h)
            pack(PARTNER, h, side_part.at[h], side_stat.at[h])
            for copy in sideways(h):
                copy.start()

        loop(0, heads, side_round)
        each_w("wait")

        def drain(h):
            for slot in (PARTNER, NEAR, NEAR_P):
                for kind in (0, 1):
                    key_value(kind, slot, h).wait_send()
            for copy in sideways(h):
                copy.wait_send()

        loop(0, heads, drain)
        for slot in (PARTNER, BELOW, BELOW_P):
            for copy in query(slot):
                copy.wait_send()

        loop(0, heads, join)

    exchange(heads - 1).wait_recv()
    out_ref[...] = (sum_ref[...] + project(other_ref, 1 - side, heads - 1)).astype(out_ref.dtype)
    loop(0, heads, lambda g: exchange(g).wait_send())

    @pl.when(inner)
    def _():
        def drain_late(h):
            swap(h).wait_send()
            for which in (0, 1):
                for copy in upward(which, h):
                    copy.wait_send()

        loop(0, last, drain_late)
        for slot in (CROSS, CROSS_P, FAR, FAR_P):
            for copy in answer(slot):
                copy.wait_send()


def grid_call(queries, keys, values, out_weight, random_blocks, window_blocks, global_blocks):
    rows, width = queries.shape
    heads = width // HEAD // 2
    dev_blocks = rows // BLOCK
    out_width = out_weight.shape[1]
    hbm = pl.BlockSpec(memory_space=pltpu.HBM)
    state = pltpu.VMEM((8, heads, rows, HEAD), jnp.float32)
    dma = pltpu.SemaphoreType.DMA
    blocks = random_blocks.shape[0]
    table = (
        jnp.pad(random_blocks.T, ((0, 2), (0, 0)))
        + jnp.pad(window_blocks[None], ((RAND, 1), (0, blocks - dev_blocks)))
        + jnp.pad(global_blocks[None], ((RAND + 1, 0), (0, blocks - GLOB)))
    )
    return pl.pallas_call(
        grid_kernel,
        out_shape=jax.ShapeDtypeStruct((rows, out_width), jnp.bfloat16),
        in_specs=[pl.BlockSpec(memory_space=pltpu.SMEM)] + [hbm] * 4,
        out_specs=pl.BlockSpec(memory_space=pltpu.VMEM),
        scratch_shapes=[
            pltpu.VMEM((8, rows, width // 2), jnp.bfloat16),
            pltpu.VMEM((8, rows, width // 2), jnp.bfloat16),
            pltpu.VMEM((8, rows, width // 2), jnp.bfloat16),
            pltpu.VMEM(out_weight.shape, jnp.bfloat16),
            pltpu.VMEM((8, dev_blocks, 8, HEAD), jnp.int32),
            pltpu.VMEM((8, 8, dev_blocks, 8, rows), jnp.float32),
            state,
            state,
            state,
            pltpu.VMEM((4, rows, rows), jnp.bfloat16),
            pltpu.VMEM((8, rows, HEAD), jnp.float32),
            pltpu.VMEM((2, heads, rows, HEAD), jnp.bfloat16),
            pltpu.VMEM((2, heads, 8, rows), jnp.float32),
            pltpu.VMEM((2, heads, rows, HEAD), jnp.bfloat16),
            pltpu.VMEM((2, heads, 8, rows), jnp.float32),
            pltpu.VMEM((heads, rows, HEAD), jnp.bfloat16),
            pltpu.VMEM((heads, 8, rows), jnp.float32),
            pltpu.VMEM((heads, rows, HEAD), jnp.bfloat16),
            pltpu.VMEM((heads, 8, rows), jnp.float32),
            pltpu.VMEM((rows, width), jnp.bfloat16),
            pltpu.VMEM((rows, width), jnp.bfloat16),
            pltpu.VMEM((rows, out_width), jnp.float32),
            dma((3,)),
            dma((2, heads, 2)),
            dma((8, 2, heads)),
            dma((8, 2, heads)),
            dma((4,)),
            dma((4,)),
            dma((8,)),
            dma((8,)),
            dma((2, 2, heads)),
            dma((2, 2, heads)),
            dma((2, heads)),
            dma((2, heads)),
            dma((heads,)),
            dma((heads,)),
            pltpu.SemaphoreType.REGULAR,
            pltpu.VMEM((4, rows, HEAD), jnp.bfloat16),
            pltpu.VMEM((4, 8, rows), jnp.float32),
            dma((2, 4)),
            dma((4,)),
            dma((4,)),
        ],
        compiler_params=pltpu.CompilerParams(
            collective_id=0, has_side_effects=True, vmem_limit_bytes=53 << 20
        ),
    )(table, queries, keys, values, out_weight)


def per_device(*arguments):
    if lax.axis_size("ctx") == GRID_DEPTH * GRID_WIDTH:
        return grid_call(*arguments)
    return ring_call(*arguments)


def ring_place(index, count):
    odd = index % 2
    return (1 - odd) * (index // 2) + odd * (count - 1 - index // 2)


def ring_index(place, count):
    late = place // (count // 2)
    return (1 - late) * (2 * place) + late * (2 * (count - 1 - place) + 1)


def ring_kernel(
    count,
    random_ref,
    window_ref,
    global_ref,
    q_hbm,
    k_hbm,
    v_hbm,
    w_hbm,
    out_any,
    q_ref,
    w_ref,
    k_all,
    v_all,
    peak_ref,
    total_ref,
    acc_ref,
    own_ref,
    other_ref,
    sum_ref,
    out_ref,
    load_sem,
    send_sem,
    recv_sem,
    last_send,
    last_recv,
    pair_send,
    pair_recv,
):
    rows, width = q_ref.shape
    heads = width // HEAD
    dev_blocks = rows // BLOCK
    half = count // 2
    position = lax.axis_index("ctx")
    side = lax.axis_index("head")
    place = ring_place(position, count)
    right = ring_index((place + 1) % count, count)
    left = ring_index((place + count - 1) % count, count)

    load_k = pltpu.make_async_copy(k_hbm, k_all.at[0], load_sem.at[0])
    load_v = pltpu.make_async_copy(v_hbm, v_all.at[0], load_sem.at[1])
    load_q = pltpu.make_async_copy(q_hbm, q_ref, load_sem.at[2])
    load_w = pltpu.make_async_copy(w_hbm, w_ref, load_sem.at[3])
    load_k.start()
    load_v.start()
    load_q.start()

    barrier = pltpu.get_barrier_semaphore()
    pl.semaphore_signal(barrier, inc=1, device_id={"ctx": left}, device_id_type=MESH)
    pl.semaphore_signal(barrier, inc=1, device_id={"ctx": right}, device_id_type=MESH)
    pl.semaphore_signal(barrier, inc=1, device_id={"head": 1 - side}, device_id_type=MESH)
    pl.semaphore_wait(barrier, 3)

    def hop(stream, slot):
        buffer = k_all if stream in (K_FWD, K_BWD) else v_all
        forward = stream in (K_FWD, V_FWD)
        source = slot - 1 if forward else (slot + 1) % count
        return pltpu.make_async_remote_copy(
            src_ref=buffer.at[source],
            dst_ref=buffer.at[slot],
            send_sem=send_sem.at[stream, slot],
            recv_sem=recv_sem.at[stream, slot],
            device_id={"ctx": right if forward else left},
            device_id_type=MESH,
        )

    load_k.wait()
    hop(K_FWD, 1).start()
    hop(K_BWD, count - 1).start()
    load_v.wait()
    hop(V_FWD, 1).start()
    hop(V_BWD, count - 1).start()
    load_q.wait()
    load_w.start()

    peak_ref[...] = jnp.full_like(peak_ref, LARGE_NEG)
    total_ref[...] = jnp.zeros_like(total_ref)
    acc_ref[...] = jnp.zeros_like(acc_ref)
    scale = math.log2(math.e) / math.sqrt(HEAD)

    def use_bias(slot):
        owner = ring_index((place + count - slot) % count, count)
        row_block = lax.broadcasted_iota(jnp.int32, (rows, HEAD), 0) // BLOCK
        biases = []
        for b in range(dev_blocks):
            key_block = owner * dev_blocks + b
            bias = jnp.full((rows, HEAD), LARGE_NEG, jnp.float32)
            for a in range(dev_blocks):
                query_block = position * dev_blocks + a
                offset = jnp.abs(key_block - query_block)
                used = (offset <= window_ref[a]) & (offset <= WMAX)
                for g in range(GLOB):
                    used = used | (global_ref[g] == key_block)
                for r in range(RAND):
                    used = used | (random_ref[r, query_block] == key_block)
                bias = jnp.where(row_block == a, jnp.where(used, 0.0, LARGE_NEG), bias)
            biases.append(bias)
        return biases

    def attend_head(slot, h, biases):
        cols = pl.ds(h * HEAD, HEAD)
        if not isinstance(h, int):
            cols = pl.ds(pl.multiple_of(h * HEAD, HEAD), HEAD)
        scores = lax.dot_general(
            q_ref[:, cols],
            k_all[slot, :, cols],
            (((1,), (1,)), ((), ())),
            preferred_element_type=jnp.float32,
        )
        scores = scores * scale
        old_peak = peak_ref[h]
        best_peak = old_peak
        parts = []
        for b, bias in enumerate(biases):
            block = scores[:, b * BLOCK : (b + 1) * BLOCK]
            row_peak = jnp.max(block, axis=1, keepdims=True)
            weights = jnp.exp2(block - row_peak)
            part = jnp.dot(
                weights.astype(jnp.bfloat16),
                v_all[slot, b * BLOCK : (b + 1) * BLOCK, cols],
                preferred_element_type=jnp.float32,
            )
            used_peak = row_peak + bias
            best_peak = jnp.maximum(best_peak, used_peak)
            parts.append((used_peak, weights, part))
        fade = jnp.exp2(old_peak - best_peak)
        total = total_ref[h] * fade
        acc = acc_ref[h] * fade
        for used_peak, weights, part in parts:
            factor = jnp.exp2(used_peak - best_peak)
            total = total + weights * factor
            acc = acc + part * factor
        return best_peak, total, acc

    def attend(slot):
        biases = use_bias(slot)

        def one_head(h, carry):
            peak_ref[h], total_ref[h], acc_ref[h] = attend_head(slot, h, biases)
            return carry

        lax.fori_loop(0, heads, one_head, 0, unroll=2)

    def last_hop(stream, h):
        buffer = k_all if stream == K_FWD else v_all
        forward = h % 2 == 0
        cols = pl.ds(h * HEAD, HEAD)
        return pltpu.make_async_remote_copy(
            src_ref=buffer.at[half - 1 if forward else half + 1, :, cols],
            dst_ref=buffer.at[half, :, cols],
            send_sem=last_send.at[stream, h],
            recv_sem=last_recv.at[stream, h],
            device_id={"ctx": right if forward else left},
            device_id_type=MESH,
        )

    attend(0)

    def middle(step, carry):
        back = count - step
        hop(K_FWD, step).wait_recv()
        hop(K_FWD, step + 1).start()
        hop(K_BWD, back).wait_recv()
        hop(K_BWD, back - 1).start()
        hop(V_FWD, step).wait_recv()
        hop(V_FWD, step + 1).start()
        hop(V_BWD, back).wait_recv()
        hop(V_BWD, back - 1).start()
        attend(step)
        attend(back)
        return carry

    lax.fori_loop(1, half - 1, middle, 0)

    for side_of, key_stream in ((0, K_FWD), (1, K_BWD)):
        hop(key_stream, half + 1 if side_of else half - 1).wait_recv()
        for pair in range(min(2, heads // 2)):
            last_hop(K_FWD, 2 * pair + side_of).start()
    for side_of, value_stream in ((0, V_FWD), (1, V_BWD)):
        hop(value_stream, half + 1 if side_of else half - 1).wait_recv()
        for pair in range(heads // 2):
            last_hop(V_FWD, 2 * pair + side_of).start()
            if pair + 2 < heads // 2:
                last_hop(K_FWD, 2 * (pair + 2) + side_of).start()
    attend(half - 1)
    attend(half + 1)
    load_w.wait()
    biases = use_bias(half)
    group = 2 * HEAD

    def exchange(g):
        cols = pl.ds(g * group, group)
        return pltpu.make_async_remote_copy(
            src_ref=own_ref.at[:, cols],
            dst_ref=other_ref.at[:, cols],
            send_sem=pair_send.at[g],
            recv_sem=pair_recv.at[g],
            device_id={"head": 1 - side},
            device_id_type=MESH,
        )

    def project(source, which, g):
        w_rows = pl.ds(pl.multiple_of(which * width + g * group, group), group)
        return jnp.dot(
            source[:, g * group : (g + 1) * group],
            w_ref[w_rows, :],
            preferred_element_type=jnp.float32,
        )

    groups = width // group
    for g in range(groups):
        for h in (2 * g, 2 * g + 1):
            last_hop(K_FWD, h).wait_recv()
            last_hop(V_FWD, h).wait_recv()
            _, total, acc = attend_head(half, h, biases)
            total = jnp.sum(total, axis=1, keepdims=True)
            own_ref[:, h * HEAD : (h + 1) * HEAD] = (acc / total).astype(jnp.bfloat16)
        exchange(g).start()
        if g == 0:
            sum_ref[...] = project(own_ref, side, g)
        else:
            exchange(g - 1).wait_recv()
            sum_ref[...] += project(other_ref, 1 - side, g - 1) + project(own_ref, side, g)
    exchange(groups - 1).wait_recv()
    out_ref[...] = (sum_ref[...] + project(other_ref, 1 - side, groups - 1)).astype(out_ref.dtype)

    store = pltpu.make_async_copy(out_ref, out_any, load_sem.at[4])
    store.start()
    for g in range(groups):
        exchange(g).wait_send()
    for h in range(heads):
        last_hop(K_FWD, h).wait_send()
        last_hop(V_FWD, h).wait_send()

    def drain(step, carry):
        hop(K_FWD, step).wait_send()
        hop(V_FWD, step).wait_send()
        hop(K_BWD, count - step).wait_send()
        hop(V_BWD, count - step).wait_send()
        return carry

    lax.fori_loop(1, half, drain, 0)
    store.wait()


def ring_call(queries, keys, values, out_weight, random_blocks, window_blocks, global_blocks):
    count = lax.axis_size("ctx")
    rows, width = queries.shape
    heads = width // HEAD
    out_width = out_weight.shape[1]
    smem = pl.BlockSpec(memory_space=pltpu.SMEM)
    hbm = pl.BlockSpec(memory_space=pltpu.HBM)
    return pl.pallas_call(
        functools.partial(ring_kernel, count),
        out_shape=jax.ShapeDtypeStruct((rows, out_width), jnp.bfloat16),
        in_specs=[smem] * 3 + [hbm] * 4,
        out_specs=pl.BlockSpec(memory_space=pl.ANY),
        scratch_shapes=[
            pltpu.VMEM((rows, width), jnp.bfloat16),
            pltpu.VMEM(out_weight.shape, jnp.bfloat16),
            pltpu.VMEM((count, rows, width), jnp.bfloat16),
            pltpu.VMEM((count, rows, width), jnp.bfloat16),
            pltpu.VMEM((heads, rows, HEAD), jnp.float32),
            pltpu.VMEM((heads, rows, HEAD), jnp.float32),
            pltpu.VMEM((heads, rows, HEAD), jnp.float32),
            pltpu.VMEM((rows, width), jnp.bfloat16),
            pltpu.VMEM((rows, width), jnp.bfloat16),
            pltpu.VMEM((rows, out_width), jnp.float32),
            pltpu.VMEM((rows, out_width), jnp.bfloat16),
            pltpu.SemaphoreType.DMA((5,)),
            pltpu.SemaphoreType.DMA((4, count)),
            pltpu.SemaphoreType.DMA((4, count)),
            pltpu.SemaphoreType.DMA((2, heads)),
            pltpu.SemaphoreType.DMA((2, heads)),
            pltpu.SemaphoreType.DMA((heads // 2,)),
            pltpu.SemaphoreType.DMA((heads // 2,)),
        ],
        compiler_params=pltpu.CompilerParams(
            collective_id=1, has_side_effects=True, vmem_limit_bytes=60 << 20
        ),
    )(random_blocks.T, window_blocks, global_blocks, queries, keys, values, out_weight)


def solution(mesh):
    placed = (
        P(("groups", "ctx"), "head"),
        P(("groups", "ctx"), "head"),
        P(("groups", "ctx"), "head"),
        P(None, "head"),
        P("groups", None),
        P(("groups", "ctx")),
        P("groups"),
    )
    return jax.shard_map(
        per_device,
        mesh=mesh,
        in_specs=placed,
        out_specs=P(("groups", "ctx"), "head"),
        check_vma=False,
    )
```
